32 devices in a mesh: fsdp: 32 (over z, y, x, core).
Axes of the slice: x: 2, y: 2, z: 4, core: 2. Of those that a mesh axis runs over, the one named last changes fastest.
Arguments:
- tokens: bfloat16 [512, 64, 768], P('fsdp'), may hold values from -6 to 6
- lengths: int32 [512], P('fsdp'), may hold values from 3 to 64, as said below
- partners: int32 [256], P('fsdp'), may hold values from 0 to 255, each once
- out_cotangent: bfloat16 [512, 64, 768], P('fsdp'), may hold values from -6 to 6
- w_query: bfloat16 [768, 768], P('fsdp'), may hold values from -0.21875 to 0.21875
- w_key: bfloat16 [768, 768], P('fsdp'), may hold values from -0.21875 to 0.21875
- w_value: bfloat16 [768, 768], P('fsdp'), may hold values from -0.21875 to 0.21875
- w_output: bfloat16 [768, 768], P('fsdp'), may hold values from -0.625 to 0.625
- b_query: bfloat16 [768], P('fsdp'), may hold values from -1.5 to 1.5
- b_value: bfloat16 [768], P('fsdp'), may hold values from -1.5 to 1.5
- b_output: bfloat16 [768], P('fsdp'), may hold values from -1.5 to 1.5
- gain_attn: bfloat16 [768], P('fsdp'), may hold values from 0.5 to 1.5
- shift_attn: bfloat16 [768], P('fsdp'), may hold values from -1.5 to 1.5
- w_inner: bfloat16 [768, 3072], P('fsdp'), may hold values from -0.21875 to 0.21875
- b_inner: bfloat16 [3072], P('fsdp'), may hold values from -1.5 to 1.5
- w_outer: bfloat16 [3072, 768], P('fsdp'), may hold values from -0.15625 to 0.15625
- b_outer: bfloat16 [768], P('fsdp'), may hold values from -1.5 to 1.5
- gain_ffn: bfloat16 [768], P('fsdp'), may hold values from 0.5 to 1.5
- shift_ffn: bfloat16 [768], P('fsdp'), may hold values from -1.5 to 1.5
Outputs:
- loss: float32 [], replicated
- block_out: bfloat16 [512, 64, 768], P('fsdp')
- grad_tokens: float32 [512, 64, 768], P('fsdp')
- grad_w_query: float32 [768, 768], P('fsdp')
- grad_w_key: float32 [768, 768], P('fsdp')
- grad_w_value: float32 [768, 768], P('fsdp')
- grad_w_output: float32 [768, 768], P('fsdp')
- grad_b_query: float32 [768], P('fsdp')
- grad_b_value: float32 [768], P('fsdp')
- grad_b_output: float32 [768], P('fsdp')
- grad_gain_attn: float32 [768], P('fsdp')
- grad_shift_attn: float32 [768], P('fsdp')
- grad_w_inner: float32 [768, 3072], P('fsdp')
- grad_b_inner: float32 [3072], P('fsdp')
- grad_w_outer: float32 [3072, 768], P('fsdp')
- grad_b_outer: float32 [768], P('fsdp')
- grad_gain_ffn: float32 [768], P('fsdp')
- grad_shift_ffn: float32 [768], P('fsdp')
The draws below stay inside these ranges and needn't reach their ends.
Inputs may be any that keep to these rules, and one draw needn't show every extreme that they name: `lengths`: each sentence slot has 3 to 64 live tokens, heavy toward short ones; at least one slot has 64.
All inputs are finite; a program needn't handle non-finite values.
Results may differ from the reference program's by a relative error of at most 0.013.
Values may be sent and summed in bfloat16 or wider, within the bound.
No kernel may reach another device: no remote copies, remote signals or barrier semaphores. Data moves between devices by JAX's collectives and lax.ppermute only.
A program may use at most 192 MiB of HBM per device.

```python
import jax
import jax.numpy as jnp
from jax import lax

D = 768
HEADS = 12
HEAD_DIM = 64
FF = 3072
LEN = 64
SENT = 512
PAIRS = 256


def draw_lengths(key, part):
    keys = jax.random.split(key, 3)
    first = jax.random.randint(keys[0], (SENT,), 0, LEN - 2)
    second = jax.random.randint(keys[1], (SENT,), 0, LEN - 2)
    spread = 3 + first * second // (LEN - 3)
    picked = jax.random.randint(keys[2], (), 0, SENT)
    slots = jnp.arange(SENT, dtype=jnp.int32)
    return jnp.where(slots == picked, LEN, spread).astype(jnp.int32)


def levels(rng, extent, cuts, smallest, largest):
    loudness, own = 1.0, jax.random.fold_in(rng, 6)
    for position, blocks in cuts:
        draws = jnp.exp(jax.random.uniform(jax.random.fold_in(own, position), (blocks,), jnp.float32, smallest / len(cuts), largest / len(cuts)))
        loudness = loudness * jnp.repeat(draws, extent[position] // blocks).reshape([-1 if axis == position else 1 for axis in range(len(extent))])
    return loudness


def normal_values(stream_key, extent, scale, bound, cuts=(), kind=jnp.bfloat16):
    values = scale * jax.random.normal(stream_key, extent, jnp.float32)
    if cuts:
        values = values * levels(stream_key, extent, cuts, -0.22, 0.18)
    return jnp.clip(values, -bound, bound).astype(kind)


def setup_inputs(seed: int = 0) -> dict:
    streams_of = jax.random.split(jax.random.key(seed), 20)
    return {
        "tokens": normal_values(streams_of[0], (SENT, LEN, D), 1.0, 6.0, ((0, 32),)),
        "lengths": draw_lengths(jax.random.fold_in(streams_of[19], 71), 0),
        "partners": jax.random.permutation(streams_of[2], PAIRS).astype(jnp.int32),
        "out_cotangent": normal_values(streams_of[3], (SENT, LEN, D), 1.0, 6.0, ((0, 32),)),
        "w_query": normal_values(streams_of[4], (D, D), D ** -0.5, 0.21875, ((0, 32),)),
        "w_key": normal_values(streams_of[5], (D, D), D ** -0.5, 0.21875, ((0, 32),)),
        "w_value": normal_values(streams_of[6], (D, D), D ** -0.5, 0.21875, ((0, 32),)),
        "w_output": normal_values(streams_of[7], (D, D), (D // 8) ** -0.5, 0.625, ((0, 32),)),
        "b_query": normal_values(streams_of[8], (D,), 0.3, 1.5, ((0, 32),)),
        "b_value": normal_values(streams_of[9], (D,), 0.3, 1.5, ((0, 32),)),
        "b_output": normal_values(streams_of[10], (D,), 0.3, 1.5, ((0, 32),)),
        "gain_attn": jnp.clip(1.0 + 0.1 * jax.random.normal(streams_of[11], (D,), jnp.float32), 0.5, 1.5).astype(jnp.bfloat16),
        "shift_attn": normal_values(streams_of[12], (D,), 0.3, 1.5, ((0, 32),)),
        "w_inner": normal_values(streams_of[13], (D, FF), D ** -0.5, 0.21875, ((0, 32),)),
        "b_inner": normal_values(streams_of[14], (FF,), 0.3, 1.5, ((0, 32),)),
        "w_outer": normal_values(streams_of[15], (FF, D), (FF // 2) ** -0.5, 0.15625, ((0, 32),)),
        "b_outer": normal_values(streams_of[16], (D,), 0.3, 1.5, ((0, 32),)),
        "gain_ffn": jnp.clip(1.0 + 0.1 * jax.random.normal(streams_of[17], (D,), jnp.float32), 0.5, 1.5).astype(jnp.bfloat16),
        "shift_ffn": normal_values(streams_of[18], (D,), 0.3, 1.5, ((0, 32),)),
    }


norm_eps = 1e-12
pool_eps = 1e-06
sim_scale = 50.0
sim_margin = 0.3

@jax.custom_vjp
def low(v):
    return lax.optimization_barrier(v.astype(jnp.bfloat16)).astype(jnp.float32)

@jax.custom_vjp
def low_back(v):
    return v

def low_keep(v):
    return (low(v), None)

def low_pass(kept, grad):
    return (grad,)

def back_keep(v):
    return (v, None)

def back_low(kept, grad):
    return (low(grad),)
low.defvjp(low_keep, low_pass)
low_back.defvjp(back_keep, back_low)

def highest(left, right):
    return jnp.dot(left, right, precision=lax.Precision.HIGHEST)

def layer_norm(field, gain_vec, shift_vec):
    centred = field - lax.optimization_barrier(jnp.mean(field, axis=-1, keepdims=True))
    variance = lax.optimization_barrier(jnp.mean(centred * centred, axis=-1, keepdims=True))
    return centred * lax.rsqrt(variance + norm_eps) * gain_vec + shift_vec

def block_group(weights, inputs, group_lengths):
    w_query, w_key, w_value, w_output, b_query, b_value, b_output, gain_attn, shift_attn, w_inner, b_inner, w_outer, b_outer, gain_ffn, shift_ffn = weights
    count = inputs.shape[0]
    shape_four = (count, LEN, HEADS, HEAD_DIM)
    token_rows = inputs.reshape(count * LEN, D)
    queries = low_back(low(highest(token_rows, w_query) + b_query)).reshape(shape_four)
    key_rows = low_back(low(highest(token_rows, w_key))).reshape(shape_four)
    value_rows = low_back(low(highest(token_rows, w_value) + b_value)).reshape(shape_four)
    scores = jnp.einsum('bqhd,bkhd->bhqk', queries, key_rows, precision=lax.Precision.HIGHEST) * HEAD_DIM ** (-0.5)
    positions = jnp.arange(LEN, dtype=jnp.int32)
    visible = (positions[None, :] < group_lengths[:, None])[:, None, None, :]
    scores = low_back(jnp.where(visible, scores, -1e+30))
    attn_probs = low(jax.nn.softmax(scores, axis=-1))
    context = jnp.einsum('bhqk,bkhd->bqhd', attn_probs, value_rows, precision=lax.Precision.HIGHEST)
    context = low_back(low(context)).reshape(count * LEN, D)
    attn_branch = low_back(highest(context, w_output) + b_output)
    normed_attn = layer_norm(token_rows + attn_branch, gain_attn, shift_attn)
    hidden_pre = low_back(highest(low(normed_attn), w_inner) + b_inner)
    hidden_act = low(jax.nn.gelu(hidden_pre, approximate=False))
    ffn_branch = low_back(highest(hidden_act, w_outer) + b_outer)
    block_rows = layer_norm(normed_attn + ffn_branch, gain_ffn, shift_ffn)
    return block_rows.reshape(count, LEN, D)

def forward(weights, inputs, lengths, partners):
    count = inputs.shape[0]
    groups = count // 64
    grouped = (inputs.reshape(groups, 64, LEN, D), lengths.reshape(groups, 64))
    step_fn = jax.checkpoint(lambda group_pair: block_group(weights, group_pair[0], group_pair[1]))
    output = lax.map(step_fn, grouped).reshape(count, LEN, D)
    cls_rows = output[:, 0, :]
    unit = low(cls_rows * lax.rsqrt(lax.optimization_barrier(jnp.sum(cls_rows * cls_rows, axis=-1, keepdims=True)) + pool_eps))
    paired = unit.reshape(count // 2, 2, D)
    sources = paired[:, 0, :]
    targets = paired[:, 1, :]
    sims = low_back(highest(sources, targets.T)) * sim_scale
    npairs = count // 2
    matched = partners[:, None] == jnp.arange(npairs, dtype=jnp.int32)[None, :]
    sims = sims - jnp.where(matched, sim_scale * sim_margin, 0.0)
    row_lse = jax.nn.logsumexp(sims, axis=1)
    col_lse = jax.nn.logsumexp(sims, axis=0)
    positive = jnp.sum(jnp.where(matched, sims, 0.0))
    loss = (jnp.sum(row_lse) + jnp.sum(col_lse) - 2.0 * positive) / (2.0 * npairs)
    return (output, loss)

def reference(tokens, lengths, partners, out_cotangent, w_query, w_key, w_value, w_output, b_query, b_value, b_output, gain_attn, shift_attn, w_inner, b_inner, w_outer, b_outer, gain_ffn, shift_ffn):
    weights = tuple((item.astype(jnp.float32) for item in (w_query, w_key, w_value, w_output, b_query, b_value, b_output, gain_attn, shift_attn, w_inner, b_inner, w_outer, b_outer, gain_ffn, shift_ffn)))
    inputs = tokens.astype(jnp.float32)

    def objective(weight_set, input_set):
        return forward(weight_set, input_set, lengths, partners)
    (output, loss), pullback = jax.vjp(objective, weights, inputs)
    weight_grads, input_grad = pullback((out_cotangent.astype(jnp.float32), jnp.asarray(PAIRS, dtype=jnp.float32)))
    grad_w_query, grad_w_key, grad_w_value, grad_w_output, grad_b_query, grad_b_value, grad_b_output, grad_gain_attn, grad_shift_attn, grad_w_inner, grad_b_inner, grad_w_outer, grad_b_outer, grad_gain_ffn, grad_shift_ffn = weight_grads
    return (loss, output.astype(jnp.bfloat16), input_grad, grad_w_query, grad_w_key, grad_w_value, grad_w_output, grad_b_query, grad_b_value, grad_b_output, grad_gain_attn, grad_shift_attn, grad_w_inner, grad_b_inner, grad_w_outer, grad_b_outer, grad_gain_ffn, grad_shift_ffn)
```

```python
import jax
import jax.numpy as jnp
from jax import lax
from jax.sharding import PartitionSpec as P

D = 768
HEADS = 12
HEAD_DIM = 64
LEN = 64
HALF = D // 2

norm_eps = 1e-12
pool_eps = 1e-06
sim_scale = 50.0
sim_margin = 0.3

AXIS = "fsdp"
CUBE = 32
CORE = [(i, i ^ 1) for i in range(CUBE)]
FAR_Z = [(i, i ^ 16) for i in range(CUBE)]
NEAR_Z = [(i, i ^ 8) for i in range(CUBE)]
FIRST = [(i, i ^ (4 if i & 1 else 2)) for i in range(CUBE)]
SECOND = [(i, i ^ (2 if i & 1 else 4)) for i in range(CUBE)]


def project(rows, weight):
    return jnp.dot(rows, weight, preferred_element_type=jnp.float32)


def project_back(grad, weight):
    return lax.dot_general(
        grad, weight, (((1,), (1,)), ((), ())), preferred_element_type=jnp.float32
    )


def weight_grad(rows, grad):
    return lax.dot_general(rows, grad, (((0,), (0,)), ((), ())), preferred_element_type=jnp.float32)


def scaled_norm(field, gain_vec):
    centred = field - jnp.mean(field, axis=-1, keepdims=True)
    variance = jnp.mean(centred * centred, axis=-1, keepdims=True)
    return centred * lax.rsqrt(variance + norm_eps) * gain_vec


def exact_gelu(field):
    return jax.nn.gelu(field, approximate=False)


def normalize(field):
    return field * lax.rsqrt(jnp.sum(field * field, axis=-1, keepdims=True) + pool_eps)


def scores_of(queries, key_rows, visible):
    raw = jnp.einsum(
        "bqhd,bkhd->bhqk", queries, key_rows, preferred_element_type=jnp.float32
    ) * HEAD_DIM ** (-0.5)
    return jnp.where(visible, raw, -1e30)


def column_sum(field):
    return jnp.sum(field.astype(jnp.float32), axis=0)


class Place:
    def __init__(self):
        me = lax.axis_index(AXIS)
        self.core = me & 1
        x, y = (me >> 1) & 1, (me >> 2) & 1
        self.near_z, self.far_z = (me >> 3) & 1, (me >> 4) & 1
        self.first = jnp.where(self.core == 0, x, y)
        self.second = jnp.where(self.core == 0, y, x)


def join(own, other, axis, bit):
    shape = own.shape[:axis] + (2,) + own.shape[axis:]
    where = lax.broadcasted_iota(jnp.int32, shape, axis)
    return jnp.where(where == bit, jnp.expand_dims(own, axis), jnp.expand_dims(other, axis))


def pick(field, axis, bit):
    return lax.dynamic_index_in_dim(field, bit, axis, keepdims=False)


def send(field, route):
    return lax.ppermute(field, AXIS, route)


def spread(block, place):
    block = join(block, send(block, FAR_Z), 0, place.far_z)
    block = join(block, send(block, NEAR_Z), 1, place.near_z)
    block = join(block, send(block, FIRST), 2, place.first)
    return join(block, send(block, SECOND), 3, place.second)


def cores(block, place):
    other = send(block, CORE)
    zero = jnp.where(place.core == 0, block, other)
    one = jnp.where(place.core == 0, other, block)
    return jnp.swapaxes(zero, 2, 3), one


def gather_rows(pieces, place):
    joined = []
    for piece in pieces:
        halves = piece.reshape(piece.shape[0], piece.shape[1], 2, HALF)
        joined.append((pick(halves, 2, place.core), pick(halves, 2, 1 - place.core)))
    away = jnp.concatenate([b.reshape(-1, HALF) for _, b in joined], axis=0)
    came = send(away, CORE)
    rows, at = [], 0
    for own, _ in joined:
        count = own.shape[0] * own.shape[1]
        other = came[at : at + count].reshape(own.shape)
        rows.append(join(own, other, 1, place.core).reshape(-1, HALF))
        at += count
    zero, one = cores(spread(jnp.concatenate(rows, axis=0), place), place)
    out, at = [], 0
    chips = CUBE // 2
    for piece in pieces:
        m, r, _ = piece.shape
        count = 2 * m * r
        both = jnp.concatenate(
            [part[..., at : at + count, :].reshape(chips, m, 2 * r, HALF) for part in (zero, one)],
            axis=-1,
        )
        out.append(jnp.swapaxes(both, 0, 1))
        at += count
    return out


def scatter_rows(pieces, place):
    chips = CUBE // 2
    whole = jnp.concatenate(
        [jnp.swapaxes(p, 0, 1).reshape(chips, -1, D) for p in pieces], axis=1
    )
    whole = whole.reshape(2, 2, 2, 2, whole.shape[1], D)
    zero = jnp.swapaxes(whole[..., :HALF], 2, 3)
    one = whole[..., HALF:]
    keep = jnp.where(place.core == 0, zero, one)
    away = jnp.where(place.core == 0, one, zero).astype(jnp.bfloat16)
    total = keep + send(away, CORE).astype(jnp.float32)
    for axis, bit, route in (
        (2, place.first, FIRST),
        (2, place.second, SECOND),
        (1, place.near_z, NEAR_Z),
        (0, place.far_z, FAR_Z),
    ):
        away = pick(total, axis, 1 - bit).astype(jnp.bfloat16)
        total = pick(total, axis, bit) + send(away, route).astype(jnp.float32)
    own, other, at = [], [], 0
    for p in pieces:
        m, _, r2, _ = p.shape
        part = total[at : at + m * r2].reshape(m, 2, r2 // 2, HALF)
        own.append(pick(part, 1, place.core).reshape(-1, HALF))
        other.append(pick(part, 1, 1 - place.core).reshape(-1, HALF))
        at += m * r2
    own = jnp.concatenate(own, axis=0)
    came = send(jnp.concatenate(other, axis=0), CORE)
    both = jnp.swapaxes(join(own, came, 0, place.core), 0, 1).reshape(-1, D)
    out, at = [], 0
    for p in pieces:
        m, _, r2, _ = p.shape
        count = m * (r2 // 2)
        out.append(both[at : at + count].reshape(m, r2 // 2, D))
        at += count
    return out


def gather_units(unit_low, place):
    zero, one = cores(spread(unit_low, place), place)
    return jnp.stack([zero, one], axis=4).reshape(-1, D)


def pad_row(parts):
    row = jnp.concatenate(parts)
    return jnp.pad(row, (0, 8 * D - row.shape[0])).reshape(1, 8, D)


def cube_gather(weights, vectors, partners, place):
    w_query, w_key, w_value, w_output, w_inner, w_outer = weights
    r = w_query.shape[0]
    low = jnp.bfloat16
    codes = [(partners % 64).astype(low), (partners // 64).astype(low)]
    row = pad_row(list(vectors) + codes)
    attn, rows = gather_rows([jnp.stack([w_query, w_key, w_value, w_output]), row], place)
    (inner,) = gather_rows([jnp.swapaxes(w_inner.reshape(r, 4, D), 0, 1)], place)
    (outer,) = gather_rows([w_outer[None]], place)
    attn = attn.reshape(4, D, D)
    inner = jnp.swapaxes(inner.reshape(4, D, D), 0, 1).reshape(D, 4 * D)
    outer = outer.reshape(4 * D, D)
    rows = rows.reshape(CUBE, 8 * D)
    full, at = [], 0
    for v in list(vectors):
        full.append(rows[:, at : at + v.shape[0]].reshape(-1))
        at += v.shape[0]
    count = partners.shape[0]
    low_code = rows[:, at : at + count].astype(jnp.int32).reshape(-1)
    high_code = rows[:, at + count : at + 2 * count].astype(jnp.int32).reshape(-1)
    return (attn[0], attn[1], attn[2], attn[3], inner, outer), full, low_code + 64 * high_code


def cut_rows(full):
    return full.reshape(1, CUBE // 2, -1, D)


def vector_rows(vectors):
    rows = jnp.concatenate([v.reshape(CUBE, -1) for v in vectors], axis=1)
    rows = jnp.pad(rows, ((0, 0), (0, 8 * D - rows.shape[1])))
    return rows.reshape(1, CUBE // 2, 16, D)


def own_vectors(row, vectors):
    row, out, at = row.reshape(-1), [], 0
    for v in vectors:
        count = v.shape[0] // CUBE
        out.append(row[at : at + count])
        at += count
    return out


def local(
    tokens,
    lengths,
    partners,
    out_cotangent,
    w_query,
    w_key,
    w_value,
    w_output,
    b_query,
    b_value,
    b_output,
    gain_attn,
    shift_attn,
    w_inner,
    b_inner,
    w_outer,
    b_outer,
    gain_ffn,
    shift_ffn,
):
    devices = lax.axis_size(AXIS)
    cube = devices == CUBE
    place = Place() if cube else None
    count = tokens.shape[0]
    half = count // 2
    shape_four = (count, LEN, HEADS, HEAD_DIM)
    token_rows = tokens.reshape(count * LEN, D)
    positions = jnp.arange(LEN, dtype=jnp.int32)
    visible = (positions[None, :] < lengths[:, None])[:, None, None, :]
    weights = (w_query, w_key, w_value, w_output, w_inner, w_outer)
    vectors = (b_query, b_value, b_output, gain_attn, shift_attn, b_inner, b_outer, gain_ffn, shift_ffn)
    if cube:
        full, vec, all_partners = cube_gather(weights, vectors, partners, place)
    else:
        full, vec, all_partners = jax.tree.map(
            lambda v: lax.all_gather(v, AXIS, axis=0, tiled=True), (weights, vectors, partners)
        )
    query_mat, key_mat, value_mat, output_mat, inner_mat, outer_mat = full
    (
        query_bias,
        value_bias,
        output_bias,
        attn_gain,
        attn_shift,
        inner_bias,
        outer_bias,
        ffn_gain,
        ffn_shift,
    ) = vec
    queries = (project(token_rows, query_mat) + query_bias).astype(jnp.bfloat16).reshape(shape_four)
    key_rows = project(token_rows, key_mat).astype(jnp.bfloat16).reshape(shape_four)
    value_rows = (
        (project(token_rows, value_mat) + value_bias).astype(jnp.bfloat16).reshape(shape_four)
    )
    scores = scores_of(queries, key_rows, visible)
    row_top = jnp.max(scores, axis=-1, keepdims=True)
    expd = jnp.exp(scores - row_top)
    row_total = jnp.sum(expd, axis=-1, keepdims=True)
    probs = expd / row_total
    score_lse = row_top + jnp.log(row_total)
    context = jnp.einsum(
        "bhqk,bkhd->bqhd",
        probs.astype(jnp.bfloat16),
        value_rows,
        preferred_element_type=jnp.float32,
    )
    context = context.astype(jnp.bfloat16).reshape(count * LEN, D)
    resid_attn = token_rows.astype(jnp.float32) + (project(context, output_mat) + output_bias)
    normed_attn = scaled_norm(resid_attn, attn_gain.astype(jnp.float32)) + attn_shift
    normed_low = normed_attn.astype(jnp.bfloat16)
    hidden_pre = project(normed_low, inner_mat) + inner_bias
    hidden_act = exact_gelu(hidden_pre).astype(jnp.bfloat16)
    resid_ffn = normed_attn + (project(hidden_act, outer_mat) + outer_bias)
    block_rows = scaled_norm(resid_ffn, ffn_gain.astype(jnp.float32)) + ffn_shift
    block_out = block_rows.astype(jnp.bfloat16).reshape(count, LEN, D)
    cls_rows = block_rows.reshape(count, LEN, D)[:, 0, :]
    unit, pool_back = jax.vjp(normalize, cls_rows)
    unit_low = unit.astype(jnp.bfloat16)
    if cube:
        every_unit = gather_units(unit_low, place)
    else:
        every_unit = lax.all_gather(unit_low, AXIS, axis=0, tiled=True)
    every_pair = every_unit.reshape(every_unit.shape[0] // 2, 2, D)
    all_sources = every_pair[:, 0, :]
    all_targets = every_pair[:, 1, :]
    npairs = all_targets.shape[0]
    sims = project_back(all_sources, all_targets) * sim_scale
    matched = all_partners[:, None] == jnp.arange(npairs, dtype=jnp.int32)[None, :]
    sims = sims - jnp.where(matched, sim_scale * sim_margin, 0.0)
    row_top = jnp.max(sims, axis=1, keepdims=True)
    row_lse = row_top + jnp.log(jnp.sum(jnp.exp(sims - row_top), axis=1, keepdims=True))
    col_top = jnp.max(sims, axis=0, keepdims=True)
    col_lse = col_top + jnp.log(jnp.sum(jnp.exp(sims - col_top), axis=0, keepdims=True))
    positive = jnp.sum(jnp.where(matched, sims, 0.0))
    loss = (jnp.sum(row_lse) + jnp.sum(col_lse) - 2.0 * positive) / (2.0 * npairs)
    d_sims = 0.5 * (jnp.exp(sims - row_lse) + jnp.exp(sims - col_lse)) - jnp.where(
        matched, 1.0, 0.0
    )
    d_sims_low = (d_sims * sim_scale).astype(jnp.bfloat16)
    first = lax.axis_index(AXIS) * half
    d_source = project(lax.dynamic_slice_in_dim(d_sims_low, first, half, 0), all_targets)
    d_target = weight_grad(lax.dynamic_slice_in_dim(d_sims_low, first, half, 1), all_sources)
    d_unit = jnp.stack([d_source, d_target], axis=1).reshape(count, D)
    (d_cls,) = pool_back(d_unit)
    d_block = out_cotangent.astype(jnp.float32).at[:, 0, :].add(d_cls).reshape(count * LEN, D)
    _, ffn_norm_back = jax.vjp(scaled_norm, resid_ffn, ffn_gain.astype(jnp.float32))
    d_resid_ffn, d_ffn_gain = ffn_norm_back(d_block)
    d_ffn_shift = jnp.sum(d_block, axis=0)
    d_branch = d_resid_ffn.astype(jnp.bfloat16)
    d_outer_bias = column_sum(d_branch)
    d_outer_mat = weight_grad(hidden_act, d_branch)
    d_act = project_back(d_branch, outer_mat)
    _, gelu_back = jax.vjp(exact_gelu, hidden_pre)
    (d_pre,) = gelu_back(d_act)
    d_hidden = d_pre.astype(jnp.bfloat16)
    d_inner_mat = weight_grad(normed_low, d_hidden)
    d_inner_bias = column_sum(d_hidden)
    d_normed = d_resid_ffn + project_back(d_hidden, inner_mat)
    if cube:
        ((g_outer,),) = (scatter_rows([cut_rows(d_outer_mat)], place),)
        (g_inner,) = scatter_rows(
            [jnp.swapaxes(d_inner_mat.reshape(D, 4, D), 0, 1).reshape(4, CUBE // 2, -1, D)], place
        )
        grad_w_outer = g_outer[0]
        grad_w_inner = jnp.swapaxes(g_inner, 0, 1).reshape(-1, 4 * D)
    _, attn_norm_back = jax.vjp(scaled_norm, resid_attn, attn_gain.astype(jnp.float32))
    d_resid_attn, d_attn_gain = attn_norm_back(d_normed)
    d_attn_shift = jnp.sum(d_normed, axis=0)
    d_attn_out = d_resid_attn.astype(jnp.bfloat16)
    d_output_bias = column_sum(d_attn_out)
    d_output_mat = weight_grad(context, d_attn_out)
    d_context = project_back(d_attn_out, output_mat).astype(jnp.bfloat16).reshape(shape_four)
    probs_again = jnp.exp(scores_of(queries, key_rows, visible) - score_lse)
    d_probs = jnp.einsum(
        "bqhd,bkhd->bhqk", d_context, value_rows, preferred_element_type=jnp.float32
    )
    d_values = jnp.einsum(
        "bhqk,bqhd->bkhd",
        probs_again.astype(jnp.bfloat16),
        d_context,
        preferred_element_type=jnp.float32,
    )
    d_values = d_values.astype(jnp.bfloat16).reshape(count * LEN, D)
    d_scores = (
        probs_again * (d_probs - jnp.sum(probs_again * d_probs, axis=-1, keepdims=True))
    ).astype(jnp.bfloat16)
    d_queries = jnp.einsum(
        "bhqk,bkhd->bqhd", d_scores, key_rows, preferred_element_type=jnp.float32
    ) * HEAD_DIM ** (-0.5)
    d_queries = d_queries.astype(jnp.bfloat16).reshape(count * LEN, D)
    d_keys = jnp.einsum(
        "bhqk,bqhd->bkhd", d_scores, queries, preferred_element_type=jnp.float32
    ) * HEAD_DIM ** (-0.5)
    d_keys = d_keys.astype(jnp.bfloat16).reshape(count * LEN, D)
    d_query_mat = weight_grad(token_rows, d_queries)
    d_key_mat = weight_grad(token_rows, d_keys)
    d_value_mat = weight_grad(token_rows, d_values)
    d_query_bias = column_sum(d_queries)
    d_value_bias = column_sum(d_values)
    grad_rows = (
        d_resid_attn
        + project_back(d_queries, query_mat)
        + project_back(d_keys, key_mat)
        + project_back(d_values, value_mat)
    )
    d_vectors = (
        d_query_bias,
        d_value_bias,
        d_output_bias,
        d_attn_gain,
        d_attn_shift,
        d_inner_bias,
        d_outer_bias,
        d_ffn_gain,
        d_ffn_shift,
    )
    if cube:
        mats = jnp.stack([d_query_mat, d_key_mat, d_value_mat, d_output_mat])
        g_attn, g_row = scatter_rows(
            [mats.reshape(4, CUBE // 2, -1, D), vector_rows(d_vectors)], place
        )
        grad_w_query, grad_w_key, grad_w_value, grad_w_output = (g_attn[i] for i in range(4))
        grads = own_vectors(g_row, d_vectors)
    else:

        def scatter(v):
            return lax.psum_scatter(v, AXIS, scatter_dimension=0, tiled=True)

        grad_w_query, grad_w_key, grad_w_value, grad_w_output, grad_w_inner, grad_w_outer = (
            scatter(v)
            for v in (d_query_mat, d_key_mat, d_value_mat, d_output_mat, d_inner_mat, d_outer_mat)
        )
        grads = [scatter(v) for v in d_vectors]
    (
        grad_b_query,
        grad_b_value,
        grad_b_output,
        grad_gain_attn,
        grad_shift_attn,
        grad_b_inner,
        grad_b_outer,
        grad_gain_ffn,
        grad_shift_ffn,
    ) = grads
    return (
        loss,
        block_out,
        grad_rows.reshape(count, LEN, D),
        grad_w_query,
        grad_w_key,
        grad_w_value,
        grad_w_output,
        grad_b_query,
        grad_b_value,
        grad_b_output,
        grad_gain_attn,
        grad_shift_attn,
        grad_w_inner,
        grad_b_inner,
        grad_w_outer,
        grad_b_outer,
        grad_gain_ffn,
        grad_shift_ffn,
    )


def solution(mesh):
    rows, cols = P(AXIS), P(AXIS, None)
    cube = P(AXIS, None, None)
    in_specs = (cube, rows, rows, cube) + (cols,) * 4 + (rows,) * 5 + (cols, rows, cols) + (rows,) * 3
    out_specs = (P(), cube, cube) + (cols,) * 4 + (rows,) * 5 + (cols, rows, cols) + (rows,) * 3
    return jax.shard_map(local, mesh=mesh, in_specs=in_specs, out_specs=out_specs, check_vma=False)
```

```python
import jax
import jax.numpy as jnp
from jax import lax
from jax.experimental import pallas as pl
from jax.experimental.pallas import tpu as pltpu
from jax.sharding import PartitionSpec as P

D = 768
HEADS = 12
HEAD_DIM = 64
LEN = 64
FF = 3072
QUAD = 4
WIDE = QUAD * HEAD_DIM
ROWS = 256
norm_eps = 1e-12
f32, low = jnp.float32, jnp.bfloat16


def nn(a, b):
    return lax.dot_general(a, b, (((1,), (0,)), ((), ())), preferred_element_type=f32)


def nt(a, b):
    return lax.dot_general(a, b, (((1,), (1,)), ((), ())), preferred_element_type=f32)


def tn(a, b):
    return lax.dot_general(a, b, (((0,), (0,)), ((), ())), preferred_element_type=f32)


def head_masks(dtype):
    lane = lax.broadcasted_iota(jnp.int32, (1, WIDE), 1) // HEAD_DIM
    return [jnp.where(lane == h, 1.0, 0.0).astype(dtype) for h in range(QUAD)]


def stacked(rows, masks):
    return jnp.concatenate([rows * m for m in masks], axis=0)


def unstacked(full, masks):
    return sum(full[LEN * h : LEN * (h + 1)] * m for h, m in enumerate(masks))


def attn_forward_body(len_ref, x_ref, wq_ref, wk_ref, wv_ref, wo_ref, vec_ref,
                      q_ref, k_ref, v_ref, p_ref, c_ref, hat_ref, inv_ref, n_ref):
    x = x_ref[...]
    q_ref[...] = (nn(x, wq_ref[...]) + vec_ref[0:1]).astype(low)
    k_ref[...] = nn(x, wk_ref[...]).astype(low)
    v_ref[...] = (nn(x, wv_ref[...]) + vec_ref[1:2]).astype(low)
    masks, masks32 = head_masks(low), head_masks(f32)
    per = ROWS // LEN
    first = pl.program_id(0) * per
    key_at = lax.broadcasted_iota(jnp.int32, (LEN, WIDE), 0)

    @pl.loop(0, per)
    def _(s):
        rows = pl.ds(pl.multiple_of(s * LEN, LEN), LEN)
        seen = key_at < len_ref[first + s]
        for g in range(HEADS // QUAD):
            cols = pl.ds(g * WIDE, WIDE)
            q, k, v = q_ref[rows, cols], k_ref[rows, cols], v_ref[rows, cols]
            scores = nt(k, stacked(q, masks)) * HEAD_DIM ** (-0.5)
            scores = jnp.where(seen, scores, -1e30)
            expd = jnp.exp(scores - jnp.max(scores, axis=0, keepdims=True))
            probs = expd / jnp.sum(expd, axis=0, keepdims=True)
            p_ref[pl.ds(pl.multiple_of((s * 3 + g) * LEN, LEN), LEN), :] = probs
            c_ref[rows, cols] = unstacked(tn(probs.astype(low), v), masks32).astype(low)

    resid = x.astype(f32) + (nn(c_ref[...], wo_ref[...]) + vec_ref[2:3])
    centred = resid - jnp.mean(resid, axis=-1, keepdims=True)
    inv = lax.rsqrt(jnp.mean(centred * centred, axis=-1, keepdims=True) + norm_eps)
    hat = centred * inv
    hat_ref[...] = hat
    inv_ref[...] = inv
    n_ref[...] = (hat * vec_ref[3:4] + vec_ref[4:5]).astype(low)


def whole(shape):
    return pl.BlockSpec(shape, lambda *_: (0,) * len(shape), pipeline_mode=pl.Buffered(1))


def attn_forward(lengths, x, wq, wk, wv, wo, vec):
    t = x.shape[0]
    row = lambda w: pl.BlockSpec((ROWS, w), lambda i, *_: (i, 0))
    mat = whole((D, D))
    S = jax.ShapeDtypeStruct
    return pl.pallas_call(
        attn_forward_body,
        grid_spec=pltpu.PrefetchScalarGridSpec(
            num_scalar_prefetch=1, grid=(t // ROWS,),
            in_specs=[row(D), mat, mat, mat, mat, whole(vec.shape)],
            out_specs=[row(D), row(D), row(D), pl.BlockSpec((3 * ROWS, WIDE), lambda i, *_: (i, 0)),
                       row(D), row(D), row(1), row(D)]),
        out_shape=[S((t, D), low)] * 3 + [S((3 * t, WIDE), f32), S((t, D), low), S((t, D), f32), S((t, 1), f32), S((t, D), low)],
        compiler_params=pltpu.CompilerParams(vmem_limit_bytes=50 << 20),
        name="attn_forward",
    )(lengths, x, wq, wk, wv, wo, vec)


def gelu_parts(h):
    z = jnp.abs(h) * 0.7071067811865476
    t = 1.0 / (1.0 + 0.3275911 * z)
    poly = t * (0.254829592 + t * (-0.284496736 + t * (1.421413741 + t * (-1.453152027 + t * 1.061405429))))
    bell = jnp.exp(-0.5 * h * h)
    tail = 0.5 * poly * bell
    cdf = jnp.where(h >= 0, 1.0 - tail, tail)
    return h * cdf, cdf + h * bell * 0.3989422804014327


FBLK = 512

def ffn_forward_body(hat_ref, n_ref, wi_ref, bi_ref, wo_ref, vec_ref,
                     a_ref, gp_ref, out_ref, hat2_ref, inv_ref, cls_ref, acc_ref):
    n = n_ref[...]
    for j in range(FF // FBLK):
        cols = pl.ds(j * FBLK, FBLK)
        h = nn(n, wi_ref[:, cols]) + bi_ref[:, cols]
        act, grad = gelu_parts(h)
        act = act.astype(low)
        a_ref[:, cols] = act
        gp_ref[:, cols] = grad.astype(low)
        part = nn(act, wo_ref[cols, :])
        if j == 0:
            acc_ref[...] = part
        else:
            acc_ref[...] += part
    normed = hat_ref[...] * vec_ref[3:4] + vec_ref[4:5]
    resid = normed + (acc_ref[...] + vec_ref[5:6])
    centred = resid - jnp.mean(resid, axis=-1, keepdims=True)
    inv = lax.rsqrt(jnp.mean(centred * centred, axis=-1, keepdims=True) + norm_eps)
    hat = centred * inv
    hat2_ref[...] = hat
    inv_ref[...] = inv
    rows = hat * vec_ref[6:7] + vec_ref[7:8]
    out_ref[...] = rows.astype(low)
    per = rows.shape[0] // LEN
    for s in range(per):
        cls_ref[pl.ds(pl.program_id(0) * per + s, 1), :] = rows[LEN * s : LEN * s + 1]


def ffn_forward(hat, n, wi, bi, wo, vec):
    t = hat.shape[0]
    R = 256
    row = lambda w: pl.BlockSpec((R, w), lambda i: (i, 0))
    S = jax.ShapeDtypeStruct
    return pl.pallas_call(
        ffn_forward_body,
        grid=(t // R,),
        in_specs=[row(D), row(D), whole((D, FF)), whole((1, FF)), whole((FF, D)), whole(vec.shape)],
        out_specs=[row(FF), row(FF), row(D), row(D), row(1), pl.BlockSpec((t // LEN, D), lambda i: (0, 0))],
        out_shape=[S((t, FF), low), S((t, FF), low), S((t, D), low), S((t, D), f32), S((t, 1), f32), S((t // LEN, D), f32)],
        scratch_shapes=[pltpu.VMEM((R, D), f32)],
        compiler_params=pltpu.CompilerParams(vmem_limit_bytes=60 << 20),
        name="ffn_forward",
    )(hat, n, wi, bi, wo, vec)


def ffn_backward_body(cot_ref, dc_ref, hat2_ref, inv2_ref, n_ref, a_ref, gp_ref, wi_ref, wo_ref, vec_ref,
                      dn_ref, dwi_ref, dwo_ref, dbi_ref, sums_ref, dbr_ref):
    j = pl.program_id(0)

    @pl.when(j == 0)
    def _():
        dgain = jnp.zeros((1, D), f32)
        dshift = jnp.zeros((1, D), f32)
        dbias = jnp.zeros((1, D), f32)
        R = 256
        head = lax.broadcasted_iota(jnp.int32, (R, D), 0)
        for b in range(cot_ref.shape[0] // R):
            rows = pl.ds(b * R, R)
            cot = cot_ref[rows, :].astype(f32)
            hat = hat2_ref[rows, :]
            extra = jnp.zeros((R, D), f32)
            for s in range(R // LEN):
                at = b * (R // LEN) + s
                extra = jnp.where(head == LEN * s, dc_ref[at : at + 1], extra)
            d = cot + extra
            dgain += jnp.sum(d * hat, axis=0, keepdims=True)
            dshift += jnp.sum(d, axis=0, keepdims=True)
            dh = d * vec_ref[6:7]
            m1 = jnp.mean(dh, axis=-1, keepdims=True)
            m2 = jnp.mean(dh * hat, axis=-1, keepdims=True)
            dres = (dh - m1 - hat * m2) * inv2_ref[rows, :]
            dn_ref[rows, :] = dres
            dbr = dres.astype(low)
            dbr_ref[rows, :] = dbr
            dbias += jnp.sum(dbr.astype(f32), axis=0, keepdims=True)
        sums_ref[...] = jnp.concatenate([dbias, dgain, dshift, jnp.zeros((5, D), f32)], axis=0)

    dbr = dbr_ref[...]
    dact = nt(dbr, wo_ref[...])
    dh = gp_ref[...].astype(f32) * dact
    dhb = dh.astype(low)
    dbi_ref[...] = jnp.sum(dhb.astype(f32), axis=0, keepdims=True)
    dwo_ref[...] = tn(a_ref[...], dbr)
    dwi_ref[...] = tn(n_ref[...], dhb)
    dn_ref[...] += nt(dhb, wi_ref[...])


def ffn_backward(cot, dc, hat2, inv2, n, a, gp, wi, wo, vec):
    t = cot.shape[0]
    J = FF // FBLK
    S = jax.ShapeDtypeStruct
    fblk = pl.BlockSpec((t, FBLK), lambda j: (0, j))
    return pl.pallas_call(
        ffn_backward_body,
        grid=(J,),
        in_specs=[whole((t, D)), whole(dc.shape), whole((t, D)), whole((t, 1)), whole((t, D)), fblk, fblk,
                  pl.BlockSpec((D, FBLK), lambda j: (0, j)), pl.BlockSpec((FBLK, D), lambda j: (j, 0)), whole(vec.shape)],
        out_specs=[whole((t, D)), pl.BlockSpec((D, FBLK), lambda j: (0, j)), pl.BlockSpec((FBLK, D), lambda j: (j, 0)),
                   pl.BlockSpec((1, FBLK), lambda j: (0, j)), whole((8, D))],
        out_shape=[S((t, D), f32), S((D, FF), f32), S((FF, D), f32), S((1, FF), f32), S((8, D), f32)],
        scratch_shapes=[pltpu.VMEM((t, D), low)],
        compiler_params=pltpu.CompilerParams(vmem_limit_bytes=60 << 20),
        name="ffn_backward",
    )(cot, dc, hat2, inv2, n, a, gp, wi, wo, vec)


def attn_backward_body(dn_ref, hat_ref, inv_ref, wo_ref, q_ref, k_ref, v_ref, p_ref, c_ref, vec_ref,
                       dr_ref, dq_ref, dk_ref, dv_ref, dwo_ref, sums_ref, dc_ref):
    i = pl.program_id(0)
    dn, hat = dn_ref[...], hat_ref[...]
    dhat = dn * vec_ref[3:4]
    m1 = jnp.mean(dhat, axis=-1, keepdims=True)
    m2 = jnp.mean(dhat * hat, axis=-1, keepdims=True)
    dres = (dhat - m1 - hat * m2) * inv_ref[...]
    dr_ref[...] = dres
    dao = dres.astype(low)
    dc_ref[...] = nt(dao, wo_ref[...]).astype(low)
    dwo = tn(c_ref[...], dao)

    @pl.when(i == 0)
    def _():
        sums_ref[...] = jnp.zeros_like(sums_ref)
        dwo_ref[...] = jnp.zeros_like(dwo_ref)

    dwo_ref[...] += dwo
    sums_ref[2:3] += jnp.sum(dao.astype(f32), axis=0, keepdims=True)
    sums_ref[3:4] += jnp.sum(dn * hat, axis=0, keepdims=True)
    sums_ref[4:5] += jnp.sum(dn, axis=0, keepdims=True)
    masks, masks32 = head_masks(low), head_masks(f32)
    per = ROWS // LEN

    @pl.loop(0, per)
    def _(s):
        rows = pl.ds(pl.multiple_of(s * LEN, LEN), LEN)
        for g in range(HEADS // QUAD):
            cols = pl.ds(g * WIDE, WIDE)
            q, k, v, dc = q_ref[rows, cols], k_ref[rows, cols], v_ref[rows, cols], dc_ref[rows, cols]
            p = p_ref[pl.ds(pl.multiple_of((s * 3 + g) * LEN, LEN), LEN), :]
            dcs = stacked(dc, masks)
            dp = nt(v, dcs)
            dv_ref[rows, cols] = nn(p.astype(low), dcs).astype(low)
            ds = (p * (dp - jnp.sum(p * dp, axis=0, keepdims=True))).astype(low)
            dk_ref[rows, cols] = (nn(ds, stacked(q, masks)) * HEAD_DIM ** (-0.5)).astype(low)
            dq_ref[rows, cols] = (unstacked(tn(ds, k), masks32) * HEAD_DIM ** (-0.5)).astype(low)

    sums_ref[0:1] += jnp.sum(dq_ref[...].astype(f32), axis=0, keepdims=True)
    sums_ref[1:2] += jnp.sum(dv_ref[...].astype(f32), axis=0, keepdims=True)


def attn_backward(dn, hat, inv, wo, q, k, v, p, c, vec):
    t = dn.shape[0]
    row = lambda w: pl.BlockSpec((ROWS, w), lambda i: (i, 0))
    S = jax.ShapeDtypeStruct
    return pl.pallas_call(
        attn_backward_body,
        grid=(t // ROWS,),
        in_specs=[row(D), row(D), row(1), whole((D, D)), row(D), row(D), row(D),
                  pl.BlockSpec((3 * ROWS, WIDE), lambda i: (i, 0)), row(D), whole(vec.shape)],
        out_specs=[row(D), row(D), row(D), row(D), whole((D, D)), whole((8, D))],
        out_shape=[S((t, D), f32)] + [S((t, D), low)] * 3 + [S((D, D), f32), S((8, D), f32)],
        scratch_shapes=[pltpu.VMEM((ROWS, D), low)],
        compiler_params=pltpu.CompilerParams(vmem_limit_bytes=50 << 20),
        name="attn_backward",
    )(dn, hat, inv, wo, q, k, v, p, c, vec)


def attn_weights_body(x_ref, dq_ref, dk_ref, dv_ref, o_ref):
    x = x_ref[...]
    o_ref[0] = tn(x, dq_ref[...])
    o_ref[1] = tn(x, dk_ref[...])
    o_ref[2] = tn(x, dv_ref[...])


def attn_weights(x, dq, dk, dv):
    t = x.shape[0]
    N = 256
    col = pl.BlockSpec((t, N), lambda j: (0, j))
    return pl.pallas_call(
        attn_weights_body, grid=(D // N,),
        in_specs=[whole((t, D)), col, col, col],
        out_specs=pl.BlockSpec((3, D, N), lambda j: (0, 0, j)),
        out_shape=jax.ShapeDtypeStruct((3, D, D), f32),
        compiler_params=pltpu.CompilerParams(vmem_limit_bytes=50 << 20),
        name="attn_weights",
    )(x, dq, dk, dv)


def token_grad_body(dr_ref, dq_ref, dk_ref, dv_ref, wq_ref, wk_ref, wv_ref, o_ref):
    o_ref[...] = dr_ref[...] + nt(dq_ref[...], wq_ref[...]) + nt(dk_ref[...], wk_ref[...]) + nt(dv_ref[...], wv_ref[...])


def token_grad(dr, dq, dk, dv, wq, wk, wv):
    t = dr.shape[0]
    row = pl.BlockSpec((ROWS, D), lambda i: (i, 0))
    return pl.pallas_call(
        token_grad_body, grid=(t // ROWS,),
        in_specs=[row] * 4 + [whole((D, D))] * 3, out_specs=row,
        out_shape=jax.ShapeDtypeStruct((t, D), f32),
        compiler_params=pltpu.CompilerParams(vmem_limit_bytes=50 << 20),
        name="token_grad",
    )(dr, dq, dk, dv, wq, wk, wv)


pool_eps = 1e-06
sim_scale = 50.0
sim_margin = 0.3
HALF = D // 2

AXIS = "fsdp"
CUBE = 32
CHIPS = CUBE // 2
CORE = [(i, i ^ 1) for i in range(CUBE)]
FAR_Z = [(i, i ^ 16) for i in range(CUBE)]
NEAR_Z = [(i, i ^ 8) for i in range(CUBE)]
FIRST = [(i, i ^ (4 if i & 1 else 2)) for i in range(CUBE)]
SECOND = [(i, i ^ (2 if i & 1 else 4)) for i in range(CUBE)]


def normalize(field):
    return field * lax.rsqrt(jnp.sum(field * field, axis=-1, keepdims=True) + pool_eps)


class Place:
    def __init__(self):
        me = lax.axis_index(AXIS)
        self.core = me & 1
        x, y = (me >> 1) & 1, (me >> 2) & 1
        self.near_z, self.far_z = (me >> 3) & 1, (me >> 4) & 1
        self.first = jnp.where(self.core == 0, x, y)
        self.second = jnp.where(self.core == 0, y, x)


def join(own, other, axis, bit):
    shape = own.shape[:axis] + (2,) + own.shape[axis:]
    where = lax.broadcasted_iota(jnp.int32, shape, axis)
    return jnp.where(where == bit, jnp.expand_dims(own, axis), jnp.expand_dims(other, axis))


def pick(field, axis, bit):
    return lax.dynamic_index_in_dim(field, bit, axis, keepdims=False)


def send(field, route):
    return lax.ppermute(field, AXIS, route)


def spread(block, place):
    block = join(block, send(block, FAR_Z), 0, place.far_z)
    block = join(block, send(block, NEAR_Z), 1, place.near_z)
    block = join(block, send(block, FIRST), 2, place.first)
    return join(block, send(block, SECOND), 3, place.second)


def cores(block, place):
    other = send(block, CORE)
    zero = jnp.where(place.core == 0, block, other)
    one = jnp.where(place.core == 0, other, block)
    return jnp.swapaxes(zero, 2, 3), one


def gather_columns(pieces, place):
    half = pieces[0].shape[-1] // 2
    mine, away = [], []
    for piece in pieces:
        halves = piece.reshape(piece.shape[0], piece.shape[1], 2, half)
        mine.append(pick(halves, 2, place.core))
        away.append(pick(halves, 2, 1 - place.core).reshape(-1, half))
    came = send(jnp.concatenate(away, axis=0), CORE)
    rows, at = [], 0
    for own in mine:
        count = own.shape[0] * own.shape[1]
        other = came[at : at + count].reshape(own.shape)
        rows.append(join(own, other, 1, place.core).reshape(-1, half))
        at += count
    zero, one = cores(spread(jnp.concatenate(rows, axis=0), place), place)
    out, at = [], 0
    for piece in pieces:
        m, r, _ = piece.shape
        count = 2 * m * r
        both = jnp.concatenate(
            [part[..., at : at + count, :].reshape(CHIPS, m, 2 * r, half) for part in (zero, one)],
            axis=-1,
        )
        out.append(jnp.swapaxes(both, 0, 1))
        at += count
    return out


def gather_blocks(block, place):
    zero, one = cores(spread(block, place), place)
    return jnp.stack([zero, one], axis=4).reshape(-1, block.shape[-1])


def reduce_chips(keep, away, place):
    total = keep.astype(f32) + send(away.astype(low), CORE).astype(f32)
    for axis, bit, route in (
        (2, place.first, FIRST),
        (2, place.second, SECOND),
        (1, place.near_z, NEAR_Z),
        (0, place.far_z, FAR_Z),
    ):
        away = pick(total, axis, 1 - bit).astype(low)
        total = pick(total, axis, bit) + send(away, route).astype(f32)
    return total


def shares(zero, one, place):
    zero = jnp.swapaxes(zero, 2, 3)
    return jnp.where(place.core == 0, zero, one), jnp.where(place.core == 0, one, zero)


def scatter_columns(pieces, place):
    half = pieces[0].shape[-1] // 2
    whole = jnp.concatenate(
        [jnp.swapaxes(p, 0, 1).reshape(CHIPS, -1, 2 * half) for p in pieces], axis=1
    )
    whole = whole.reshape(2, 2, 2, 2, whole.shape[1], 2 * half)
    total = reduce_chips(*shares(whole[..., :half], whole[..., half:], place), place)
    own, other, at = [], [], 0
    for p in pieces:
        m, _, r2, _ = p.shape
        part = total[at : at + m * r2].reshape(m, 2, r2 // 2, half)
        own.append(pick(part, 1, place.core).reshape(-1, half))
        other.append(pick(part, 1, 1 - place.core).reshape(-1, half))
        at += m * r2
    own = jnp.concatenate(own, axis=0)
    came = send(jnp.concatenate(other, axis=0), CORE)
    both = jnp.swapaxes(join(own, came, 0, place.core), 0, 1).reshape(-1, 2 * half)
    out, at = [], 0
    for p in pieces:
        m, _, r2, _ = p.shape
        count = m * (r2 // 2)
        out.append(both[at : at + count].reshape(m, r2 // 2, 2 * half))
        at += count
    return out


def scatter_blocks(full, place):
    whole = full.reshape(2, 2, 2, 2, 2, -1, full.shape[-1])
    return reduce_chips(*shares(whole[:, :, :, :, 0], whole[:, :, :, :, 1], place), place)


def cube_gather(weights, vectors, partners, place):
    w_query, w_key, w_value, w_output, w_inner, w_outer = weights
    codes = [(partners % 64).astype(low), (partners // 64).astype(low)]
    row = jnp.concatenate(list(vectors) + codes)
    row = jnp.pad(row, (0, 8 * D - row.shape[0])).reshape(1, 8, D)
    attn, rows = gather_columns([jnp.stack([w_query, w_key, w_value, w_output]), row], place)
    (inner,) = gather_columns([w_inner[None]], place)
    outer = gather_blocks(w_outer, place)
    attn = attn.reshape(4, D, D)
    rows = rows.reshape(CUBE, 8 * D)
    full, at = [], 0
    for v in list(vectors):
        full.append(rows[:, at : at + v.shape[0]].reshape(-1))
        at += v.shape[0]
    count = partners.shape[0]
    low_code = rows[:, at : at + count].astype(jnp.int32).reshape(-1)
    high_code = rows[:, at + count : at + 2 * count].astype(jnp.int32).reshape(-1)
    return (attn[0], attn[1], attn[2], attn[3], inner.reshape(D, FF), outer), full, low_code + 64 * high_code


def vector_rows(vectors):
    rows = jnp.concatenate([v.reshape(CUBE, -1) for v in vectors], axis=1)
    rows = jnp.pad(rows, ((0, 0), (0, 8 * D - rows.shape[1])))
    return rows.reshape(1, CHIPS, 16, D)


def own_vectors(row, vectors):
    row, out, at = row.reshape(-1), [], 0
    for v in vectors:
        count = v.shape[0] // CUBE
        out.append(row[at : at + count])
        at += count
    return out


def pair_loss(every_unit, partners, cls_rows, half):
    every_pair = every_unit.reshape(every_unit.shape[0] // 2, 2, D)
    all_sources, all_targets = every_pair[:, 0, :], every_pair[:, 1, :]
    npairs = all_targets.shape[0]
    sims = nt(all_sources, all_targets) * sim_scale
    matched = partners[:, None] == jnp.arange(npairs, dtype=jnp.int32)[None, :]
    sims = sims - jnp.where(matched, sim_scale * sim_margin, 0.0)
    row_top = jnp.max(sims, axis=1, keepdims=True)
    row_lse = row_top + jnp.log(jnp.sum(jnp.exp(sims - row_top), axis=1, keepdims=True))
    col_top = jnp.max(sims, axis=0, keepdims=True)
    col_lse = col_top + jnp.log(jnp.sum(jnp.exp(sims - col_top), axis=0, keepdims=True))
    positive = jnp.sum(jnp.where(matched, sims, 0.0))
    loss = (jnp.sum(row_lse) + jnp.sum(col_lse) - 2.0 * positive) / (2.0 * npairs)
    d_sims = 0.5 * (jnp.exp(sims - row_lse) + jnp.exp(sims - col_lse)) - jnp.where(matched, 1.0, 0.0)
    d_sims_low = (d_sims * sim_scale).astype(low)
    first = lax.axis_index(AXIS) * half
    d_source = nn(lax.dynamic_slice_in_dim(d_sims_low, first, half, 0), all_targets)
    d_target = tn(lax.dynamic_slice_in_dim(d_sims_low, first, half, 1), all_sources)
    d_unit = jnp.stack([d_source, d_target], axis=1).reshape(2 * half, D)
    _, pool_back = jax.vjp(normalize, cls_rows)
    (d_cls,) = pool_back(d_unit)
    return loss, d_cls


def local(
    tokens,
    lengths,
    partners,
    out_cotangent,
    w_query,
    w_key,
    w_value,
    w_output,
    b_query,
    b_value,
    b_output,
    gain_attn,
    shift_attn,
    w_inner,
    b_inner,
    w_outer,
    b_outer,
    gain_ffn,
    shift_ffn,
):
    cube = lax.axis_size(AXIS) == CUBE
    place = Place() if cube else None
    count = tokens.shape[0]
    x = tokens.reshape(count * LEN, D)
    weights = (w_query, w_key, w_value, w_output, w_inner, w_outer)
    vectors = (b_query, b_value, b_output, gain_attn, shift_attn, b_outer, gain_ffn, shift_ffn, b_inner)
    if cube:
        full, vecs, all_partners = cube_gather(weights, vectors, partners, place)
    else:
        full, vecs, all_partners = jax.tree.map(
            lambda v: lax.all_gather(v, AXIS, axis=0, tiled=True), (weights, vectors, partners)
        )
    query_mat, key_mat, value_mat, output_mat, inner_mat, outer_mat = full
    vec = jnp.stack(vecs[:8]).astype(f32)
    inner_bias = vecs[8].astype(f32).reshape(1, FF)
    queries, keys, values, probs, context, hat1, inv1, normed = attn_forward(
        lengths, x, query_mat, key_mat, value_mat, output_mat, vec
    )
    act, slope, block_out, hat2, inv2, cls_rows = ffn_forward(
        hat1, normed, inner_mat, inner_bias, outer_mat, vec
    )
    unit_low = normalize(cls_rows).astype(low)
    if cube:
        every_unit = gather_blocks(unit_low, place)
    else:
        every_unit = lax.all_gather(unit_low, AXIS, axis=0, tiled=True)
    loss, d_cls = pair_loss(every_unit, all_partners, cls_rows, count // 2)
    d_normed, d_inner_mat, d_outer_mat, d_inner_bias, sums_ffn = ffn_backward(
        out_cotangent.reshape(count * LEN, D), d_cls, hat2, inv2, normed, act, slope, inner_mat, outer_mat, vec
    )
    d_resid, d_queries, d_keys, d_values, d_output_mat, sums_attn = attn_backward(
        d_normed, hat1, inv1, output_mat, queries, keys, values, probs, context, vec
    )
    d_mats = attn_weights(x, d_queries, d_keys, d_values)
    grad_rows = token_grad(d_resid, d_queries, d_keys, d_values, query_mat, key_mat, value_mat)
    d_vectors = tuple(sums_attn[i] for i in range(5)) + tuple(sums_ffn[i] for i in range(3)) + (d_inner_bias[0],)
    if cube:
        grad_w_outer = scatter_blocks(d_outer_mat, place)
        (grad_w_inner,) = scatter_columns([d_inner_mat.reshape(1, CHIPS, -1, FF)], place)
        grad_w_inner = grad_w_inner[0]
        mats = jnp.concatenate([d_mats, d_output_mat[None]], axis=0)
        g_attn, g_row = scatter_columns(
            [mats.reshape(4, CHIPS, -1, D), vector_rows(d_vectors)], place
        )
        g_mats = [g_attn[i] for i in range(4)]
        grads = own_vectors(g_row, d_vectors)
    else:

        def scatter(v):
            return lax.psum_scatter(v, AXIS, scatter_dimension=0, tiled=True)

        g_mats = [scatter(v) for v in (d_mats[0], d_mats[1], d_mats[2], d_output_mat)]
        grad_w_inner, grad_w_outer = scatter(d_inner_mat), scatter(d_outer_mat)
        grads = [scatter(v) for v in d_vectors]
    (
        grad_b_query,
        grad_b_value,
        grad_b_output,
        grad_gain_attn,
        grad_shift_attn,
        grad_b_outer,
        grad_gain_ffn,
        grad_shift_ffn,
        grad_b_inner,
    ) = grads
    return (
        loss,
        block_out.reshape(count, LEN, D),
        grad_rows.reshape(count, LEN, D),
        *g_mats,
        grad_b_query,
        grad_b_value,
        grad_b_output,
        grad_gain_attn,
        grad_shift_attn,
        grad_w_inner,
        grad_b_inner,
        grad_w_outer,
        grad_b_outer,
        grad_gain_ffn,
        grad_shift_ffn,
    )


def solution(mesh):
    rows, cols = P(AXIS), P(AXIS, None)
    cube = P(AXIS, None, None)
    in_specs = (cube, rows, rows, cube) + (cols,) * 4 + (rows,) * 5 + (cols, rows, cols) + (rows,) * 3
    out_specs = (P(), cube, cube) + (cols,) * 4 + (rows,) * 5 + (cols, rows, cols) + (rows,) * 3
    return jax.shard_map(local, mesh=mesh, in_specs=in_specs, out_specs=out_specs, check_vma=False)
```

```python
import jax
import jax.numpy as jnp
from jax import lax
from jax.experimental import pallas as pl
from jax.experimental.pallas import tpu as pltpu
from jax.sharding import PartitionSpec as P

D = 768
HEADS = 12
HEAD_DIM = 64
LEN = 64
FF = 3072
QUAD = 4
WIDE = QUAD * HEAD_DIM
GROUPS = HEADS // QUAD
ROWS = 256
BLOCK = 768
AXIS = "fsdp"
norm_eps = 1e-12
pool_eps = 1e-06
sim_scale = 50.0
sim_margin = 0.3
f32, low = jnp.float32, jnp.bfloat16
S = jax.ShapeDtypeStruct

B_QUERY, B_VALUE, B_OUTPUT, G_ATTN, S_ATTN, B_OUTER, G_FFN, S_FFN, B_INNER = range(9)
CODES = B_INNER + FF // D


def nn(a, b):
    return lax.dot_general(a, b, (((1,), (0,)), ((), ())), preferred_element_type=f32)


def nt(a, b):
    return lax.dot_general(a, b, (((1,), (1,)), ((), ())), preferred_element_type=f32)


def tn(a, b):
    return lax.dot_general(a, b, (((0,), (0,)), ((), ())), preferred_element_type=f32)


def whole(shape):
    return pl.BlockSpec(shape, lambda *_: (0,) * len(shape), pipeline_mode=pl.Buffered(1))


def row_block(width, rows=ROWS):
    return pl.BlockSpec((rows, width), lambda i, *_: (i, 0))


def params(flops, nbytes, exps=0):
    return dict(
        compiler_params=pltpu.CompilerParams(vmem_limit_bytes=60 << 20),
        cost_estimate=pl.CostEstimate(flops=int(flops), bytes_accessed=int(nbytes), transcendentals=int(exps)),
    )


ANY = pl.BlockSpec(memory_space=pl.ANY)


def part_copies(parts, target, sems, cut):
    me = lax.axis_index(AXIS)
    core, x, y = me & 1, (me >> 1) & 1, (me >> 2) & 1

    def start(zero, one):
        for i in range(2):
            pltpu.make_async_copy(cut(zero[i]), target.at[:, (y + i) & 1, :, 0], sems.at[2 * i]).start()
            pltpu.make_async_copy(cut(one[i]), target.at[:, :, (x + i) & 1, 1], sems.at[2 * i + 1]).start()

    @pl.when(core == 0)
    def _():
        start(parts[:2], parts[2:])

    @pl.when(core == 1)
    def _():
        start(parts[2:], parts[:2])


def part_waits(parts, target, sems, cut):
    for i in range(2):
        pltpu.make_async_copy(cut(parts[i]), target.at[:, i, :, 0], sems.at[2 * i]).wait()
        pltpu.make_async_copy(cut(parts[i]), target.at[:, :, i, 1], sems.at[2 * i + 1]).wait()


def everything(ref):
    return ref


def project_body(cube, x_ref, vec_ref, *refs):
    parts, (q_ref, k_ref, v_ref, full_ref, w_ref, sems, out_sem) = refs[:-7], refs[-7:]
    step = pl.program_id(0)
    full_copy = pltpu.make_async_copy(w_ref, full_ref, out_sem)

    @pl.when(step == 0)
    def _():
        if cube:
            def cut(m):
                return lambda ref: ref.at[:, :, pl.ds(m * 24, 24), :]

            for m in range(4):
                part_copies(parts, w_ref.at[m], sems.at[m], cut(m))
            for m in range(4):
                part_waits(parts, w_ref.at[m], sems.at[m], cut(m))
        else:
            copy = pltpu.make_async_copy(parts[0], w_ref, sems.at[0, 0])
            copy.start()
            copy.wait()
        full_copy.start()

    x = x_ref[...]

    def mat(m):
        return w_ref.at[m].reshape(D, D)[...] if cube else w_ref[m]

    q_ref[...] = (nn(x, mat(0)) + vec_ref[B_QUERY : B_QUERY + 1].astype(f32)).astype(low)
    k_ref[...] = nn(x, mat(1)).astype(low)
    v_ref[...] = (nn(x, mat(2)) + vec_ref[B_VALUE : B_VALUE + 1].astype(f32)).astype(low)

    @pl.when(step == pl.num_programs(0) - 1)
    def _():
        full_copy.wait()


def project(x, vec, parts, cube):
    t = x.shape[0]
    shape = (4, 4, 2, 2, 2, 24, D) if cube else (4, D, D)
    q, k, v, full = pl.pallas_call(
        lambda *refs: project_body(cube, *refs),
        grid=(t // ROWS,),
        in_specs=[row_block(D), whole(vec.shape)] + [ANY] * len(parts),
        out_specs=[row_block(D)] * 3 + [ANY],
        out_shape=[S((t, D), low)] * 3 + [S(shape, low)],
        scratch_shapes=[pltpu.VMEM(shape, low), pltpu.SemaphoreType.DMA((4, 4)), pltpu.SemaphoreType.DMA],
        name="project",
        **params(6 * t * D * D, 8 * t * D + 16 * D * D),
    )(x, vec, *parts)
    return q, k, v, full.reshape(4, D, D)


def head_masks(dtype):
    lane = lax.broadcasted_iota(jnp.int32, (1, WIDE), 1) // HEAD_DIM
    return [jnp.where(lane == h, 1.0, 0.0).astype(dtype) for h in range(QUAD)]


def stacked(rows, masks):
    return jnp.concatenate([rows * m for m in masks], axis=0)


def unstacked(full, masks):
    return sum(full[LEN * h : LEN * (h + 1)] * m for h, m in enumerate(masks))


def table_rows(s, g):
    return pl.ds(pl.multiple_of((s * GROUPS + g) * LEN, LEN), LEN)


def layer_norm(resid):
    centred = resid - jnp.mean(resid, axis=-1, keepdims=True)
    inv = lax.rsqrt(jnp.mean(centred * centred, axis=-1, keepdims=True) + norm_eps)
    return centred * inv, inv


def layer_norm_back(grad, gain, hat, inv):
    grad = grad * gain
    mean = jnp.mean(grad, axis=-1, keepdims=True)
    along = jnp.mean(grad * hat, axis=-1, keepdims=True)
    return (grad - mean - hat * along) * inv


def attend_body(start, len_ref, x_ref, q_ref, k_ref, v_ref, wo_ref, vec_ref, *refs):
    p_ref, c_ref, hat_ref, inv_ref, n_ref = refs[-5:]
    masks, masks32 = head_masks(low), head_masks(f32)
    per = ROWS // LEN
    first = (start + pl.program_id(0)) * per
    key_at = lax.broadcasted_iota(jnp.int32, (LEN, WIDE), 0)

    def sentence(s):
        rows = pl.ds(pl.multiple_of(s * LEN, LEN), LEN)
        seen = key_at < len_ref[first + s]
        for g in range(GROUPS):
            cols = pl.ds(g * WIDE, WIDE)
            q, k, v = q_ref[rows, cols], k_ref[rows, cols], v_ref[rows, cols]
            scores = nt(k, stacked(q, masks)) * HEAD_DIM ** (-0.5)
            scores = jnp.where(seen, scores, -1e30)
            expd = jnp.exp(scores - jnp.max(scores, axis=0, keepdims=True))
            probs = expd * (1.0 / jnp.sum(expd, axis=0, keepdims=True))
            p_ref[table_rows(s, g), :] = probs
            c_ref[rows, cols] = unstacked(tn(probs.astype(low), v), masks32).astype(low)

    pl.loop(0, per, unroll=UNROLL)(sentence)
    branch = nn(c_ref[...], wo_ref[0]) + vec_ref[B_OUTPUT : B_OUTPUT + 1].astype(f32)
    hat, inv = layer_norm(x_ref[...].astype(f32) + branch)
    hat_ref[...] = hat
    inv_ref[...] = inv
    n_ref[...] = (hat * vec_ref[G_ATTN : G_ATTN + 1].astype(f32) + vec_ref[S_ATTN : S_ATTN + 1].astype(f32)).astype(low)


UNROLL = 2


def some_rows(start):
    return lambda width, rows=ROWS: pl.BlockSpec((rows, width), lambda i, *_: (start + i, 0))


def mat_of(m):
    return pl.BlockSpec((1, D, D), lambda *_: (m, 0, 0), pipeline_mode=pl.Buffered(1))


def attend(lengths, x, q, k, v, full, vec, start, count, before=()):
    t = x.shape[0]
    rows = some_rows(start)
    return pl.pallas_call(
        lambda *refs: attend_body(start, *refs),
        grid_spec=pltpu.PrefetchScalarGridSpec(
            num_scalar_prefetch=1,
            grid=(count,),
            in_specs=[rows(D)] * 4 + [mat_of(3), whole(vec.shape)] + [ANY] * len(before),
            out_specs=[rows(WIDE, GROUPS * ROWS), rows(D), rows(D), rows(1), rows(D)],
        ),
        out_shape=[S((GROUPS * t, WIDE), f32), S((t, D), low), S((t, D), f32), S((t, 1), f32), S((t, D), low)],
        input_output_aliases={7 + i: i for i in range(len(before))},
        name="attend",
        **params(12 * count * ROWS * D * D, 26 * count * ROWS * D, count * ROWS * D),
    )(lengths, x, q, k, v, full, vec, *before)


def attend_back_body(
    dres_ref, dh_ref, wi_ref, hat_ref, inv_ref, wo_ref, q_ref, k_ref, v_ref, p_ref, vec_ref, *refs
):
    dr_ref, dq_ref, dk_ref, dv_ref, sums_ref, dc_ref = refs[-6:]
    hat = hat_ref[...]
    dn = dres_ref[...] + nt(dh_ref[...], wi_ref[...])
    dres = layer_norm_back(dn, vec_ref[G_ATTN : G_ATTN + 1].astype(f32), hat, inv_ref[...])
    dr_ref[...] = dres
    dao = dres.astype(low)
    dc_ref[...] = nt(dao, wo_ref[0]).astype(low)

    @pl.when(pl.program_id(0) == 0)
    def _():
        sums_ref[...] = jnp.zeros_like(sums_ref)

    sums_ref[B_OUTPUT : B_OUTPUT + 1] += jnp.sum(dao.astype(f32), axis=0, keepdims=True)
    sums_ref[G_ATTN : G_ATTN + 1] += jnp.sum(dn * hat, axis=0, keepdims=True)
    sums_ref[S_ATTN : S_ATTN + 1] += jnp.sum(dn, axis=0, keepdims=True)
    masks, masks32 = head_masks(low), head_masks(f32)

    def sentence(s):
        rows = pl.ds(pl.multiple_of(s * LEN, LEN), LEN)
        for g in range(GROUPS):
            cols = pl.ds(g * WIDE, WIDE)
            q, k, v, dc = q_ref[rows, cols], k_ref[rows, cols], v_ref[rows, cols], dc_ref[rows, cols]
            p = p_ref[table_rows(s, g), :]
            dcs = stacked(dc, masks)
            dp = nt(v, dcs)
            dv_ref[rows, cols] = nn(p.astype(low), dcs).astype(low)
            ds = (p * (dp - jnp.sum(p * dp, axis=0, keepdims=True))).astype(low)
            dk_ref[rows, cols] = (nn(ds, stacked(q, masks)) * HEAD_DIM ** (-0.5)).astype(low)
            dq_ref[rows, cols] = (unstacked(tn(ds, k), masks32) * HEAD_DIM ** (-0.5)).astype(low)

    pl.loop(0, ROWS // LEN, unroll=UNROLL)(sentence)
    sums_ref[B_QUERY : B_QUERY + 1] += jnp.sum(dq_ref[...].astype(f32), axis=0, keepdims=True)
    sums_ref[B_VALUE : B_VALUE + 1] += jnp.sum(dv_ref[...].astype(f32), axis=0, keepdims=True)


def attend_back(dres, dh, wi, hat, inv, full, q, k, v, p, vec, start, count, before=()):
    t = dres.shape[0]
    rows = some_rows(start)
    return pl.pallas_call(
        attend_back_body,
        grid=(count,),
        in_specs=[rows(D), rows(FF), whole((D, FF)), rows(D), rows(1), mat_of(3), rows(D), rows(D), rows(D),
                  rows(WIDE, GROUPS * ROWS), whole(vec.shape)] + [ANY] * len(before),
        out_specs=[rows(D)] * 4 + [whole((8, D))],
        out_shape=[S((t, D), f32)] + [S((t, D), low)] * 3 + [S((8, D), f32)],
        input_output_aliases={11 + i: i for i in range(len(before))},
        scratch_shapes=[pltpu.VMEM((ROWS, D), low)],
        name="attend_back",
        **params(24 * count * ROWS * D * D, 40 * count * ROWS * D),
    )(dres, dh, wi, hat, inv, full, q, k, v, p, vec, *before)


def gelu_parts(h):
    d = 1.0 + (0.3275911 * 0.7071067811865476) * jnp.abs(h)
    t = pl.reciprocal(d, approx=True)
    t = t * (2.0 - d * t)
    poly = t * (0.127414796 + t * (-0.142248368 + t * (0.7107068705 + t * (-0.7265760135 + t * 0.5307027145))))
    bell = jnp.exp(-0.5 * (h * h))
    tail = poly * bell
    cdf = jnp.where(h >= 0, 1.0 - tail, tail)
    return h * cdf, cdf + h * (bell * 0.3989422804014327)


def assemble(cube, parts, w_ref, full_ref, sems, out_sem):
    onward = pltpu.make_async_copy(w_ref, full_ref, out_sem)

    @pl.when(pl.program_id(0) == 0)
    def _():
        if cube:
            part_copies(parts, w_ref, sems, everything)
            part_waits(parts, w_ref, sems, everything)
        else:
            copy = pltpu.make_async_copy(parts[0], w_ref, sems.at[0])
            copy.start()
            copy.wait()
        onward.start()

    return onward


def inner_body(cube, n_ref, vec_ref, *refs):
    parts, (a_ref, gp_ref, full_ref, w_ref, sems, out_sem) = refs[:-6], refs[-6:]
    onward = assemble(cube, parts, w_ref, full_ref, sems, out_sem)
    n = n_ref[...]
    w = w_ref.reshape(D, FF) if cube else w_ref
    for j in range(FF // BLOCK):
        cols = pl.ds(j * BLOCK, BLOCK)
        h = nn(n, w[:, cols]) + vec_ref[B_INNER + j : B_INNER + j + 1].astype(f32)
        act, slope = gelu_parts(h)
        a_ref[:, cols] = act.astype(low)
        gp_ref[:, cols] = slope.astype(low)

    @pl.when(pl.program_id(0) == pl.num_programs(0) - 1)
    def _():
        onward.wait()


def inner(n, vec, parts, cube):
    t = n.shape[0]
    shape = (4, 2, 2, 2, 24, FF) if cube else (D, FF)
    act, slope, full = pl.pallas_call(
        lambda *refs: inner_body(cube, *refs),
        grid=(t // ROWS,),
        in_specs=[row_block(D), whole(vec.shape)] + [ANY] * len(parts),
        out_specs=[row_block(FF), row_block(FF), ANY],
        out_shape=[S((t, FF), low), S((t, FF), low), S(shape, low)],
        scratch_shapes=[pltpu.VMEM(shape, low), pltpu.SemaphoreType.DMA((4,)), pltpu.SemaphoreType.DMA],
        name="inner",
        **params(6 * t * D * FF, 2 * t * D + 4 * t * FF + 4 * D * FF, 2 * t * FF),
    )(n, vec, *parts)
    return act, slope, full.reshape(D, FF)


def outer_body(cube, a_ref, hat_ref, vec_ref, *refs):
    parts = refs[:-9]
    out_ref, hat2_ref, inv_ref, cls_ref, unit_ref, full_ref, w_ref, sems, out_sem = refs[-9:]
    onward = assemble(cube, parts, w_ref, full_ref, sems, out_sem)
    step = pl.program_id(0)
    w = w_ref.reshape(FF, D) if cube else w_ref
    branch = nn(a_ref[...], w[...]) + vec_ref[B_OUTER : B_OUTER + 1].astype(f32)
    normed = hat_ref[...] * vec_ref[G_ATTN : G_ATTN + 1].astype(f32) + vec_ref[S_ATTN : S_ATTN + 1].astype(f32)
    hat, inv = layer_norm(normed + branch)
    hat2_ref[...] = hat
    inv_ref[...] = inv
    rows = hat * vec_ref[G_FFN : G_FFN + 1].astype(f32) + vec_ref[S_FFN : S_FFN + 1].astype(f32)
    out_ref[...] = rows.astype(low)
    pairs = rows.shape[0] // LEN // 2
    for s in range(pairs):
        at = pl.ds(step * pairs + s, 1)
        for side in range(2):
            cols = pl.ds(side * D, D)
            cls = rows[LEN * (2 * s + side) : LEN * (2 * s + side) + 1]
            cls_ref[at, cols] = cls
            unit_ref[at, cols] = cls * lax.rsqrt(jnp.sum(cls * cls, axis=-1, keepdims=True) + pool_eps)

    @pl.when(step == pl.num_programs(0) - 1)
    def _():
        onward.wait()


def outer(act, hat, vec, parts, cube):
    t = hat.shape[0]
    shape = (4, 2, 2, 2, 96, D) if cube else (FF, D)
    pairs = t // LEN // 2
    once = pl.BlockSpec((pairs, 2 * D), lambda i: (0, 0))
    *outs, full = pl.pallas_call(
        lambda *refs: outer_body(cube, *refs),
        grid=(t // ROWS,),
        in_specs=[row_block(FF), row_block(D), whole(vec.shape)] + [ANY] * len(parts),
        out_specs=[row_block(D), row_block(D), row_block(1), once, once, ANY],
        out_shape=[S((t, D), low), S((t, D), f32), S((t, 1), f32), S((pairs, 2 * D), f32), S((pairs, 2 * D), f32), S(shape, low)],
        scratch_shapes=[pltpu.VMEM(shape, low), pltpu.SemaphoreType.DMA((4,)), pltpu.SemaphoreType.DMA],
        name="outer",
        **params(2 * t * D * FF, 10 * t * D + 2 * t * FF + 4 * D * FF),
    )(act, hat, vec, *parts)
    return *outs, full.reshape(FF, D)


def write_shares(full, keep_ref, away_ref, put):
    core = lax.axis_index(AXIS) & 1

    def write(zero, one):
        for y in range(2):
            for x in range(2):
                put(zero, x, y, full(y, x, 0))
                put(one, y, x, full(y, x, 1))

    @pl.when(core == 0)
    def _():
        write(keep_ref, away_ref)

    @pl.when(core == 1)
    def _():
        write(away_ref, keep_ref)


def outer_back_body(cube, cot_ref, dc_ref, hat2_ref, inv2_ref, a_ref, vec_ref, dres_ref, dbr_ref, sums_ref, *refs):
    j = pl.program_id(0)

    @pl.when(j == 0)
    def _():
        dgain = jnp.zeros((1, D), f32)
        dshift = jnp.zeros((1, D), f32)
        dbias = jnp.zeros((1, D), f32)
        at = lax.broadcasted_iota(jnp.int32, (ROWS, D), 0)
        for b in range(cot_ref.shape[0] // ROWS):
            rows = pl.ds(b * ROWS, ROWS)
            d = cot_ref[rows, :].astype(f32)
            hat = hat2_ref[rows, :]
            for s in range(ROWS // LEN):
                whose = b * (ROWS // LEN) + s
                extra = dc_ref[whose // 2 : whose // 2 + 1, (whose % 2) * D : (whose % 2 + 1) * D]
                d += jnp.where(at == LEN * s, extra, 0.0)
            dgain += jnp.sum(d * hat, axis=0, keepdims=True)
            dshift += jnp.sum(d, axis=0, keepdims=True)
            dres = layer_norm_back(d, vec_ref[G_FFN : G_FFN + 1].astype(f32), hat, inv2_ref[rows, :])
            dres_ref[rows, :] = dres
            dbr = dres.astype(low)
            dbr_ref[rows, :] = dbr
            dbias += jnp.sum(dbr.astype(f32), axis=0, keepdims=True)
        sums_ref[...] = jnp.zeros_like(sums_ref)
        sums_ref[0:1] = dbias
        sums_ref[1:2] = dgain
        sums_ref[2:3] = dshift

    dw = tn(a_ref[...], dbr_ref[...])
    if cube:
        dw = dw.reshape(2, 2, 2, 96, D)

        def put(ref, p, q, value):
            ref[0, p, q] = value.astype(ref.dtype)

        write_shares(lambda y, x, c: dw[y, x, c], *refs, put)
    else:
        refs[0][...] = dw


def outer_back(cot, dc, hat2, inv2, a, vec, cube):
    t = cot.shape[0]
    if cube:
        spec = pl.BlockSpec((1, 2, 2, 96, D), lambda j: (j, 0, 0, 0, 0))
        specs, shapes = [spec] * 2, [S((4, 2, 2, 96, D), KEEP), S((4, 2, 2, 96, D), low)]
    else:
        specs, shapes = [pl.BlockSpec((BLOCK, D), lambda j: (j, 0))], [S((FF, D), f32)]
    return pl.pallas_call(
        lambda *refs: outer_back_body(cube, *refs),
        grid=(FF // BLOCK,),
        in_specs=[whole((t, D)), whole(dc.shape), whole((t, D)), whole((t, 1)), pl.BlockSpec((t, BLOCK), lambda j: (0, j)),
                  whole(vec.shape)],
        out_specs=[whole((t, D)), whole((t, D)), whole((8, D))] + specs,
        out_shape=[S((t, D), f32), S((t, D), low), S((8, D), f32)] + shapes,
        name="outer_back",
        **params(4 * t * D * FF, 14 * t * D + 2 * t * FF + 8 * D * FF),
    )(cot, dc, hat2, inv2, a, vec)


def inner_back_body(cube, dbr_ref, n_ref, gp_ref, wo_ref, dh_ref, sums_ref, *refs):
    dh = (gp_ref[...].astype(f32) * nt(dbr_ref[...], wo_ref[...])).astype(low)
    dh_ref[...] = dh
    sums_ref[pl.ds(pl.program_id(0), 1), :] = jnp.sum(dh.astype(f32), axis=0, keepdims=True)
    dw = tn(n_ref[...], dh)
    if cube:
        dw = dw.reshape(4, 2, 2, 2, 24, BLOCK)

        def put(ref, p, q, value):
            ref[:, p, q] = value.astype(ref.dtype)

        write_shares(lambda y, x, c: dw[:, y, x, c], *refs, put)
    else:
        refs[0][...] = dw


def inner_back(dbr, n, gp, wo, cube):
    t = n.shape[0]
    fblk = pl.BlockSpec((t, BLOCK), lambda j: (0, j))
    if cube:
        spec = pl.BlockSpec((4, 2, 2, 24, BLOCK), lambda j: (0, 0, 0, 0, j))
        specs, shapes = [spec] * 2, [S((4, 2, 2, 24, FF), KEEP), S((4, 2, 2, 24, FF), low)]
    else:
        specs, shapes = [pl.BlockSpec((D, BLOCK), lambda j: (0, j))], [S((D, FF), f32)]
    return pl.pallas_call(
        lambda *refs: inner_back_body(cube, *refs),
        grid=(FF // BLOCK,),
        in_specs=[whole((t, D)), whole((t, D)), fblk, pl.BlockSpec((BLOCK, D), lambda j: (j, 0))],
        out_specs=[fblk, whole((4, D))] + specs,
        out_shape=[S((t, FF), low), S((4, D), f32)] + shapes,
        name="inner_back",
        **params(4 * t * D * FF, 4 * t * D + 4 * t * FF + 8 * D * FF),
    )(dbr, n, gp, wo)


KEEP = f32


def mats_body(cube, x_ref, c_ref, dq_ref, dk_ref, dv_ref, dr_ref, *refs):
    x = x_ref[...]
    for m, (rows, grad) in enumerate(((x_ref, dq_ref), (x_ref, dk_ref), (x_ref, dv_ref), (c_ref, dr_ref))):
        full = tn(rows[...], grad[...].astype(low))
        if cube:
            full = full.reshape(4, 2, 2, 2, 24, full.shape[-1])

            def put(ref, p, q, value, m=m):
                ref[:, p, q, m] = value.astype(ref.dtype)

            write_shares(lambda y, x, c: full[:, y, x, c], *refs, put)
        else:
            refs[0][m] = full


def mats(x, c, dq, dk, dv, dr, cube):
    t = x.shape[0]
    wide = 256
    col = pl.BlockSpec((t, wide), lambda j: (0, j))
    if cube:
        spec = pl.BlockSpec((4, 2, 2, 4, 24, wide), lambda j: (0, 0, 0, 0, 0, j))
        specs, shapes = [spec] * 2, [S((4, 2, 2, 4, 24, D), KEEP), S((4, 2, 2, 4, 24, D), low)]
    else:
        specs, shapes = [pl.BlockSpec((4, D, wide), lambda j: (0, 0, j))], [S((4, D, D), f32)]
    return pl.pallas_call(
        lambda *refs: mats_body(cube, *refs),
        grid=(D // wide,),
        in_specs=[whole((t, D)), whole((t, D)), col, col, col, col],
        out_specs=specs,
        out_shape=shapes,
        name="mats",
        **params(8 * t * D * D, 14 * t * D + 16 * D * D),
    )(x, c, dq, dk, dv, dr)


def token_grad_body(dr_ref, dq_ref, dk_ref, dv_ref, wq_ref, wk_ref, wv_ref, o_ref):
    o_ref[...] = (
        dr_ref[...] + nt(dq_ref[...], wq_ref[0]) + nt(dk_ref[...], wk_ref[0]) + nt(dv_ref[...], wv_ref[0])
    )


def token_grad(dr, dq, dk, dv, full):
    t = dr.shape[0]

    return pl.pallas_call(
        token_grad_body,
        grid=(t // ROWS,),
        in_specs=[row_block(D)] * 4 + [mat_of(0), mat_of(1), mat_of(2)],
        out_specs=row_block(D),
        out_shape=S((t, D), f32),
        name="token_grad",
        **params(6 * t * D * D, 14 * t * D + 6 * D * D),
    )(dr, dq, dk, dv, full, full, full)


def loss_body(units_ref, codes_ref, cls_ref, loss_ref, dc_ref, table_ref, ds_ref):
    sources, targets = units_ref[:, :D], units_ref[:, D:]
    pairs, own = units_ref.shape[0], cls_ref.shape[0]
    codes = codes_ref[CODES : CODES + 2, :pairs].astype(f32)
    partner = (codes[0:1] + 64.0 * codes[1:2]).astype(jnp.int32)
    matched = lax.broadcasted_iota(jnp.int32, (pairs, pairs), 0) == partner
    sims = nt(targets, sources) * sim_scale - jnp.where(matched, sim_scale * sim_margin, 0.0)
    row_top = jnp.max(sims, axis=0, keepdims=True)
    row_lse = row_top + jnp.log(jnp.sum(jnp.exp(sims - row_top), axis=0, keepdims=True))
    col_top = jnp.max(sims, axis=1, keepdims=True)
    col_lse = col_top + jnp.log(jnp.sum(jnp.exp(sims - col_top), axis=1, keepdims=True))
    total = (
        jnp.sum(row_lse, axis=1, keepdims=True)
        + jnp.sum(col_lse, axis=0, keepdims=True)
        - 2.0 * jnp.sum(jnp.sum(jnp.where(matched, sims, 0.0), axis=1, keepdims=True), axis=0, keepdims=True)
    )
    loss_ref[...] = jnp.broadcast_to(total * (0.5 / pairs), loss_ref.shape)
    d_sims = 0.5 * (jnp.exp(sims - row_lse) + jnp.exp(sims - col_lse)) - jnp.where(matched, 1.0, 0.0)
    d_low = (d_sims * sim_scale).astype(low)
    table_ref[...] = nn(d_low, sources)
    ds_ref[...] = tn(d_low, targets)
    mine = pl.ds(pl.multiple_of(lax.axis_index(AXIS) * own, own), own)
    for side, ref in enumerate((ds_ref, table_ref)):
        cols = pl.ds(side * D, D)
        cls, du = cls_ref[:, cols], ref[mine, :]
        inv = lax.rsqrt(jnp.sum(cls * cls, axis=-1, keepdims=True) + pool_eps)
        dc_ref[:, cols] = inv * du - cls * (inv * inv * inv * jnp.sum(du * cls, axis=-1, keepdims=True))


def pair_loss(units, vec, cls):
    pairs, own = units.shape[0], cls.shape[0]
    loss, dc = pl.pallas_call(
        loss_body,
        in_specs=[whole(units.shape), whole(vec.shape), whole(cls.shape)],
        out_specs=[whole((8, 128)), whole(cls.shape)],
        out_shape=[S((8, 128), f32), S(cls.shape, f32)],
        scratch_shapes=[pltpu.VMEM((pairs, D), f32), pltpu.VMEM((pairs, D), f32)],
        grid=(1,),
        name="pair_loss",
        **params(6 * pairs * pairs * D, 4 * pairs * D, 4 * pairs * pairs),
    )(units, vec, cls)
    return loss[0, 0], dc


CUBE = 32
CORE = [(i, i ^ 1) for i in range(CUBE)]
FAR_Z = [(i, i ^ 16) for i in range(CUBE)]
NEAR_Z = [(i, i ^ 8) for i in range(CUBE)]
FIRST = [(i, i ^ (4 if i & 1 else 2)) for i in range(CUBE)]
SECOND = [(i, i ^ (2 if i & 1 else 4)) for i in range(CUBE)]
ROUTES = (CORE, FIRST, SECOND, NEAR_Z, FAR_Z)


class Place:
    def __init__(self):
        self.me = lax.axis_index(AXIS)
        self.core = self.me & 1
        x, y = (self.me >> 1) & 1, (self.me >> 2) & 1
        self.near_z, self.far_z = (self.me >> 3) & 1, (self.me >> 4) & 1
        self.first = jnp.where(self.core == 0, x, y)
        self.second = jnp.where(self.core == 0, y, x)


def join(own, other, axis, bit):
    shape = own.shape[:axis] + (2,) + own.shape[axis:]
    where = lax.broadcasted_iota(jnp.int32, shape, axis)
    return jnp.where(where == bit, jnp.expand_dims(own, axis), jnp.expand_dims(other, axis))


def pick(field, axis, bit):
    return lax.dynamic_index_in_dim(field, bit, axis, keepdims=False)


def send(field, route):
    return lax.ppermute(field, AXIS, route)


def spread(block, place):
    block = join(block, send(block, FAR_Z), 0, place.far_z)
    block = join(block, send(block, NEAR_Z), 1, place.near_z)
    return join(block, send(block, FIRST), 2, place.first)


def gather_blocks(block, place):
    near = spread(block, place)
    block = join(near, send(near, SECOND), 3, place.second)
    other = send(block, CORE)
    zero = jnp.where(place.core == 0, block, other)
    one = jnp.where(place.core == 0, other, block)
    return jnp.stack([jnp.swapaxes(zero, 2, 3), one], axis=4).reshape(-1, block.shape[-1])


def together(*values):
    return lax.optimization_barrier(values)


class Reduction:
    def __init__(self, keep, came, place):
        self.stages = ((2, place.first), (2, place.second), (1, place.near_z), (0, place.far_z))
        shape = (2, 2, *keep.shape[1:])
        self.total = keep.reshape(shape).astype(f32) + came.reshape(shape).astype(f32)

    def split(self, stage):
        axis, bit = self.stages[stage]
        return pick(self.total, axis, bit), pick(self.total, axis, 1 - bit).astype(low)

    def meet(self, kept, came):
        self.total = kept + came.astype(f32)
        return self


def spread_rows(rows, at, count):
    r = rows.shape[1]
    lane = lax.broadcasted_iota(jnp.int32, (r, D), 1)
    copies = nn(rows, jnp.where(lane % r == lax.broadcasted_iota(jnp.int32, (r, D), 0), 1.0, 0.0).astype(low))
    lane = lax.broadcasted_iota(jnp.int32, (count, D), 1)
    row = lax.broadcasted_iota(jnp.int32, (count, D), 0)
    return copies, lane // r, row


def vector_table(vectors, partners, place):
    *small, inner = vectors
    copies, lane, _ = spread_rows(jnp.stack(small), place.me, len(small))
    table = [jnp.where(lane == place.me, copies, 0.0)]
    fold = D // inner.shape[0]
    copies, lane, row = spread_rows(inner[None], place.me, FF // D)
    table.append(jnp.where((row == place.me // fold) & (lane == place.me % fold), copies, 0.0))
    codes = jnp.stack([partners % 64, partners // 64]).astype(low)
    copies, lane, _ = spread_rows(codes, place.me, 2)
    table.append(jnp.where(lane == place.me, copies, 0.0))
    table.append(jnp.zeros((2, D), f32))
    table = jnp.concatenate(table, axis=0).astype(low)
    for route in (FAR_Z, NEAR_Z, FIRST, SECOND, CORE):
        table = table + send(table, route)
    return table


def own_vectors(sums_attn, sums_ffn, place):
    total = jnp.concatenate([sums_attn, sums_ffn], axis=0)
    for route in ROUTES:
        total = total + send(total.astype(low), route).astype(f32)
    r, fold = D // CUBE, FF // CUBE
    mine = lax.dynamic_slice(total, (0, place.me * r), (16, r))
    inner = lax.dynamic_slice(total, (11 + place.me // (D // fold), (place.me % (D // fold)) * fold), (1, fold))
    return [mine[i] for i in (0, 1, 2, 3, 4, 8, 9, 10)] + [inner[0]]


def pack_body(*refs):
    *mats, out, sems = refs
    r = mats[0].shape[0]
    copies = [pltpu.make_async_copy(m, out.at[pl.ds(i * r, r), :], sems.at[i]) for i, m in enumerate(mats)]
    for copy in copies:
        copy.start()
    for copy in copies:
        copy.wait()


def pack(*mats):
    r, n = mats[0].shape
    return pl.pallas_call(
        pack_body,
        in_specs=[ANY] * len(mats),
        out_specs=ANY,
        out_shape=S((len(mats) * r, n), low),
        scratch_shapes=[pltpu.SemaphoreType.DMA((len(mats),))],
        name="pack",
    )(*mats)


def plain_loss(units, partners, cls):
    sources, targets = units[:, :D], units[:, D:]
    npairs, own = units.shape[0], cls.shape[0]
    sims = nt(sources, targets) * sim_scale
    matched = partners[:, None] == jnp.arange(npairs, dtype=jnp.int32)[None, :]
    sims = sims - jnp.where(matched, sim_scale * sim_margin, 0.0)
    row_top = jnp.max(sims, axis=1, keepdims=True)
    row_lse = row_top + jnp.log(jnp.sum(jnp.exp(sims - row_top), axis=1, keepdims=True))
    col_top = jnp.max(sims, axis=0, keepdims=True)
    col_lse = col_top + jnp.log(jnp.sum(jnp.exp(sims - col_top), axis=0, keepdims=True))
    positive = jnp.sum(jnp.where(matched, sims, 0.0))
    loss = (jnp.sum(row_lse) + jnp.sum(col_lse) - 2.0 * positive) / (2.0 * npairs)
    d_sims = 0.5 * (jnp.exp(sims - row_lse) + jnp.exp(sims - col_lse)) - jnp.where(matched, 1.0, 0.0)
    d_low = (d_sims * sim_scale).astype(low)
    first = lax.axis_index(AXIS) * own
    du = [
        nn(lax.dynamic_slice_in_dim(d_low, first, own, 0), targets),
        tn(lax.dynamic_slice_in_dim(d_low, first, own, 1), sources),
    ]
    dc = []
    for side in range(2):
        c = cls[:, side * D : (side + 1) * D]
        inv = lax.rsqrt(jnp.sum(c * c, axis=-1, keepdims=True) + pool_eps)
        dc.append(inv * du[side] - c * (inv * inv * inv * jnp.sum(du[side] * c, axis=-1, keepdims=True)))
    return loss, jnp.concatenate(dc, axis=1)


def every(v):
    return lax.all_gather(v, AXIS, axis=0, tiled=True)


def scatter(v):
    return lax.psum_scatter(v, AXIS, scatter_dimension=0, tiled=True)


def local(
    tokens,
    lengths,
    partners,
    out_cotangent,
    w_query,
    w_key,
    w_value,
    w_output,
    b_query,
    b_value,
    b_output,
    gain_attn,
    shift_attn,
    w_inner,
    b_inner,
    w_outer,
    b_outer,
    gain_ffn,
    shift_ffn,
):
    cube = lax.axis_size(AXIS) == CUBE
    count = tokens.shape[0]
    x = tokens.reshape(count * LEN, D)
    vectors = (b_query, b_value, b_output, gain_attn, shift_attn, b_outer, gain_ffn, shift_ffn, b_inner)
    if cube:
        place = Place()
        attn = pack(w_query, w_key, w_value, w_output)
        attn = join(attn, send(attn, FAR_Z), 0, place.far_z)
        attn = join(attn, send(attn, NEAR_Z), 1, place.near_z)
        w_inner, attn = together(w_inner, attn)
        inn = join(w_inner, send(w_inner, FAR_Z), 0, place.far_z)
        attn = join(attn, send(attn, FIRST), 2, place.first)
        w_outer, inn, attn = together(w_outer, inn, attn)
        out = join(w_outer, send(w_outer, FAR_Z), 0, place.far_z)
        inn = join(inn, send(inn, NEAR_Z), 1, place.near_z)
        vec = vector_table(vectors, partners, place)
        attn_near = attn.reshape(4, 2, 96, D)
        attn_far = send(attn_near, SECOND)
        inn, attn_far = together(inn, attn_far)
        out = join(out, send(out, NEAR_Z), 1, place.near_z)
        attn_parts = (attn_near, attn_far, send(attn_near, CORE), send(attn_far, CORE))
        attn_parts, inn = together(attn_parts, inn)
        inn = join(inn, send(inn, FIRST), 2, place.first).reshape(4, 2, 24, FF)
        queries, keys, values, full = project(x, vec, attn_parts, cube)
        queries, inn, out = together(queries, inn, out)
        blocks = count * LEN // ROWS
        inn_far = send(inn, SECOND)
        out = join(out, send(out, FIRST), 2, place.first).reshape(4, 2, 96, D)
        upper = attend(lengths, x, queries, keys, values, full, vec, 0, blocks // 2)
        upper, inn, inn_far, out = together(upper, inn, inn_far, out)
        inn_parts = (inn, inn_far, send(inn, CORE), send(inn_far, CORE))
        out_far = send(out, SECOND)
        probs, context, hat1, inv1, normed = attend(
            lengths, x, queries, keys, values, full, vec, blocks // 2, blocks - blocks // 2, upper
        )
        normed, inn_parts = together(normed, inn_parts)
        act, slope, inner_mat = inner(normed, vec, inn_parts, cube)
        out_parts = (out, out_far, send(out, CORE), send(out_far, CORE))
        block_out, hat2, inv2, cls, unit, outer_mat = outer(act, hat1, vec, out_parts, cube)
        loss, d_cls = pair_loss(gather_blocks(unit.astype(low), place), vec, cls)
        dres, dbr, sums_outer, keep_o, away_o = outer_back(
            out_cotangent.reshape(count * LEN, D), d_cls, hat2, inv2, act, vec, cube
        )
        dbr, away_o = together(dbr, away_o)
        came_o = send(away_o, CORE)
        dh, sums_inner, keep_i, away_i = inner_back(dbr, normed, slope, outer_mat, cube)
        out, inn = Reduction(keep_o, came_o, place), None
        kept_o, away_o = out.split(0)
        dh, kept_o, away_o, away_i = together(dh, kept_o, away_o, away_i)
        came_i, came_o = send(away_i, CORE), send(away_o, FIRST)
        upper = attend_back(dres, dh, inner_mat, hat1, inv1, full, queries, keys, values, probs, vec, 0, blocks // 2)
        inn = Reduction(keep_i, came_i, place)
        kept_i, away_i = inn.split(0)
        kept_o, away_o = out.meet(kept_o, came_o).split(1)
        upper, kept_i, away_i, kept_o, away_o = together(upper, kept_i, away_i, kept_o, away_o)
        came_i, came_o = send(away_i, FIRST), send(away_o, SECOND)
        d_resid, d_queries, d_keys, d_values, sums_lower = attend_back(
            dres, dh, inner_mat, hat1, inv1, full, queries, keys, values, probs, vec,
            blocks // 2, blocks - blocks // 2, upper[:4],
        )
        kept_i, away_i = inn.meet(kept_i, came_i).split(1)
        kept_o, away_o = out.meet(kept_o, came_o).split(2)
        d_resid, kept_i, away_i, kept_o, away_o = together(d_resid, kept_i, away_i, kept_o, away_o)
        came_i, came_o = send(away_i, SECOND), send(away_o, NEAR_Z)
        keep_a, away_a = mats(x, context, d_queries, d_keys, d_values, d_resid, cube)
        kept_i, away_i = inn.meet(kept_i, came_i).split(2)
        kept_o, away_o = out.meet(kept_o, came_o).split(3)
        keep_a, away_a, kept_i, away_i, kept_o, away_o, d_resid = together(
            keep_a, away_a, kept_i, away_i, kept_o, away_o, d_resid
        )
        came_a, came_i, came_o = send(away_a, CORE), send(away_i, NEAR_Z), send(away_o, FAR_Z)
        grad_rows = token_grad(d_resid, d_queries, d_keys, d_values, full)
        grad_w_outer = out.meet(kept_o, came_o).total
        kept_i, away_i = inn.meet(kept_i, came_i).split(3)
        att = Reduction(keep_a, came_a, place)
        kept_a, away_a = att.split(0)
        kept_i, away_i, kept_a, away_a, grad_rows = together(kept_i, away_i, kept_a, away_a, grad_rows)
        grad_w_inner = inn.meet(kept_i, send(away_i, FAR_Z)).total
        for stage in range(3):
            kept_a, away_a = att.meet(kept_a, send(away_a, ROUTES[1 + stage])).split(stage + 1)
        g_mats = att.meet(kept_a, send(away_a, FAR_Z)).total
        sums_ffn = jnp.concatenate([sums_outer[:3], sums_inner, sums_outer[3:4]], axis=0)
        grads = own_vectors(upper[4] + sums_lower, sums_ffn, place)
    else:
        rows = [every(v).reshape(-1, D) for v in vectors]
        vec = jnp.concatenate(rows + [jnp.zeros((4, D), low)], axis=0)
        mats_in = (jnp.stack([every(w) for w in (w_query, w_key, w_value, w_output)]),)
        blocks = count * LEN // ROWS
        queries, keys, values, full = project(x, vec, mats_in, cube)
        probs, context, hat1, inv1, normed = attend(lengths, x, queries, keys, values, full, vec, 0, blocks)
        act, slope, inner_mat = inner(normed, vec, (every(w_inner),), cube)
        block_out, hat2, inv2, cls, unit, outer_mat = outer(act, hat1, vec, (every(w_outer),), cube)
        loss, d_cls = plain_loss(every(unit.astype(low)), every(partners), cls)
        dres, dbr, sums_outer, d_outer = outer_back(
            out_cotangent.reshape(count * LEN, D), d_cls, hat2, inv2, act, vec, cube
        )
        dh, sums_inner, d_inner = inner_back(dbr, normed, slope, outer_mat, cube)
        d_resid, d_queries, d_keys, d_values, sums_attn = attend_back(
            dres, dh, inner_mat, hat1, inv1, full, queries, keys, values, probs, vec, 0, blocks
        )
        (d_mats,) = mats(x, context, d_queries, d_keys, d_values, d_resid, cube)
        grad_rows = token_grad(d_resid, d_queries, d_keys, d_values, full)
        grad_w_outer, grad_w_inner = scatter(d_outer), scatter(d_inner)
        g_mats = [scatter(d_mats[m]) for m in range(4)]
        grads = [scatter(sums_attn[i]) for i in range(5)] + [scatter(sums_outer[i]) for i in range(3)]
        grads.append(scatter(sums_inner.reshape(-1)))
    (
        grad_b_query,
        grad_b_value,
        grad_b_output,
        grad_gain_attn,
        grad_shift_attn,
        grad_b_outer,
        grad_gain_ffn,
        grad_shift_ffn,
        grad_b_inner,
    ) = grads
    return (
        loss,
        block_out.reshape(count, LEN, D),
        grad_rows.reshape(count, LEN, D),
        g_mats[0],
        g_mats[1],
        g_mats[2],
        g_mats[3],
        grad_b_query,
        grad_b_value,
        grad_b_output,
        grad_gain_attn,
        grad_shift_attn,
        grad_w_inner,
        grad_b_inner,
        grad_w_outer,
        grad_b_outer,
        grad_gain_ffn,
        grad_shift_ffn,
    )


def solution(mesh):
    rows, cols = P(AXIS), P(AXIS, None)
    cube = P(AXIS, None, None)
    in_specs = (cube, rows, rows, cube) + (cols,) * 4 + (rows,) * 5 + (cols, rows, cols) + (rows,) * 3
    out_specs = (P(), cube, cube) + (cols,) * 4 + (rows,) * 5 + (cols, rows, cols) + (rows,) * 3
    return jax.shard_map(local, mesh=mesh, in_specs=in_specs, out_specs=out_specs, check_vma=False)
```

```python
import jax
import jax.numpy as jnp
from jax import lax
from jax.experimental import pallas as pl
from jax.experimental.pallas import tpu as pltpu
from jax.sharding import PartitionSpec as P

D = 768
HEADS = 12
HEAD_DIM = 64
LEN = 64
FF = 3072
QUAD = 4
WIDE = QUAD * HEAD_DIM
GROUPS = HEADS // QUAD
ROWS = 256
BLOCK = 768
AXIS = "fsdp"
norm_eps = 1e-12
pool_eps = 1e-06
sim_scale = 50.0
sim_margin = 0.3
f32, low = jnp.float32, jnp.bfloat16
S = jax.ShapeDtypeStruct

B_QUERY, B_VALUE, B_OUTPUT, G_ATTN, S_ATTN, B_OUTER, G_FFN, S_FFN, B_INNER = range(9)
CODES = B_INNER + FF // D


def nn(a, b):
    return lax.dot_general(a, b, (((1,), (0,)), ((), ())), preferred_element_type=f32)


def nt(a, b):
    return lax.dot_general(a, b, (((1,), (1,)), ((), ())), preferred_element_type=f32)


def tn(a, b):
    return lax.dot_general(a, b, (((0,), (0,)), ((), ())), preferred_element_type=f32)


def whole(shape):
    return pl.BlockSpec(shape, lambda *_: (0,) * len(shape), pipeline_mode=pl.Buffered(1))


def row_block(width, rows=ROWS):
    return pl.BlockSpec((rows, width), lambda i, *_: (i, 0))


def params(flops, nbytes, exps=0, room=60):
    return dict(
        compiler_params=pltpu.CompilerParams(vmem_limit_bytes=room << 20),
        cost_estimate=pl.CostEstimate(flops=int(flops), bytes_accessed=int(nbytes), transcendentals=int(exps)),
    )


ANY = pl.BlockSpec(memory_space=pl.ANY)


def part_copies(parts, target, sems, cut):
    me = lax.axis_index(AXIS)
    core, x, y = me & 1, (me >> 1) & 1, (me >> 2) & 1

    def start(zero, one):
        for i in range(2):
            pltpu.make_async_copy(cut(zero[i]), target.at[:, (y + i) & 1, :, 0], sems.at[2 * i]).start()
            pltpu.make_async_copy(cut(one[i]), target.at[:, :, (x + i) & 1, 1], sems.at[2 * i + 1]).start()

    @pl.when(core == 0)
    def _():
        start(parts[:2], parts[2:])

    @pl.when(core == 1)
    def _():
        start(parts[2:], parts[:2])


def part_waits(parts, target, sems, cut):
    for i in range(2):
        pltpu.make_async_copy(cut(parts[i]), target.at[:, i, :, 0], sems.at[2 * i]).wait()
        pltpu.make_async_copy(cut(parts[i]), target.at[:, :, i, 1], sems.at[2 * i + 1]).wait()


def everything(ref):
    return ref


def project_body(cube, x_ref, vec_ref, *refs):
    parts, (q_ref, k_ref, v_ref, full_ref, w_ref, sems, out_sem) = refs[:-7], refs[-7:]
    step = pl.program_id(0)
    onward = pltpu.make_async_copy(w_ref, full_ref, out_sem)

    @pl.when(step == 0)
    def _():
        if cube:

            def cut(m):
                return lambda ref: ref.at[:, :, pl.ds(m * 24, 24), :]

            for m in range(3):
                part_copies(parts, w_ref.at[m], sems.at[m], cut(m))
            for m in range(3):
                part_waits(parts, w_ref.at[m], sems.at[m], cut(m))
        else:
            copy = pltpu.make_async_copy(parts[0], w_ref, sems.at[0, 0])
            copy.start()
            copy.wait()
        onward.start()

    x = x_ref[...]

    def mat(m):
        return w_ref.at[m].reshape(D, D)[...] if cube else w_ref[m]

    q_ref[...] = (nn(x, mat(0)) + vec_ref[B_QUERY : B_QUERY + 1].astype(f32)).astype(low)
    k_ref[...] = nn(x, mat(1)).astype(low)
    v_ref[...] = (nn(x, mat(2)) + vec_ref[B_VALUE : B_VALUE + 1].astype(f32)).astype(low)

    @pl.when(step == pl.num_programs(0) - 1)
    def _():
        onward.wait()


def project(x, vec, parts, cube):
    t = x.shape[0]
    shape = (3, 4, 2, 2, 2, 24, D) if cube else (3, D, D)
    q, k, v, full = pl.pallas_call(
        lambda *refs: project_body(cube, *refs),
        grid=(t // ROWS,),
        in_specs=[row_block(D), whole(vec.shape)] + [ANY] * len(parts),
        out_specs=[row_block(D)] * 3 + [ANY],
        out_shape=[S((t, D), low)] * 3 + [S(shape, low)],
        scratch_shapes=[pltpu.VMEM(shape, low), pltpu.SemaphoreType.DMA((3, 4)), pltpu.SemaphoreType.DMA],
        name="project",
        **params(6 * t * D * D, 8 * t * D + 12 * D * D, room=60),
    )(x, vec, *parts)
    return q, k, v, full.reshape(3, D, D)


def assemble(cube, parts, w_ref, full_ref, sems, out_sem):
    onward = pltpu.make_async_copy(w_ref, full_ref, out_sem)

    @pl.when(pl.program_id(0) == 0)
    def _():
        if cube:
            part_copies(parts, w_ref, sems, everything)
            part_waits(parts, w_ref, sems, everything)
        else:
            copy = pltpu.make_async_copy(parts[0], w_ref, sems.at[0])
            copy.start()
            copy.wait()
        onward.start()

    return onward


def scratch_for(shape):
    return [pltpu.VMEM(shape, low), pltpu.SemaphoreType.DMA((4,)), pltpu.SemaphoreType.DMA]


def head_masks(dtype):
    lane = lax.broadcasted_iota(jnp.int32, (1, WIDE), 1) // HEAD_DIM
    return [jnp.where(lane == h, 1.0, 0.0).astype(dtype) for h in range(QUAD)]


def stacked(rows, masks):
    return jnp.concatenate([rows * m for m in masks], axis=0)


def unstacked(full, masks):
    return sum(full[LEN * h : LEN * (h + 1)] * m for h, m in enumerate(masks))


def layer_norm(resid):
    centred = resid - jnp.mean(resid, axis=-1, keepdims=True)
    inv = lax.rsqrt(jnp.mean(centred * centred, axis=-1, keepdims=True) + norm_eps)
    return centred * inv, inv


def layer_norm_back(grad, gain, hat, inv):
    grad = grad * gain
    mean = jnp.mean(grad, axis=-1, keepdims=True)
    along = jnp.mean(grad * hat, axis=-1, keepdims=True)
    return (grad - mean - hat * along) * inv


def attend_body(start, len_ref, q_ref, k_ref, v_ref, *refs):
    p_ref, c_ref = refs[-2:]
    masks, masks32 = head_masks(low), head_masks(f32)
    per = ROWS // LEN
    first = (start + pl.program_id(0)) * per
    key_at = lax.broadcasted_iota(jnp.int32, (LEN, WIDE), 0)

    def sentence(s):
        rows = pl.ds(pl.multiple_of(s * LEN, LEN), LEN)
        seen = key_at < len_ref[first + s]
        for g in range(GROUPS):
            cols = pl.ds(g * WIDE, WIDE)
            q, k, v = q_ref[rows, cols], k_ref[rows, cols], v_ref[rows, cols]
            scores = nt(k, stacked(q, masks)) * HEAD_DIM ** (-0.5)
            scores = jnp.where(seen, scores, -1e30)
            expd = jnp.exp(scores - jnp.max(scores, axis=0, keepdims=True))
            probs = expd * (1.0 / jnp.sum(expd, axis=0, keepdims=True))
            p_ref[g, rows, :] = probs
            c_ref[rows, cols] = unstacked(tn(probs.astype(low), v), masks32).astype(low)

    pl.loop(0, per, unroll=UNROLL)(sentence)


UNROLL = 4


def some_rows(start):
    return lambda width, rows=ROWS: pl.BlockSpec((rows, width), lambda i, *_: (start + i, 0))


def mat_of(m):
    return pl.BlockSpec((1, D, D), lambda *_: (m, 0, 0), pipeline_mode=pl.Buffered(1))


def attend(lengths, q, k, v, start, count, before=()):
    t = q.shape[0]
    rows = some_rows(start)
    return pl.pallas_call(
        lambda *refs: attend_body(start, *refs),
        grid_spec=pltpu.PrefetchScalarGridSpec(
            num_scalar_prefetch=1,
            grid=(count,),
            in_specs=[rows(D)] * 3 + [ANY] * len(before),
            out_specs=[pl.BlockSpec((GROUPS, ROWS, WIDE), lambda i, *_: (0, start + i, 0)), rows(D)],
        ),
        out_shape=[S((GROUPS, t, WIDE), f32), S((t, D), low)],
        input_output_aliases={4 + i: i for i in range(len(before))},
        name="attend",
        **params(10 * count * ROWS * D * D, 20 * count * ROWS * D, count * ROWS * D, room=60),
    )(lengths, q, k, v, *before)


def close_body(cube, x_ref, c_ref, vec_ref, *refs):
    parts, (hat_ref, inv_ref, n_ref, full_ref, w_ref, sems, out_sem) = refs[:-7], refs[-7:]
    onward = assemble(cube, parts, w_ref, full_ref, sems, out_sem)
    w = w_ref.reshape(D, D) if cube else w_ref
    branch = nn(c_ref[...], w[...]) + vec_ref[B_OUTPUT : B_OUTPUT + 1].astype(f32)
    hat, inv = layer_norm(x_ref[...].astype(f32) + branch)
    hat_ref[...] = hat
    inv_ref[...] = inv
    n_ref[...] = (hat * vec_ref[G_ATTN : G_ATTN + 1].astype(f32) + vec_ref[S_ATTN : S_ATTN + 1].astype(f32)).astype(low)

    @pl.when(pl.program_id(0) == pl.num_programs(0) - 1)
    def _():
        onward.wait()


def close(x, c, vec, parts, cube):
    t = x.shape[0]
    shape = (4, 2, 2, 2, 24, D) if cube else (D, D)
    hat, inv, n, full = pl.pallas_call(
        lambda *refs: close_body(cube, *refs),
        grid=(t // ROWS,),
        in_specs=[row_block(D), row_block(D), whole(vec.shape)] + [ANY] * len(parts),
        out_specs=[row_block(D), row_block(1), row_block(D), ANY],
        out_shape=[S((t, D), f32), S((t, 1), f32), S((t, D), low), S(shape, low)],
        scratch_shapes=scratch_for(shape),
        name="close",
        **params(2 * t * D * D, 10 * t * D + 4 * D * D, room=60),
    )(x, c, vec, *parts)
    return hat, inv, n, full.reshape(1, D, D)


def open_back_body(dres_ref, dh_ref, wi_ref, hat_ref, inv_ref, wo_ref, vec_ref, before_ref, dr_ref, da_ref, dc_ref, sums_ref):
    hat = hat_ref[...]
    dn = dres_ref[...] + nt(dh_ref[...], wi_ref[...])
    dres = layer_norm_back(dn, vec_ref[G_ATTN : G_ATTN + 1].astype(f32), hat, inv_ref[...])
    dr_ref[...] = dres
    dao = dres.astype(low)
    da_ref[...] = dao
    dc_ref[...] = nt(dao, wo_ref[0]).astype(low)

    @pl.when(pl.program_id(0) == 0)
    def _():
        sums_ref[...] = before_ref[...]

    sums_ref[B_OUTPUT : B_OUTPUT + 1] += jnp.sum(dao.astype(f32), axis=0, keepdims=True)
    sums_ref[G_ATTN : G_ATTN + 1] += jnp.sum(dn * hat, axis=0, keepdims=True)
    sums_ref[S_ATTN : S_ATTN + 1] += jnp.sum(dn, axis=0, keepdims=True)


def open_back(dres, dh, wi, hat, inv, full, vec, sums):
    t = dres.shape[0]
    return pl.pallas_call(
        open_back_body,
        grid=(t // ROWS,),
        in_specs=[row_block(D), row_block(FF), whole(wi.shape), row_block(D), row_block(1), mat_of(0), whole(vec.shape), whole((16, D))],
        out_specs=[row_block(D)] * 3 + [whole((16, D))],
        out_shape=[S((t, D), f32), S((t, D), low), S((t, D), low), S((16, D), f32)],
        name="open_back",
        **params(10 * t * D * D, 20 * t * D + 10 * D * D, room=60),
    )(dres, dh, wi, hat, inv, full, vec, sums)


def heads_back_body(cube, q_ref, k_ref, v_ref, dc_ref, p_ref, x_ref, before_ref, c_hbm, da_hbm, *refs):
    dq_ref, dk_ref, dv_ref, sums_ref = refs[:4]
    shares, (c_ref, da_ref, sems) = refs[4:-3], refs[-3:]
    step = pl.program_id(0)
    copies = [pltpu.make_async_copy(c_hbm, c_ref, sems.at[0]), pltpu.make_async_copy(da_hbm, da_ref, sems.at[1])]
    masks, masks32 = head_masks(low), head_masks(f32)

    @pl.when(step == 0)
    def _():
        for copy in copies:
            copy.start()

    def sentence(s):
        rows = pl.ds(pl.multiple_of(s * LEN, LEN), LEN)
        q, k, v, dc, p = q_ref[rows, :], k_ref[rows, :], v_ref[rows, :], dc_ref[rows, :], p_ref[0, rows, :]
        dcs = stacked(dc, masks)
        dp = nt(v, dcs)
        dv_ref[rows, :] = nn(p.astype(low), dcs).astype(low)
        ds = (p * (dp - jnp.sum(p * dp, axis=0, keepdims=True))).astype(low)
        dk_ref[rows, :] = (nn(ds, stacked(q, masks)) * HEAD_DIM ** (-0.5)).astype(low)
        dq_ref[rows, :] = (unstacked(tn(ds, k), masks32) * HEAD_DIM ** (-0.5)).astype(low)

    @pl.when(step < GROUPS)
    def _():
        pl.loop(0, q_ref.shape[0] // LEN, unroll=BACK_UNROLL)(sentence)
        sums_ref[...] = jnp.zeros_like(sums_ref)
        sums_ref[0, :16, :] = before_ref[...]
        sums_ref[0, B_QUERY : B_QUERY + 1] = jnp.sum(dq_ref[...].astype(f32), axis=0, keepdims=True)
        sums_ref[0, B_VALUE : B_VALUE + 1] = jnp.sum(dv_ref[...].astype(f32), axis=0, keepdims=True)
        for m, grad in enumerate((dq_ref, dk_ref, dv_ref)):
            put_shares(cube, tn(x_ref[...], grad[...]), shares, m)

    @pl.when(step == GROUPS)
    def _():
        for copy in copies:
            copy.wait()
        for m in range(GROUPS):
            put_shares(cube, tn(c_ref[...], da_ref[:, m * WIDE : (m + 1) * WIDE]), shares, m)


BACK_UNROLL = 16


def put_shares(cube, full, refs, m):
    if cube:
        full = full.reshape(4, 2, 2, 2, 24, WIDE)

        def put(ref, p, q, value):
            ref[:, p, q, m] = value.astype(ref.dtype)

        write_shares(lambda y, x, c: full[:, y, x, c], *refs, put)
    else:
        refs[0][m] = full


def heads_back(q, k, v, dc, p, x, sums, c, da, cube):
    t = q.shape[0]
    col = pl.BlockSpec((t, WIDE), lambda i: (0, jnp.minimum(i, GROUPS - 1)))
    if cube:
        spec = pl.BlockSpec((4, 2, 2, 3, 24, WIDE), lambda i: (0, 0, 0, i, 0, 0))
        shape = (4, 2, 2, 3 * GROUPS + 3, 24, WIDE)
        specs, shapes = [spec] * 2, [S(shape, KEEP), S(shape, low)]
    else:
        specs, shapes = [pl.BlockSpec((3, D, WIDE), lambda i: (i, 0, 0))], [S((3 * GROUPS + 3, D, WIDE), f32)]
    return pl.pallas_call(
        lambda *refs: heads_back_body(cube, *refs),
        grid=(GROUPS + 1,),
        in_specs=[col] * 4
        + [pl.BlockSpec((1, t, WIDE), lambda i: (jnp.minimum(i, GROUPS - 1), 0, 0)), whole((t, D))]
        + [pl.BlockSpec((16, WIDE), lambda i: (0, jnp.minimum(i, GROUPS - 1))), ANY, ANY],
        out_specs=[col] * 3 + [pl.BlockSpec((1, 24, WIDE), lambda i: (jnp.minimum(i, GROUPS - 1), 0, 0))] + specs,
        out_shape=[S((t, D), low)] * 3 + [S((GROUPS, 24, WIDE), f32)] + shapes,
        scratch_shapes=[pltpu.VMEM((t, D), low), pltpu.VMEM((t, D), low), pltpu.SemaphoreType.DMA((2,))],
        name="heads_back",
        **params(t * D * 24000, t * D * 20, room=60),
    )(q, k, v, dc, p, x, sums, c, da)


def gelu_parts(h):
    d = 1.0 + (0.3275911 * 0.7071067811865476) * jnp.abs(h)
    t = pl.reciprocal(d, approx=True)
    t = t * (2.0 - d * t)
    poly = t * (0.127414796 + t * (-0.142248368 + t * (0.7107068705 + t * (-0.7265760135 + t * 0.5307027145))))
    bell = jnp.exp(-0.5 * (h * h))
    tail = poly * bell
    cdf = jnp.where(h >= 0, 1.0 - tail, tail)
    return h * cdf, cdf + h * (bell * 0.3989422804014327)


def inner_body(cube, n_ref, vec_ref, *refs):
    parts, (a_ref, gp_ref, full_ref, w_ref, sems, out_sem) = refs[:-6], refs[-6:]
    onward = assemble(cube, parts, w_ref, full_ref, sems, out_sem)
    n = n_ref[...]
    w = w_ref.reshape(D, FF) if cube else w_ref
    for j in range(FF // BLOCK):
        cols = pl.ds(j * BLOCK, BLOCK)
        h = nn(n, w[:, cols]) + vec_ref[B_INNER + j : B_INNER + j + 1].astype(f32)
        act, slope = gelu_parts(h)
        a_ref[:, cols] = act.astype(low)
        gp_ref[:, cols] = slope.astype(low)

    @pl.when(pl.program_id(0) == pl.num_programs(0) - 1)
    def _():
        onward.wait()


def inner(n, vec, parts, cube):
    t = n.shape[0]
    shape = (4, 2, 2, 2, 24, FF) if cube else (D, FF)
    act, slope, full = pl.pallas_call(
        lambda *refs: inner_body(cube, *refs),
        grid=(t // ROWS,),
        in_specs=[row_block(D), whole(vec.shape)] + [ANY] * len(parts),
        out_specs=[row_block(FF), row_block(FF), ANY],
        out_shape=[S((t, FF), low), S((t, FF), low), S(shape, low)],
        scratch_shapes=[pltpu.VMEM(shape, low), pltpu.SemaphoreType.DMA((4,)), pltpu.SemaphoreType.DMA],
        name="inner",
        **params(6 * t * D * FF, 2 * t * D + 4 * t * FF + 4 * D * FF, 2 * t * FF, room=60),
    )(n, vec, *parts)
    return act, slope, full.reshape(D, FF)


def outer_body(cube, a_ref, hat_ref, vec_ref, *refs):
    parts = refs[:-9]
    out_ref, hat2_ref, inv_ref, cls_ref, unit_ref, full_ref, w_ref, sems, out_sem = refs[-9:]
    onward = assemble(cube, parts, w_ref, full_ref, sems, out_sem)
    step = pl.program_id(0)
    w = w_ref.reshape(FF, D) if cube else w_ref
    branch = nn(a_ref[...], w[...]) + vec_ref[B_OUTER : B_OUTER + 1].astype(f32)
    normed = hat_ref[...] * vec_ref[G_ATTN : G_ATTN + 1].astype(f32) + vec_ref[S_ATTN : S_ATTN + 1].astype(f32)
    hat, inv = layer_norm(normed + branch)
    hat2_ref[...] = hat
    inv_ref[...] = inv
    rows = hat * vec_ref[G_FFN : G_FFN + 1].astype(f32) + vec_ref[S_FFN : S_FFN + 1].astype(f32)
    out_ref[...] = rows.astype(low)
    pairs = rows.shape[0] // LEN // 2
    for s in range(pairs):
        at = pl.ds(step * pairs + s, 1)
        for side in range(2):
            cols = pl.ds(side * D, D)
            cls = rows[LEN * (2 * s + side) : LEN * (2 * s + side) + 1]
            cls_ref[at, cols] = cls
            unit_ref[at, cols] = cls * lax.rsqrt(jnp.sum(cls * cls, axis=-1, keepdims=True) + pool_eps)

    @pl.when(step == pl.num_programs(0) - 1)
    def _():
        onward.wait()


def outer(act, hat, vec, parts, cube):
    t = hat.shape[0]
    shape = (4, 2, 2, 2, 96, D) if cube else (FF, D)
    pairs = t // LEN // 2
    once = pl.BlockSpec((pairs, 2 * D), lambda i: (0, 0))
    *outs, full = pl.pallas_call(
        lambda *refs: outer_body(cube, *refs),
        grid=(t // ROWS,),
        in_specs=[row_block(FF), row_block(D), whole(vec.shape)] + [ANY] * len(parts),
        out_specs=[row_block(D), row_block(D), row_block(1), once, once, ANY],
        out_shape=[S((t, D), low), S((t, D), f32), S((t, 1), f32), S((pairs, 2 * D), f32), S((pairs, 2 * D), f32), S(shape, low)],
        scratch_shapes=[pltpu.VMEM(shape, low), pltpu.SemaphoreType.DMA((4,)), pltpu.SemaphoreType.DMA],
        name="outer",
        **params(2 * t * D * FF, 10 * t * D + 2 * t * FF + 4 * D * FF, room=60),
    )(act, hat, vec, *parts)
    return *outs, full.reshape(FF, D)


def write_shares(full, keep_ref, away_ref, put):
    core = lax.axis_index(AXIS) & 1

    def write(zero, one):
        for y in range(2):
            for x in range(2):
                put(zero, x, y, full(y, x, 0))
                put(one, y, x, full(y, x, 1))

    @pl.when(core == 0)
    def _():
        write(keep_ref, away_ref)

    @pl.when(core == 1)
    def _():
        write(away_ref, keep_ref)


def outer_back_body(cube, cot_ref, dc_ref, hat2_ref, inv2_ref, a_ref, vec_ref, dres_ref, dbr_ref, sums_ref, *refs):
    j = pl.program_id(0)

    @pl.when(j == 0)
    def _():
        dgain = jnp.zeros((1, D), f32)
        dshift = jnp.zeros((1, D), f32)
        dbias = jnp.zeros((1, D), f32)
        at = lax.broadcasted_iota(jnp.int32, (ROWS, D), 0)
        for b in range(cot_ref.shape[0] // ROWS):
            rows = pl.ds(b * ROWS, ROWS)
            d = cot_ref[rows, :].astype(f32)
            hat = hat2_ref[rows, :]
            for s in range(ROWS // LEN):
                whose = b * (ROWS // LEN) + s
                extra = dc_ref[whose // 2 : whose // 2 + 1, (whose % 2) * D : (whose % 2 + 1) * D]
                d += jnp.where(at == LEN * s, extra, 0.0)
            dgain += jnp.sum(d * hat, axis=0, keepdims=True)
            dshift += jnp.sum(d, axis=0, keepdims=True)
            dres = layer_norm_back(d, vec_ref[G_FFN : G_FFN + 1].astype(f32), hat, inv2_ref[rows, :])
            dres_ref[rows, :] = dres
            dbr = dres.astype(low)
            dbr_ref[rows, :] = dbr
            dbias += jnp.sum(dbr.astype(f32), axis=0, keepdims=True)
        sums_ref[...] = jnp.zeros_like(sums_ref)
        sums_ref[B_OUTER : B_OUTER + 1] = dbias
        sums_ref[G_FFN : G_FFN + 1] = dgain
        sums_ref[S_FFN : S_FFN + 1] = dshift

    dw = tn(a_ref[...], dbr_ref[...])
    if cube:
        dw = dw.reshape(2, 2, 2, 96, D)

        def put(ref, p, q, value):
            ref[0, p, q] = value.astype(ref.dtype)

        write_shares(lambda y, x, c: dw[y, x, c], *refs, put)
    else:
        refs[0][...] = dw


def outer_back(cot, dc, hat2, inv2, a, vec, cube):
    t = cot.shape[0]
    if cube:
        spec = pl.BlockSpec((1, 2, 2, 96, D), lambda j: (j, 0, 0, 0, 0))
        specs, shapes = [spec] * 2, [S((4, 2, 2, 96, D), KEEP), S((4, 2, 2, 96, D), low)]
    else:
        specs, shapes = [pl.BlockSpec((BLOCK, D), lambda j: (j, 0))], [S((FF, D), f32)]
    return pl.pallas_call(
        lambda *refs: outer_back_body(cube, *refs),
        grid=(FF // BLOCK,),
        in_specs=[whole((t, D)), whole(dc.shape), whole((t, D)), whole((t, 1)), pl.BlockSpec((t, BLOCK), lambda j: (0, j)),
                  whole(vec.shape)],
        out_specs=[whole((t, D)), whole((t, D)), whole((16, D))] + specs,
        out_shape=[S((t, D), f32), S((t, D), low), S((16, D), f32)] + shapes,
        name="outer_back",
        **params(4 * t * D * FF, 14 * t * D + 2 * t * FF + 8 * D * FF, room=60),
    )(cot, dc, hat2, inv2, a, vec)


def inner_back_body(cube, dbr_ref, n_ref, gp_ref, wo_ref, before_ref, dh_ref, sums_ref, *refs):
    @pl.when(pl.program_id(0) == 0)
    def _():
        sums_ref[...] = before_ref[...]

    dh = (gp_ref[...].astype(f32) * nt(dbr_ref[...], wo_ref[...])).astype(low)
    dh_ref[...] = dh
    sums_ref[pl.ds(B_INNER + pl.program_id(0), 1), :] = jnp.sum(dh.astype(f32), axis=0, keepdims=True)
    dw = tn(n_ref[...], dh)
    if cube:
        dw = dw.reshape(4, 2, 2, 2, 24, BLOCK)

        def put(ref, p, q, value):
            ref[:, p, q] = value.astype(ref.dtype)

        write_shares(lambda y, x, c: dw[:, y, x, c], *refs, put)
    else:
        refs[0][...] = dw


def inner_back(dbr, n, gp, wo, sums, cube):
    t = n.shape[0]
    fblk = pl.BlockSpec((t, BLOCK), lambda j: (0, j))
    if cube:
        spec = pl.BlockSpec((4, 2, 2, 24, BLOCK), lambda j: (0, 0, 0, 0, j))
        specs, shapes = [spec] * 2, [S((4, 2, 2, 24, FF), KEEP), S((4, 2, 2, 24, FF), low)]
    else:
        specs, shapes = [pl.BlockSpec((D, BLOCK), lambda j: (0, j))], [S((D, FF), f32)]
    return pl.pallas_call(
        lambda *refs: inner_back_body(cube, *refs),
        grid=(FF // BLOCK,),
        in_specs=[whole((t, D)), whole((t, D)), fblk, pl.BlockSpec((BLOCK, D), lambda j: (j, 0)), whole((16, D))],
        out_specs=[fblk, whole((16, D))] + specs,
        out_shape=[S((t, FF), low), S((16, D), f32)] + shapes,
        name="inner_back",
        **params(4 * t * D * FF, 4 * t * D + 4 * t * FF + 8 * D * FF, room=60),
    )(dbr, n, gp, wo, sums)


KEEP = low


def token_grad_body(dr_ref, dq_ref, dk_ref, dv_ref, wq_ref, wk_ref, wv_ref, o_ref):
    o_ref[...] = (
        dr_ref[...] + nt(dq_ref[...], wq_ref[0]) + nt(dk_ref[...], wk_ref[0]) + nt(dv_ref[...], wv_ref[0])
    )


def token_grad(dr, dq, dk, dv, full):
    t = dr.shape[0]

    return pl.pallas_call(
        token_grad_body,
        grid=(t // ROWS,),
        in_specs=[row_block(D)] * 4 + [mat_of(0), mat_of(1), mat_of(2)],
        out_specs=row_block(D),
        out_shape=S((t, D), f32),
        name="token_grad",
        **params(6 * t * D * D, 14 * t * D + 6 * D * D, room=60),
    )(dr, dq, dk, dv, full, full, full)


def loss_body(units_ref, codes_ref, cls_ref, loss_ref, dc_ref, table_ref, ds_ref):
    sources, targets = units_ref[:, :D], units_ref[:, D:]
    pairs, own = units_ref.shape[0], cls_ref.shape[0]
    codes = codes_ref[CODES : CODES + 2, :pairs].astype(f32)
    partner = (codes[0:1] + 64.0 * codes[1:2]).astype(jnp.int32)
    matched = lax.broadcasted_iota(jnp.int32, (pairs, pairs), 0) == partner
    sims = nt(targets, sources) * sim_scale - jnp.where(matched, sim_scale * sim_margin, 0.0)
    row_top = jnp.max(sims, axis=0, keepdims=True)
    row_lse = row_top + jnp.log(jnp.sum(jnp.exp(sims - row_top), axis=0, keepdims=True))
    col_top = jnp.max(sims, axis=1, keepdims=True)
    col_lse = col_top + jnp.log(jnp.sum(jnp.exp(sims - col_top), axis=1, keepdims=True))
    total = (
        jnp.sum(row_lse, axis=1, keepdims=True)
        + jnp.sum(col_lse, axis=0, keepdims=True)
        - 2.0 * jnp.sum(jnp.sum(jnp.where(matched, sims, 0.0), axis=1, keepdims=True), axis=0, keepdims=True)
    )
    loss_ref[...] = jnp.broadcast_to(total * (0.5 / pairs), loss_ref.shape)
    d_sims = 0.5 * (jnp.exp(sims - row_lse) + jnp.exp(sims - col_lse)) - jnp.where(matched, 1.0, 0.0)
    d_low = (d_sims * sim_scale).astype(low)
    table_ref[...] = nn(d_low, sources)
    ds_ref[...] = tn(d_low, targets)
    mine = pl.ds(pl.multiple_of(lax.axis_index(AXIS) * own, own), own)
    for side, ref in enumerate((ds_ref, table_ref)):
        cols = pl.ds(side * D, D)
        cls, du = cls_ref[:, cols], ref[mine, :]
        inv = lax.rsqrt(jnp.sum(cls * cls, axis=-1, keepdims=True) + pool_eps)
        dc_ref[:, cols] = inv * du - cls * (inv * inv * inv * jnp.sum(du * cls, axis=-1, keepdims=True))


def pair_loss(units, vec, cls):
    pairs, own = units.shape[0], cls.shape[0]
    loss, dc = pl.pallas_call(
        loss_body,
        in_specs=[whole(units.shape), whole(vec.shape), whole(cls.shape)],
        out_specs=[whole((8, 128)), whole(cls.shape)],
        out_shape=[S((8, 128), f32), S(cls.shape, f32)],
        scratch_shapes=[pltpu.VMEM((pairs, D), f32), pltpu.VMEM((pairs, D), f32)],
        grid=(1,),
        name="pair_loss",
        **params(6 * pairs * pairs * D, 4 * pairs * D, 4 * pairs * pairs, room=60),
    )(units, vec, cls)
    return loss[0, 0], dc


CUBE = 32
CORE = [(i, i ^ 1) for i in range(CUBE)]
FAR_Z = [(i, i ^ 16) for i in range(CUBE)]
NEAR_Z = [(i, i ^ 8) for i in range(CUBE)]
FIRST = [(i, i ^ (4 if i & 1 else 2)) for i in range(CUBE)]
SECOND = [(i, i ^ (2 if i & 1 else 4)) for i in range(CUBE)]
ROUTES = (CORE, FIRST, SECOND, NEAR_Z, FAR_Z)


class Place:
    def __init__(self):
        self.me = lax.axis_index(AXIS)
        self.core = self.me & 1
        x, y = (self.me >> 1) & 1, (self.me >> 2) & 1
        self.near_z, self.far_z = (self.me >> 3) & 1, (self.me >> 4) & 1
        self.first = jnp.where(self.core == 0, x, y)
        self.second = jnp.where(self.core == 0, y, x)


def join(own, other, axis, bit):
    shape = own.shape[:axis] + (2,) + own.shape[axis:]
    where = lax.broadcasted_iota(jnp.int32, shape, axis)
    return jnp.where(where == bit, jnp.expand_dims(own, axis), jnp.expand_dims(other, axis))


def pick(field, axis, bit):
    return lax.dynamic_index_in_dim(field, bit, axis, keepdims=False)


def send(field, route):
    return lax.ppermute(field, AXIS, route)


def spread(block, place):
    block = join(block, send(block, FAR_Z), 0, place.far_z)
    block = join(block, send(block, NEAR_Z), 1, place.near_z)
    return join(block, send(block, FIRST), 2, place.first)


def gather_blocks(block, place):
    near = spread(block, place)
    block = join(near, send(near, SECOND), 3, place.second)
    other = send(block, CORE)
    zero = jnp.where(place.core == 0, block, other)
    one = jnp.where(place.core == 0, other, block)
    return jnp.stack([jnp.swapaxes(zero, 2, 3), one], axis=4).reshape(-1, block.shape[-1])


def together(*values):
    return lax.optimization_barrier(values)


class Reduction:
    def __init__(self, shares, place, early_z=False):
        keep, self.away = shares
        self.terms = [keep.reshape(2, 2, *keep.shape[1:])]
        self.left = [(2, place.first), (2, place.second), (1, place.near_z), (0, place.far_z)]
        if early_z:
            self.left = [(1, place.near_z), (1, place.first), (1, place.second), (0, place.far_z)]
        self.came = self.along = None

    def total(self):
        self.settle()
        return sum(term.astype(f32) for term in self.terms)

    def take_along(self, along):
        self.along = along

    def start(self, route):
        away = self.away
        if self.along is not None:
            away = jnp.concatenate([away.reshape(-1, *self.along.shape[1:]), self.along.astype(low)], axis=0)
        self.came, self.away = send(away, route), None

    def settle(self):
        if self.came is not None:
            came, self.came = self.came, None
            if self.along is not None:
                count = self.along.shape[0]
                self.along = self.along + came[-count:].astype(f32)
                came = came[:-count]
            self.terms.append(came.reshape(self.terms[0].shape))
            if self.left:
                axis, bit = self.left.pop(0)
                self.away = sum(pick(term, axis, 1 - bit).astype(f32) for term in self.terms).astype(low)
                self.terms = [pick(term, axis, bit) for term in self.terms]


def windows(sums, *values):
    for s in sums:
        s.settle()
    aways = [s.away for s in sums if s.away is not None]
    done = together(*values, *aways)
    values, aways = done[: len(values)], list(done[len(values) :])
    for s in sums:
        if s.away is not None:
            s.away = aways.pop(0)
    return values


def spread_rows(rows, at, count):
    r = rows.shape[1]
    lane = lax.broadcasted_iota(jnp.int32, (r, D), 1)
    copies = nn(rows, jnp.where(lane % r == lax.broadcasted_iota(jnp.int32, (r, D), 0), 1.0, 0.0).astype(low))
    lane = lax.broadcasted_iota(jnp.int32, (count, D), 1)
    row = lax.broadcasted_iota(jnp.int32, (count, D), 0)
    return copies, lane // r, row


def vector_table(vectors, partners, place):
    *small, inner = vectors
    copies, lane, _ = spread_rows(jnp.stack(small), place.me, len(small))
    table = [jnp.where(lane == place.me, copies, 0.0)]
    fold = D // inner.shape[0]
    copies, lane, row = spread_rows(inner[None], place.me, FF // D)
    table.append(jnp.where((row == place.me // fold) & (lane == place.me % fold), copies, 0.0))
    codes = jnp.stack([partners % 64, partners // 64]).astype(low)
    copies, lane, _ = spread_rows(codes, place.me, 2)
    table.append(jnp.where(lane == place.me, copies, 0.0))
    table.append(jnp.zeros((2, D), f32))
    return jnp.concatenate(table, axis=0).astype(low)


def own_vectors(total, place):
    r, fold = D // CUBE, FF // CUBE
    mine = lax.dynamic_slice(total, (0, place.me * r), (B_INNER, r))
    inner = lax.dynamic_slice(total, (B_INNER + place.me // (D // fold), (place.me % (D // fold)) * fold), (1, fold))
    return [mine[i] for i in range(B_INNER)] + [inner[0]]


def pack_body(*refs):
    *mats, out = refs
    r = mats[0].shape[0]
    for i, mat in enumerate(mats):
        out[i * r : (i + 1) * r, :] = mat[...]


def pack(*mats):
    r, n = mats[0].shape
    return pl.pallas_call(pack_body, out_shape=S((len(mats) * r, n), low), name="pack")(*mats)


def plain_loss(units, partners, cls):
    sources, targets = units[:, :D], units[:, D:]
    npairs, own = units.shape[0], cls.shape[0]
    sims = nt(sources, targets) * sim_scale
    matched = partners[:, None] == jnp.arange(npairs, dtype=jnp.int32)[None, :]
    sims = sims - jnp.where(matched, sim_scale * sim_margin, 0.0)
    row_top = jnp.max(sims, axis=1, keepdims=True)
    row_lse = row_top + jnp.log(jnp.sum(jnp.exp(sims - row_top), axis=1, keepdims=True))
    col_top = jnp.max(sims, axis=0, keepdims=True)
    col_lse = col_top + jnp.log(jnp.sum(jnp.exp(sims - col_top), axis=0, keepdims=True))
    positive = jnp.sum(jnp.where(matched, sims, 0.0))
    loss = (jnp.sum(row_lse) + jnp.sum(col_lse) - 2.0 * positive) / (2.0 * npairs)
    d_sims = 0.5 * (jnp.exp(sims - row_lse) + jnp.exp(sims - col_lse)) - jnp.where(matched, 1.0, 0.0)
    d_low = (d_sims * sim_scale).astype(low)
    first = lax.axis_index(AXIS) * own
    du = [
        nn(lax.dynamic_slice_in_dim(d_low, first, own, 0), targets),
        tn(lax.dynamic_slice_in_dim(d_low, first, own, 1), sources),
    ]
    dc = []
    for side in range(2):
        c = cls[:, side * D : (side + 1) * D]
        inv = lax.rsqrt(jnp.sum(c * c, axis=-1, keepdims=True) + pool_eps)
        dc.append(inv * du[side] - c * (inv * inv * inv * jnp.sum(du[side] * c, axis=-1, keepdims=True)))
    return loss, jnp.concatenate(dc, axis=1)


def every(v):
    return lax.all_gather(v, AXIS, axis=0, tiled=True)


def scatter(v):
    return lax.psum_scatter(v, AXIS, scatter_dimension=0, tiled=True)


def local(
    tokens,
    lengths,
    partners,
    out_cotangent,
    w_query,
    w_key,
    w_value,
    w_output,
    b_query,
    b_value,
    b_output,
    gain_attn,
    shift_attn,
    w_inner,
    b_inner,
    w_outer,
    b_outer,
    gain_ffn,
    shift_ffn,
):
    cube = lax.axis_size(AXIS) == CUBE
    count = tokens.shape[0]
    x = tokens.reshape(count * LEN, D)
    vectors = (b_query, b_value, b_output, gain_attn, shift_attn, b_outer, gain_ffn, shift_ffn, b_inner)
    blocks = count * LEN // ROWS
    lower, higher = blocks // 2, blocks - blocks // 2
    if cube:
        place = Place()
        qkv = pack(w_query, w_key, w_value)
        vec = vector_table(vectors, partners, place)
        qkv = join(qkv, send(qkv, FAR_Z), 0, place.far_z)
        vec = vec + send(vec, FAR_Z)
        qkv, vec, w_output = together(qkv, vec, w_output)
        qkv = join(qkv, send(qkv, NEAR_Z), 1, place.near_z)
        vec = vec + send(vec, NEAR_Z)
        prj = join(w_output, send(w_output, FAR_Z), 0, place.far_z)
        qkv, vec, prj, w_inner = together(qkv, vec, prj, w_inner)
        qkv = join(qkv, send(qkv, FIRST), 2, place.first).reshape(4, 2, 72, D)
        vec = vec + send(vec, FIRST)
        prj = join(prj, send(prj, NEAR_Z), 1, place.near_z)
        inn = join(w_inner, send(w_inner, FAR_Z), 0, place.far_z)
        qkv, vec, prj, inn = together(qkv, vec, prj, inn)
        far = send(qkv, SECOND)
        other = send(qkv, CORE)
        vec = vec + send(vec, SECOND)
        prj = join(prj, send(prj, FIRST), 2, place.first).reshape(4, 2, 24, D)
        inn = join(inn, send(inn, NEAR_Z), 1, place.near_z)
        far, other, vec, prj, inn = together(far, other, vec, prj, inn)
        qkv_parts = (qkv, far, other, send(far, CORE))
        vec = vec + send(vec, CORE)
        qkv_parts, vec, prj, inn, w_outer = together(qkv_parts, vec, prj, inn, w_outer)
        inn = join(inn, send(inn, FIRST), 2, place.first).reshape(4, 2, 24, FF)
        prj_far = send(prj, SECOND)
        out = join(w_outer, send(w_outer, FAR_Z), 0, place.far_z)
        queries, keys, values, full = project(x, vec, qkv_parts, cube)
        queries, prj_far, inn, out = together(queries, prj_far, inn, out)
        inn_far = send(inn, SECOND)
        out = join(out, send(out, NEAR_Z), 1, place.near_z)
        prj_parts = (prj, prj_far, send(prj, CORE), send(prj_far, CORE))
        probs, context = attend(lengths, queries, keys, values, 0, blocks)
        context, inn, inn_far, out, prj_parts = together(context, inn, inn_far, out, prj_parts)
        inn_parts = (inn, inn_far, send(inn, CORE), send(inn_far, CORE))
        out = join(out, send(out, FIRST), 2, place.first).reshape(4, 2, 96, D)
        hat1, inv1, normed, output_mat = close(x, context, vec, prj_parts, cube)
        normed, inn_parts, out = together(normed, inn_parts, out)
        out_far = send(out, SECOND)
        other = send(out, CORE)
        act, slope, inner_mat = inner(normed, vec, inn_parts, cube)
        act, out_far, other = together(act, out_far, other)
        out_parts = (out, out_far, other, send(out_far, CORE))
        block_out, hat2, inv2, cls, unit, outer_mat = outer(act, hat1, vec, out_parts, cube)
        loss, d_cls = pair_loss(gather_blocks(unit.astype(low), place), vec, cls)
        dres, dbr, sums, *shares = outer_back(
            out_cotangent.reshape(count * LEN, D), d_cls, hat2, inv2, act, vec, cube
        )
        o = Reduction(shares, place)
        (dbr,) = windows([o], dbr)
        o.start(CORE)
        dh, sums, *shares = inner_back(dbr, normed, slope, outer_mat, sums, cube)
        i = Reduction(shares, place, early_z=True)
        (dh,) = windows([o, i], dh)
        o.start(FIRST)
        i.start(CORE)
        d_resid, d_attn, d_context, sums = open_back(dres, dh, inner_mat, hat1, inv1, output_mat, vec, sums)
        (d_context,) = windows([o, i], d_context)
        o.start(SECOND)
        i.start(NEAR_Z)
        d_queries, d_keys, d_values, sums, *shares = heads_back(
            queries, keys, values, d_context, probs, x, sums, context, d_attn, cube
        )
        a = Reduction(shares, place)
        d_queries, sums, *came = together(d_queries, sums, a.away, o.came, i.came)
        a.away, o.came, i.came = came
        a.start(CORE)
        sums = sums + send(sums.astype(low), CORE).astype(f32)
        a.settle()
        a.take_along(sums)
        windows([o, i, a])
        a.start(FIRST)
        o.start(NEAR_Z)
        i.start(FIRST)
        grad_rows = token_grad(d_resid, d_queries, d_keys, d_values, full)
        (grad_rows,) = windows([o, i, a], grad_rows)
        a.start(SECOND)
        i.start(SECOND)
        o.start(FAR_Z)
        windows([i, a])
        a.start(NEAR_Z)
        i.start(FAR_Z)
        windows([a])
        a.start(FAR_Z)
        grad_w_outer, grad_w_inner, g_a = o.total(), i.total(), a.total()
        g_mats = [jnp.concatenate([g_a[n], g_a[3 + n], g_a[6 + n]], axis=1) for n in range(3)]
        g_mats.append(jnp.concatenate([g_a[9], g_a[10], g_a[11]], axis=1))
        sums = jnp.concatenate([a.along[g] for g in range(GROUPS)], axis=1)
        grads = own_vectors(sums, place)
    else:
        rows = [every(v).reshape(-1, D) for v in vectors]
        vec = jnp.concatenate(rows + [jnp.zeros((4, D), low)], axis=0)
        qkv_parts = (jnp.stack([every(w) for w in (w_query, w_key, w_value)]),)
        queries, keys, values, full = project(x, vec, qkv_parts, cube)
        probs, context = attend(lengths, queries, keys, values, 0, blocks)
        hat1, inv1, normed, output_mat = close(x, context, vec, (every(w_output),), cube)
        act, slope, inner_mat = inner(normed, vec, (every(w_inner),), cube)
        block_out, hat2, inv2, cls, unit, outer_mat = outer(act, hat1, vec, (every(w_outer),), cube)
        loss, d_cls = plain_loss(every(unit.astype(low)), every(partners), cls)
        dres, dbr, sums, d_outer = outer_back(
            out_cotangent.reshape(count * LEN, D), d_cls, hat2, inv2, act, vec, cube
        )
        dh, sums, d_inner = inner_back(dbr, normed, slope, outer_mat, sums, cube)
        d_resid, d_attn, d_context, sums = open_back(dres, dh, inner_mat, hat1, inv1, output_mat, vec, sums)
        d_queries, d_keys, d_values, sums, d_a = heads_back(
            queries, keys, values, d_context, probs, x, sums, context, d_attn, cube
        )
        sums = jnp.concatenate([sums[g] for g in range(GROUPS)], axis=1)
        grad_rows = token_grad(d_resid, d_queries, d_keys, d_values, full)
        grad_w_outer, grad_w_inner = scatter(d_outer), scatter(d_inner)
        d_mats = [jnp.concatenate([d_a[n], d_a[3 + n], d_a[6 + n]], axis=1) for n in range(3)]
        d_mats.append(jnp.concatenate([d_a[9], d_a[10], d_a[11]], axis=1))
        g_mats = [scatter(d) for d in d_mats]
        grads = [scatter(sums[n]) for n in range(B_INNER)] + [scatter(sums[B_INNER:CODES].reshape(-1))]
    (
        grad_b_query,
        grad_b_value,
        grad_b_output,
        grad_gain_attn,
        grad_shift_attn,
        grad_b_outer,
        grad_gain_ffn,
        grad_shift_ffn,
        grad_b_inner,
    ) = grads
    return (
        loss,
        block_out.reshape(count, LEN, D),
        grad_rows.reshape(count, LEN, D),
        g_mats[0],
        g_mats[1],
        g_mats[2],
        g_mats[3],
        grad_b_query,
        grad_b_value,
        grad_b_output,
        grad_gain_attn,
        grad_shift_attn,
        grad_w_inner,
        grad_b_inner,
        grad_w_outer,
        grad_b_outer,
        grad_gain_ffn,
        grad_shift_ffn,
    )


def solution(mesh):
    rows, cols = P(AXIS), P(AXIS, None)
    cube = P(AXIS, None, None)
    in_specs = (cube, rows, rows, cube) + (cols,) * 4 + (rows,) * 5 + (cols, rows, cols) + (rows,) * 3
    out_specs = (P(), cube, cube) + (cols,) * 4 + (rows,) * 5 + (cols, rows, cols) + (rows,) * 3
    return jax.shard_map(local, mesh=mesh, in_specs=in_specs, out_specs=out_specs, check_vma=False)
```

```python
import jax
import jax.numpy as jnp
from jax import lax
from jax.experimental import pallas as pl
from jax.experimental.pallas import tpu as pltpu
from jax.sharding import PartitionSpec as P

D = 768
HEADS = 12
HEAD_DIM = 64
LEN = 64
FF = 3072
QUAD = 4
WIDE = QUAD * HEAD_DIM
GROUPS = HEADS // QUAD
ROWS = 256
BLOCK = 768
AXIS = "fsdp"
CUBE = 32
norm_eps = 1e-12
pool_eps = 1e-06
sim_scale = 50.0
sim_margin = 0.3
f32, low = jnp.float32, jnp.bfloat16
S = jax.ShapeDtypeStruct

B_QUERY, B_VALUE, B_OUTPUT, G_ATTN, S_ATTN, B_OUTER, G_FFN, S_FFN, B_INNER = range(9)
CODES = B_INNER + FF // D


def nn(a, b):
    return lax.dot_general(a, b, (((1,), (0,)), ((), ())), preferred_element_type=f32)


def nt(a, b):
    return lax.dot_general(a, b, (((1,), (1,)), ((), ())), preferred_element_type=f32)


def tn(a, b):
    return lax.dot_general(a, b, (((0,), (0,)), ((), ())), preferred_element_type=f32)


def whole(shape):
    return pl.BlockSpec(shape, lambda *_: (0,) * len(shape), pipeline_mode=pl.Buffered(1))


def row_block(width, rows=ROWS):
    return pl.BlockSpec((rows, width), lambda i, *_: (i, 0))


def params(flops, nbytes, exps=0, room=60):
    return dict(
        compiler_params=pltpu.CompilerParams(vmem_limit_bytes=room << 20),
        cost_estimate=pl.CostEstimate(flops=int(flops), bytes_accessed=int(nbytes), transcendentals=int(exps)),
    )


ANY = pl.BlockSpec(memory_space=pl.ANY)


def part_copies(parts, target, sems, cut):
    me = lax.axis_index(AXIS)
    core, x, y = me & 1, (me >> 1) & 1, (me >> 2) & 1

    def start(zero, one):
        for i in range(2):
            pltpu.make_async_copy(cut(zero[i]), target.at[:, (y + i) & 1, :, 0], sems.at[2 * i]).start()
            pltpu.make_async_copy(cut(one[i]), target.at[:, :, (x + i) & 1, 1], sems.at[2 * i + 1]).start()

    @pl.when(core == 0)
    def _():
        start(parts[:2], parts[2:])

    @pl.when(core == 1)
    def _():
        start(parts[2:], parts[:2])


def part_waits(parts, target, sems, cut):
    for i in range(2):
        pltpu.make_async_copy(cut(parts[i]), target.at[:, i, :, 0], sems.at[2 * i]).wait()
        pltpu.make_async_copy(cut(parts[i]), target.at[:, :, i, 1], sems.at[2 * i + 1]).wait()


def everything(ref):
    return ref


def project_body(cube, x_ref, vec_ref, *refs):
    parts, (q_ref, k_ref, v_ref, full_ref, w_ref, sems, out_sem) = refs[:-7], refs[-7:]
    step = pl.program_id(0)
    onward = pltpu.make_async_copy(w_ref, full_ref, out_sem)

    @pl.when(step == 0)
    def _():
        if cube:

            def cut(m):
                return lambda ref: ref.at[:, :, pl.ds(m * 24, 24), :]

            for m in range(3):
                part_copies(parts, w_ref.at[m], sems.at[m], cut(m))
            for m in range(3):
                part_waits(parts, w_ref.at[m], sems.at[m], cut(m))
        else:
            copy = pltpu.make_async_copy(parts[0], w_ref, sems.at[0, 0])
            copy.start()
            copy.wait()
        onward.start()

    x = x_ref[...]

    def mat(m):
        return w_ref.at[m].reshape(D, D)[...] if cube else w_ref[m]

    q_ref[...] = (nn(x, mat(0)) + vec_ref[B_QUERY : B_QUERY + 1].astype(f32)).astype(low)
    k_ref[...] = nn(x, mat(1)).astype(low)
    v_ref[...] = (nn(x, mat(2)) + vec_ref[B_VALUE : B_VALUE + 1].astype(f32)).astype(low)

    @pl.when(step == pl.num_programs(0) - 1)
    def _():
        onward.wait()


def project(x, vec, parts, cube):
    t = x.shape[0]
    shape = (3, 4, 2, 2, 2, 24, D) if cube else (3, D, D)
    q, k, v, full = pl.pallas_call(
        lambda *refs: project_body(cube, *refs),
        grid=(t // ROWS,),
        in_specs=[row_block(D), whole(vec.shape)] + [ANY] * len(parts),
        out_specs=[row_block(D)] * 3 + [ANY],
        out_shape=[S((t, D), low)] * 3 + [S(shape, low)],
        scratch_shapes=[pltpu.VMEM(shape, low), pltpu.SemaphoreType.DMA((3, 4)), pltpu.SemaphoreType.DMA],
        name="project",
        **params(6 * t * D * D, 8 * t * D + 12 * D * D, room=60),
    )(x, vec, *parts)
    return q, k, v, full.reshape(3, D, D)


def assemble(cube, parts, w_ref, full_ref, sems, out_sem):
    onward = pltpu.make_async_copy(w_ref, full_ref, out_sem)

    @pl.when(pl.program_id(0) == 0)
    def _():
        if cube:
            part_copies(parts, w_ref, sems, everything)
            part_waits(parts, w_ref, sems, everything)
        else:
            copy = pltpu.make_async_copy(parts[0], w_ref, sems.at[0])
            copy.start()
            copy.wait()
        onward.start()

    return onward


def scratch_for(shape):
    return [pltpu.VMEM(shape, low), pltpu.SemaphoreType.DMA((4,)), pltpu.SemaphoreType.DMA]


def head_masks(dtype):
    lane = lax.broadcasted_iota(jnp.int32, (1, WIDE), 1) // HEAD_DIM
    return [jnp.where(lane == h, 1.0, 0.0).astype(dtype) for h in range(QUAD)]


def stacked(rows, masks):
    return jnp.concatenate([rows * m for m in masks], axis=0)


def unstacked(full, masks):
    return sum(full[LEN * h : LEN * (h + 1)] * m for h, m in enumerate(masks))


def layer_norm(resid):
    centred = resid - jnp.mean(resid, axis=-1, keepdims=True)
    inv = lax.rsqrt(jnp.mean(centred * centred, axis=-1, keepdims=True) + norm_eps)
    return centred * inv, inv


def layer_norm_back(grad, gain, hat, inv):
    grad = grad * gain
    mean = jnp.mean(grad, axis=-1, keepdims=True)
    along = jnp.mean(grad * hat, axis=-1, keepdims=True)
    return (grad - mean - hat * along) * inv


def attend_body(start, len_ref, q_ref, k_ref, v_ref, *refs):
    p_ref, c_ref = refs[-2:]
    masks, masks32 = head_masks(low), head_masks(f32)
    per = ROWS // LEN
    first = (start + pl.program_id(0)) * per
    key_at = lax.broadcasted_iota(jnp.int32, (LEN, WIDE), 0)

    def sentence(s):
        rows = pl.ds(pl.multiple_of(s * LEN, LEN), LEN)
        seen = key_at < len_ref[first + s]
        for g in range(GROUPS):
            cols = pl.ds(g * WIDE, WIDE)
            q, k, v = q_ref[rows, cols], k_ref[rows, cols], v_ref[rows, cols]
            scores = nt(k, stacked(q, masks)) * HEAD_DIM ** (-0.5)
            scores = jnp.where(seen, scores, -1e30)
            expd = jnp.exp(scores - jnp.max(scores, axis=0, keepdims=True))
            probs = expd * (1.0 / jnp.sum(expd, axis=0, keepdims=True))
            p_ref[g, rows, :] = probs
            c_ref[rows, cols] = unstacked(tn(probs.astype(low), v), masks32).astype(low)

    pl.loop(0, per, unroll=UNROLL)(sentence)


UNROLL = 4


def some_rows(start):
    return lambda width, rows=ROWS: pl.BlockSpec((rows, width), lambda i, *_: (start + i, 0))


def mat_of(m):
    return pl.BlockSpec((1, D, D), lambda *_: (m, 0, 0), pipeline_mode=pl.Buffered(1))


def attend(lengths, q, k, v, start, count, before=()):
    t = q.shape[0]
    rows = some_rows(start)
    return pl.pallas_call(
        lambda *refs: attend_body(start, *refs),
        grid_spec=pltpu.PrefetchScalarGridSpec(
            num_scalar_prefetch=1,
            grid=(count,),
            in_specs=[rows(D)] * 3 + [ANY] * len(before),
            out_specs=[pl.BlockSpec((GROUPS, ROWS, WIDE), lambda i, *_: (0, start + i, 0)), rows(D)],
        ),
        out_shape=[S((GROUPS, t, WIDE), f32), S((t, D), low)],
        input_output_aliases={4 + i: i for i in range(len(before))},
        name="attend",
        **params(10 * count * ROWS * D * D, 20 * count * ROWS * D, count * ROWS * D, room=60),
    )(lengths, q, k, v, *before)


def halves(ref):
    return [slice(i * ROWS, (i + 1) * ROWS) for i in range(ref.shape[0] // ROWS)]


def close_body(cube, x_ref, c_ref, vec_ref, *refs):
    parts, (hat_ref, inv_ref, n_ref, full_ref, w_ref, sems, out_sem) = refs[:-7], refs[-7:]
    onward = assemble(cube, parts, w_ref, full_ref, sems, out_sem)
    w = (w_ref.reshape(D, D) if cube else w_ref)[...]
    branches = [nn(c_ref[r, :], w) + vec_ref[B_OUTPUT : B_OUTPUT + 1].astype(f32) for r in halves(x_ref)]
    for r, branch in zip(halves(x_ref), branches):
        hat, inv = layer_norm(x_ref[r, :].astype(f32) + branch)
        hat_ref[r, :] = hat
        inv_ref[r, :] = inv
        n_ref[r, :] = (hat * vec_ref[G_ATTN : G_ATTN + 1].astype(f32) + vec_ref[S_ATTN : S_ATTN + 1].astype(f32)).astype(low)

    @pl.when(pl.program_id(0) == pl.num_programs(0) - 1)
    def _():
        onward.wait()


def close(x, c, vec, parts, cube):
    t = x.shape[0]
    shape = (4, 2, 2, 2, 24, D) if cube else (D, D)
    hat, inv, n, full = pl.pallas_call(
        lambda *refs: close_body(cube, *refs),
        grid=(t // (2 * ROWS),),
        in_specs=[row_block(D, 2 * ROWS), row_block(D, 2 * ROWS), whole(vec.shape)] + [ANY] * len(parts),
        out_specs=[row_block(D, 2 * ROWS), row_block(1, 2 * ROWS), row_block(D, 2 * ROWS), ANY],
        out_shape=[S((t, D), f32), S((t, 1), f32), S((t, D), low), S(shape, low)],
        scratch_shapes=scratch_for(shape),
        name="close",
        **params(2 * t * D * D, 10 * t * D + 4 * D * D, room=60),
    )(x, c, vec, *parts)
    return hat, inv, n, full.reshape(1, D, D)


def open_back_body(dres_ref, dh_ref, wi_ref, hat_ref, inv_ref, wo_ref, vec_ref, before_ref, dr_ref, da_ref, dc_ref, sums_ref):
    @pl.when(pl.program_id(0) == 0)
    def _():
        sums_ref[...] = before_ref[...]

    grads = [dres_ref[r, :] + nt(dh_ref[r, :], wi_ref[...]) for r in halves(dres_ref)]
    for r, dn in zip(halves(dres_ref), grads):
        hat = hat_ref[r, :]
        dres = layer_norm_back(dn, vec_ref[G_ATTN : G_ATTN + 1].astype(f32), hat, inv_ref[r, :])
        dr_ref[r, :] = dres
        dao = dres.astype(low)
        da_ref[r, :] = dao
        dc_ref[r, :] = nt(dao, wo_ref[0]).astype(low)
        sums_ref[B_OUTPUT : B_OUTPUT + 1] += jnp.sum(dao.astype(f32), axis=0, keepdims=True)
        sums_ref[G_ATTN : G_ATTN + 1] += jnp.sum(dn * hat, axis=0, keepdims=True)
        sums_ref[S_ATTN : S_ATTN + 1] += jnp.sum(dn, axis=0, keepdims=True)


def open_back(dres, dh, wi, hat, inv, full, vec, sums):
    t = dres.shape[0]
    return pl.pallas_call(
        open_back_body,
        grid=(t // (2 * ROWS),),
        in_specs=[row_block(D, 2 * ROWS), row_block(FF, 2 * ROWS), whole(wi.shape), row_block(D, 2 * ROWS), row_block(1, 2 * ROWS), mat_of(0), whole(vec.shape), whole((16, D))],
        out_specs=[row_block(D, 2 * ROWS)] * 3 + [whole((16, D))],
        out_shape=[S((t, D), f32), S((t, D), low), S((t, D), low), S((16, D), f32)],
        name="open_back",
        **params(10 * t * D * D, 20 * t * D + 10 * D * D, room=60),
    )(dres, dh, wi, hat, inv, full, vec, sums)


def device_rows(table):
    rows = 8 * CUBE
    row, lane = (lax.broadcasted_iota(jnp.int32, (rows, D), axis) for axis in range(2))
    out = []
    for values, r in (
        (jnp.concatenate([table[:8]] * CUBE, axis=0), D // CUBE),
        (jnp.concatenate([jnp.broadcast_to(table[B_INNER + j : B_INNER + j + 1], (rows * D // FF, D)) for j in range(FF // D)], axis=0), FF // CUBE),
    ):
        own = jnp.where(lane // r == (row // 8) % (D // r), values, 0.0).astype(low)
        at, to = (lax.broadcasted_iota(jnp.int32, (D, WIDE // 2), axis) for axis in range(2))
        out.append(nn(own, jnp.where(at % r == to, 1.0, 0.0).astype(low)))
    return jnp.concatenate(out, axis=1)


def heads_back_body(cube, q_ref, k_ref, v_ref, dc_ref, p_ref, x_ref, before_ref, c_ref, da_ref, *refs):
    dq_ref, dk_ref, dv_ref, *shares = refs[:-1]
    table_ref = refs[-1]
    step = pl.program_id(0)
    masks, masks32 = head_masks(low), head_masks(f32)

    def sentence(s):
        rows = pl.ds(pl.multiple_of(s * LEN, LEN), LEN)
        q, k, v, dc, p = q_ref[rows, :], k_ref[rows, :], v_ref[rows, :], dc_ref[rows, :], p_ref[0, rows, :]
        dcs = stacked(dc, masks)
        dp = nt(v, dcs)
        dv_ref[rows, :] = nn(p.astype(low), dcs).astype(low)
        ds = (p * (dp - jnp.sum(p * dp, axis=0, keepdims=True))).astype(low)
        dk_ref[rows, :] = (nn(ds, stacked(q, masks)) * HEAD_DIM ** (-0.5)).astype(low)
        dq_ref[rows, :] = (unstacked(tn(ds, k), masks32) * HEAD_DIM ** (-0.5)).astype(low)

    @pl.when(step == 0)
    def _():
        table_ref[...] = before_ref[...]

    pl.loop(0, q_ref.shape[0] // LEN, unroll=BACK_UNROLL)(sentence)
    cols = pl.ds(pl.multiple_of(step * WIDE, WIDE), WIDE)
    table_ref[B_QUERY : B_QUERY + 1, cols] = jnp.sum(dq_ref[...].astype(f32), axis=0, keepdims=True)
    table_ref[B_VALUE : B_VALUE + 1, cols] = jnp.sum(dv_ref[...].astype(f32), axis=0, keepdims=True)
    for m, (rows, grad) in enumerate(((x_ref, dq_ref), (x_ref, dk_ref), (x_ref, dv_ref), (c_ref, da_ref))):
        full = tn(rows[...], grad[...])
        if cube:
            full = full.reshape(4, 2, 2, 2, 24, WIDE)

            def put(ref, p, q, value, m=m):
                ref[:, p, q, 24 * m : 24 * (m + 1)] = value.astype(ref.dtype)

            write_shares(lambda y, x, c: full[:, y, x, c], *shares, put)
        else:
            shares[1][m] = full
    if cube:

        def put_rows(ref, p, q, value):
            ref[:, p, q, 96:] = value.astype(ref.dtype)

        @pl.when(step < GROUPS - 1)
        def _():
            write_shares(lambda y, x, c: jnp.zeros((4, 8, WIDE), f32), *shares, put_rows)

        @pl.when(step == GROUPS - 1)
        def _():
            values = device_rows(table_ref[...]).reshape(4, 2, 2, 2, 8, WIDE)
            write_shares(lambda y, x, c: values[:, y, x, c], *shares, put_rows)
    else:
        shares[0][...] = table_ref[...]


BACK_UNROLL = 16


def heads_back(q, k, v, dc, p, x, sums, c, da, cube):
    t = q.shape[0]
    col = pl.BlockSpec((t, WIDE), lambda i: (0, i))
    if cube:
        spec = pl.BlockSpec((4, 2, 2, 104, WIDE), lambda i: (0, 0, 0, 0, i))
        shape = (4, 2, 2, 104, D)
        specs, shapes = [spec] * 2, [S(shape, KEEP), S(shape, low)]
    else:
        specs = [whole((16, D)), pl.BlockSpec((4, D, WIDE), lambda i: (0, 0, i))]
        shapes = [S((16, D), f32), S((4, D, D), f32)]
    return pl.pallas_call(
        lambda *refs: heads_back_body(cube, *refs),
        grid=(GROUPS,),
        in_specs=[col] * 4
        + [pl.BlockSpec((1, t, WIDE), lambda i: (i, 0, 0)), whole((t, D)), whole((16, D)), whole((t, D)), col],
        out_specs=[col] * 3 + specs,
        out_shape=[S((t, D), low)] * 3 + shapes,
        scratch_shapes=[pltpu.VMEM((16, D), f32)],
        name="heads_back",
        **params(t * D * 24000, t * D * 20, room=60),
    )(q, k, v, dc, p, x, sums, c, da)


def gelu_parts(h):
    d = 1.0 + (0.3275911 * 0.7071067811865476) * jnp.abs(h)
    t = pl.reciprocal(d, approx=True)
    t = t * (2.0 - d * t)
    poly = t * (0.127414796 + t * (-0.142248368 + t * (0.7107068705 + t * (-0.7265760135 + t * 0.5307027145))))
    bell = jnp.exp(-0.5 * (h * h))
    tail = poly * bell
    cdf = jnp.where(h >= 0, 1.0 - tail, tail)
    return h * cdf, cdf + h * (bell * 0.3989422804014327)


def inner_body(cube, n_ref, vec_ref, *refs):
    parts, (a_ref, gp_ref, full_ref, w_ref, sems, out_sem) = refs[:-6], refs[-6:]
    onward = assemble(cube, parts, w_ref, full_ref, sems, out_sem)
    n = n_ref[...]
    w = w_ref.reshape(D, FF) if cube else w_ref
    for j in range(FF // BLOCK):
        cols = pl.ds(j * BLOCK, BLOCK)
        h = nn(n, w[:, cols]) + vec_ref[B_INNER + j : B_INNER + j + 1].astype(f32)
        act, slope = gelu_parts(h)
        a_ref[:, cols] = act.astype(low)
        gp_ref[:, cols] = slope.astype(low)

    @pl.when(pl.program_id(0) == pl.num_programs(0) - 1)
    def _():
        onward.wait()


def inner(n, vec, parts, cube):
    t = n.shape[0]
    shape = (4, 2, 2, 2, 24, FF) if cube else (D, FF)
    act, slope, full = pl.pallas_call(
        lambda *refs: inner_body(cube, *refs),
        grid=(t // ROWS,),
        in_specs=[row_block(D), whole(vec.shape)] + [ANY] * len(parts),
        out_specs=[row_block(FF), row_block(FF), ANY],
        out_shape=[S((t, FF), low), S((t, FF), low), S(shape, low)],
        scratch_shapes=[pltpu.VMEM(shape, low), pltpu.SemaphoreType.DMA((4,)), pltpu.SemaphoreType.DMA],
        name="inner",
        **params(6 * t * D * FF, 2 * t * D + 4 * t * FF + 4 * D * FF, 2 * t * FF, room=60),
    )(n, vec, *parts)
    return act, slope, full.reshape(D, FF)


def outer_body(cube, a_ref, hat_ref, vec_ref, *refs):
    parts = refs[:-9]
    out_ref, hat2_ref, inv_ref, cls_ref, unit_ref, full_ref, w_ref, sems, out_sem = refs[-9:]
    onward = assemble(cube, parts, w_ref, full_ref, sems, out_sem)
    step = pl.program_id(0)
    w = w_ref.reshape(FF, D) if cube else w_ref
    branch = nn(a_ref[...], w[...]) + vec_ref[B_OUTER : B_OUTER + 1].astype(f32)
    normed = hat_ref[...] * vec_ref[G_ATTN : G_ATTN + 1].astype(f32) + vec_ref[S_ATTN : S_ATTN + 1].astype(f32)
    hat, inv = layer_norm(normed + branch)
    hat2_ref[...] = hat
    inv_ref[...] = inv
    rows = hat * vec_ref[G_FFN : G_FFN + 1].astype(f32) + vec_ref[S_FFN : S_FFN + 1].astype(f32)
    out_ref[...] = rows.astype(low)
    pairs = rows.shape[0] // LEN // 2
    for s in range(pairs):
        at = pl.ds(step * pairs + s, 1)
        for side in range(2):
            cols = pl.ds(side * D, D)
            cls = rows[LEN * (2 * s + side) : LEN * (2 * s + side) + 1]
            cls_ref[at, cols] = cls

    @pl.when(step == pl.num_programs(0) - 1)
    def _():
        for side in range(2):
            cls = cls_ref[:, side * D : (side + 1) * D]
            unit = cls * lax.rsqrt(jnp.sum(cls * cls, axis=-1, keepdims=True) + pool_eps)
            unit_ref[:, side * D : (side + 1) * D] = unit.astype(low)
        onward.wait()


def outer(act, hat, vec, parts, cube):
    t = hat.shape[0]
    shape = (4, 2, 2, 2, 96, D) if cube else (FF, D)
    pairs = t // LEN // 2
    once = pl.BlockSpec((pairs, 2 * D), lambda i: (0, 0))
    *outs, full = pl.pallas_call(
        lambda *refs: outer_body(cube, *refs),
        grid=(t // ROWS,),
        in_specs=[row_block(FF), row_block(D), whole(vec.shape)] + [ANY] * len(parts),
        out_specs=[row_block(D), row_block(D), row_block(1), once, once, ANY],
        out_shape=[S((t, D), low), S((t, D), f32), S((t, 1), f32), S((pairs, 2 * D), f32), S((pairs, 2 * D), low), S(shape, low)],
        scratch_shapes=[pltpu.VMEM(shape, low), pltpu.SemaphoreType.DMA((4,)), pltpu.SemaphoreType.DMA],
        name="outer",
        **params(2 * t * D * FF, 10 * t * D + 2 * t * FF + 4 * D * FF, room=60),
    )(act, hat, vec, *parts)
    return *outs, full.reshape(FF, D)


def write_shares(full, keep_ref, away_ref, put):
    core = lax.axis_index(AXIS) & 1

    def write(zero, one):
        for y in range(2):
            for x in range(2):
                put(zero, x, y, full(y, x, 0))
                put(one, y, x, full(y, x, 1))

    @pl.when(core == 0)
    def _():
        write(keep_ref, away_ref)

    @pl.when(core == 1)
    def _():
        write(away_ref, keep_ref)


def outer_back_body(cube, cot_ref, dc_ref, hat2_ref, inv2_ref, a_ref, vec_ref, dres_ref, dbr_ref, sums_ref, *refs):
    j = pl.program_id(0)

    def write(dw):
        if cube:
            dw = dw.reshape(2, 2, 2, 96, D)

            def put(ref, p, q, value):
                ref[0, p, q] = value.astype(ref.dtype)

            write_shares(lambda y, x, c: dw[y, x, c], *refs, put)
        else:
            refs[0][...] = dw

    @pl.when(j == 0)
    def _():
        dw = jnp.zeros((BLOCK, D), f32)
        dgain = jnp.zeros((1, D), f32)
        dshift = jnp.zeros((1, D), f32)
        dbias = jnp.zeros((1, D), f32)
        at = lax.broadcasted_iota(jnp.int32, (ROWS, D), 0)
        for b in range(cot_ref.shape[0] // ROWS):
            rows = pl.ds(b * ROWS, ROWS)
            d = cot_ref[rows, :].astype(f32)
            hat = hat2_ref[rows, :]
            for s in range(ROWS // LEN):
                whose = b * (ROWS // LEN) + s
                extra = dc_ref[whose // 2 : whose // 2 + 1, (whose % 2) * D : (whose % 2 + 1) * D]
                d += jnp.where(at == LEN * s, extra, 0.0)
            dgain += jnp.sum(d * hat, axis=0, keepdims=True)
            dshift += jnp.sum(d, axis=0, keepdims=True)
            dres = layer_norm_back(d, vec_ref[G_FFN : G_FFN + 1].astype(f32), hat, inv2_ref[rows, :])
            dres_ref[rows, :] = dres
            dbr = dres.astype(low)
            dbr_ref[rows, :] = dbr
            dbias += jnp.sum(dbr.astype(f32), axis=0, keepdims=True)
            dw += tn(a_ref[rows, :], dbr)
        write(dw)
        sums_ref[...] = jnp.zeros_like(sums_ref)
        sums_ref[B_OUTER : B_OUTER + 1] = dbias
        sums_ref[G_FFN : G_FFN + 1] = dgain
        sums_ref[S_FFN : S_FFN + 1] = dshift

    @pl.when(j > 0)
    def _():
        write(tn(a_ref[...], dbr_ref[...]))


def outer_back(cot, dc, hat2, inv2, a, vec, cube):
    t = cot.shape[0]
    if cube:
        spec = pl.BlockSpec((1, 2, 2, 96, D), lambda j: (j, 0, 0, 0, 0))
        specs, shapes = [spec] * 2, [S((4, 2, 2, 96, D), KEEP), S((4, 2, 2, 96, D), low)]
    else:
        specs, shapes = [pl.BlockSpec((BLOCK, D), lambda j: (j, 0))], [S((FF, D), f32)]
    return pl.pallas_call(
        lambda *refs: outer_back_body(cube, *refs),
        grid=(FF // BLOCK,),
        in_specs=[whole((t, D)), whole(dc.shape), whole((t, D)), whole((t, 1)), pl.BlockSpec((t, BLOCK), lambda j: (0, j)),
                  whole(vec.shape)],
        out_specs=[whole((t, D)), whole((t, D)), whole((16, D))] + specs,
        out_shape=[S((t, D), f32), S((t, D), low), S((16, D), f32)] + shapes,
        name="outer_back",
        **params(4 * t * D * FF, 14 * t * D + 2 * t * FF + 8 * D * FF, room=60),
    )(cot, dc, hat2, inv2, a, vec)


def inner_back_body(cube, dbr_ref, n_ref, gp_ref, wo_ref, before_ref, dh_ref, sums_ref, *refs):
    @pl.when(pl.program_id(0) == 0)
    def _():
        sums_ref[...] = before_ref[...]

    dh = (gp_ref[...].astype(f32) * nt(dbr_ref[...], wo_ref[...])).astype(low)
    dh_ref[...] = dh
    sums_ref[pl.ds(B_INNER + pl.program_id(0), 1), :] = jnp.sum(dh.astype(f32), axis=0, keepdims=True)
    dw = tn(n_ref[...], dh)
    if cube:
        dw = dw.reshape(4, 2, 2, 2, 24, BLOCK)

        def put(ref, p, q, value):
            ref[:, p, q] = value.astype(ref.dtype)

        write_shares(lambda y, x, c: dw[:, y, x, c], *refs, put)
    else:
        refs[0][...] = dw


def inner_back(dbr, n, gp, wo, sums, cube):
    t = n.shape[0]
    fblk = pl.BlockSpec((t, BLOCK), lambda j: (0, j))
    if cube:
        spec = pl.BlockSpec((4, 2, 2, 24, BLOCK), lambda j: (0, 0, 0, 0, j))
        specs, shapes = [spec] * 2, [S((4, 2, 2, 24, FF), KEEP), S((4, 2, 2, 24, FF), low)]
    else:
        specs, shapes = [pl.BlockSpec((D, BLOCK), lambda j: (0, j))], [S((D, FF), f32)]
    return pl.pallas_call(
        lambda *refs: inner_back_body(cube, *refs),
        grid=(FF // BLOCK,),
        in_specs=[whole((t, D)), whole((t, D)), fblk, pl.BlockSpec((BLOCK, D), lambda j: (j, 0)), whole((16, D))],
        out_specs=[fblk, whole((16, D))] + specs,
        out_shape=[S((t, FF), low), S((16, D), f32)] + shapes,
        name="inner_back",
        **params(4 * t * D * FF, 4 * t * D + 4 * t * FF + 8 * D * FF, room=60),
    )(dbr, n, gp, wo, sums)


KEEP = low


def token_grad_body(dr_ref, dq_ref, dk_ref, dv_ref, wq_ref, wk_ref, wv_ref, o_ref):
    o_ref[...] = (
        dr_ref[...] + nt(dq_ref[...], wq_ref[0]) + nt(dk_ref[...], wk_ref[0]) + nt(dv_ref[...], wv_ref[0])
    )


def token_grad(dr, dq, dk, dv, full):
    t = dr.shape[0]

    return pl.pallas_call(
        token_grad_body,
        grid=(t // ROWS,),
        in_specs=[row_block(D)] * 4 + [mat_of(0), mat_of(1), mat_of(2)],
        out_specs=row_block(D),
        out_shape=S((t, D), f32),
        name="token_grad",
        **params(6 * t * D * D, 14 * t * D + 6 * D * D, room=60),
    )(dr, dq, dk, dv, full, full, full)


def loss_body(units_ref, codes_ref, cls_ref, loss_ref, dc_ref, table_ref, ds_ref):
    sources, targets = units_ref[:, :D], units_ref[:, D:]
    pairs, own = units_ref.shape[0], cls_ref.shape[0]
    codes = codes_ref[CODES : CODES + 2, :pairs].astype(f32)
    partner = (codes[0:1] + 64.0 * codes[1:2]).astype(jnp.int32)
    matched = lax.broadcasted_iota(jnp.int32, (pairs, pairs), 0) == partner
    sims = nt(targets, sources) * sim_scale - jnp.where(matched, sim_scale * sim_margin, 0.0)
    row_top = jnp.max(sims, axis=0, keepdims=True)
    row_lse = row_top + jnp.log(jnp.sum(jnp.exp(sims - row_top), axis=0, keepdims=True))
    col_top = jnp.max(sims, axis=1, keepdims=True)
    col_lse = col_top + jnp.log(jnp.sum(jnp.exp(sims - col_top), axis=1, keepdims=True))
    total = (
        jnp.sum(row_lse, axis=1, keepdims=True)
        + jnp.sum(col_lse, axis=0, keepdims=True)
        - 2.0 * jnp.sum(jnp.sum(jnp.where(matched, sims, 0.0), axis=1, keepdims=True), axis=0, keepdims=True)
    )
    loss_ref[...] = jnp.broadcast_to(total * (0.5 / pairs), loss_ref.shape)
    d_sims = 0.5 * (jnp.exp(sims - row_lse) + jnp.exp(sims - col_lse)) - jnp.where(matched, 1.0, 0.0)
    d_low = (d_sims * sim_scale).astype(low)
    table_ref[...] = nn(d_low, sources)
    ds_ref[...] = tn(d_low, targets)
    mine = pl.ds(pl.multiple_of(lax.axis_index(AXIS) * own, own), own)
    for side, ref in enumerate((ds_ref, table_ref)):
        cols = pl.ds(side * D, D)
        cls, du = cls_ref[:, cols], ref[mine, :]
        inv = lax.rsqrt(jnp.sum(cls * cls, axis=-1, keepdims=True) + pool_eps)
        dc_ref[:, cols] = inv * du - cls * (inv * inv * inv * jnp.sum(du * cls, axis=-1, keepdims=True))


def pair_loss(units, vec, cls):
    pairs, own = units.shape[0], cls.shape[0]
    loss, dc = pl.pallas_call(
        loss_body,
        in_specs=[whole(units.shape), whole(vec.shape), whole(cls.shape)],
        out_specs=[whole((8, 128)), whole(cls.shape)],
        out_shape=[S((8, 128), f32), S(cls.shape, f32)],
        scratch_shapes=[pltpu.VMEM((pairs, D), f32), pltpu.VMEM((pairs, D), f32)],
        grid=(1,),
        name="pair_loss",
        **params(6 * pairs * pairs * D, 4 * pairs * D, 4 * pairs * pairs, room=60),
    )(units, vec, cls)
    return loss[0, 0], dc


CORE = [(i, i ^ 1) for i in range(CUBE)]
FAR_Z = [(i, i ^ 16) for i in range(CUBE)]
NEAR_Z = [(i, i ^ 8) for i in range(CUBE)]
FIRST = [(i, i ^ (4 if i & 1 else 2)) for i in range(CUBE)]
SECOND = [(i, i ^ (2 if i & 1 else 4)) for i in range(CUBE)]
ROUTES = (CORE, FIRST, SECOND, NEAR_Z, FAR_Z)


class Place:
    def __init__(self):
        self.me = lax.axis_index(AXIS)
        self.core = self.me & 1
        x, y = (self.me >> 1) & 1, (self.me >> 2) & 1
        self.near_z, self.far_z = (self.me >> 3) & 1, (self.me >> 4) & 1
        self.first = jnp.where(self.core == 0, x, y)
        self.second = jnp.where(self.core == 0, y, x)
        self.bits = [b.reshape(1) for b in (self.first, self.second, self.near_z, self.far_z)]


def join(own, other, axis, bit):
    shape = own.shape[:axis] + (2,) + own.shape[axis:]
    where = lax.broadcasted_iota(jnp.int32, shape, axis)
    return jnp.where(where == bit, jnp.expand_dims(own, axis), jnp.expand_dims(other, axis))


def pick(field, axis, bit):
    return lax.dynamic_index_in_dim(field, bit, axis, keepdims=False)


def send(field, route):
    return lax.ppermute(field, AXIS, route)


def spread(block, place):
    block = join(block, send(block, FAR_Z), 0, place.far_z)
    block = join(block, send(block, NEAR_Z), 1, place.near_z)
    return join(block, send(block, FIRST), 2, place.first)


def gather_blocks(block, place):
    near = spread(block, place)
    block = join(near, send(near, SECOND), 3, place.second)
    other = send(block, CORE)
    zero = jnp.where(place.core == 0, block, other)
    one = jnp.where(place.core == 0, other, block)
    return jnp.stack([jnp.swapaxes(zero, 2, 3), one], axis=4).reshape(-1, block.shape[-1])


def together(*values):
    return lax.optimization_barrier(values)


class Reduction:
    def __init__(self, shares, place, early_z=False):
        keep, self.away = shares
        self.terms = [keep.reshape(2, 2, *keep.shape[1:])]
        self.left = [(2, place.first), (2, place.second), (1, place.near_z), (0, place.far_z)]
        if early_z:
            self.left = [(1, place.near_z), (1, place.first), (1, place.second), (0, place.far_z)]
        self.came = None

    def start(self, route):
        self.came, self.away = send(self.away, route), None

    def settle(self):
        self.terms.append(self.came.reshape(self.terms[0].shape))
        axis, bit = self.left.pop(0)
        self.away = sum(pick(term, axis, 1 - bit).astype(f32) for term in self.terms).astype(low)
        self.terms = [pick(term, axis, bit) for term in self.terms]

    def total(self):
        return sum(term.astype(f32) for term in (*self.terms, self.came))


def arrive(sums, *values):
    done = together(*values, *[s.came for s in sums])
    for s, came in zip(sums, done[len(values) :]):
        s.came = came
    return done[: len(values)]


def spread_rows(rows, at, count):
    r = rows.shape[1]
    lane = lax.broadcasted_iota(jnp.int32, (r, D), 1)
    copies = nn(rows, jnp.where(lane % r == lax.broadcasted_iota(jnp.int32, (r, D), 0), 1.0, 0.0).astype(low))
    lane = lax.broadcasted_iota(jnp.int32, (count, D), 1)
    row = lax.broadcasted_iota(jnp.int32, (count, D), 0)
    return copies, lane // r, row


def vector_table(vectors, partners, place):
    *small, inner = vectors
    copies, lane, _ = spread_rows(jnp.stack(small), place.me, len(small))
    table = [jnp.where(lane == place.me, copies, 0.0)]
    fold = D // inner.shape[0]
    copies, lane, row = spread_rows(inner[None], place.me, FF // D)
    table.append(jnp.where((row == place.me // fold) & (lane == place.me % fold), copies, 0.0))
    codes = jnp.stack([partners % 64, partners // 64]).astype(low)
    copies, lane, _ = spread_rows(codes, place.me, 2)
    table.append(jnp.where(lane == place.me, copies, 0.0))
    table.append(jnp.zeros((2, D), f32))
    return jnp.concatenate(table, axis=0).astype(low)


def pack_body(*refs):
    *mats, out = refs
    r = mats[0].shape[0]
    for i, mat in enumerate(mats):
        out[i * r : (i + 1) * r, :] = mat[...]


def pack(*mats):
    r, n = mats[0].shape
    return pl.pallas_call(pack_body, out_shape=S((len(mats) * r, n), low), name="pack")(*mats)


def plain_loss(units, partners, cls):
    sources, targets = units[:, :D], units[:, D:]
    npairs, own = units.shape[0], cls.shape[0]
    sims = nt(sources, targets) * sim_scale
    matched = partners[:, None] == jnp.arange(npairs, dtype=jnp.int32)[None, :]
    sims = sims - jnp.where(matched, sim_scale * sim_margin, 0.0)
    row_top = jnp.max(sims, axis=1, keepdims=True)
    row_lse = row_top + jnp.log(jnp.sum(jnp.exp(sims - row_top), axis=1, keepdims=True))
    col_top = jnp.max(sims, axis=0, keepdims=True)
    col_lse = col_top + jnp.log(jnp.sum(jnp.exp(sims - col_top), axis=0, keepdims=True))
    positive = jnp.sum(jnp.where(matched, sims, 0.0))
    loss = (jnp.sum(row_lse) + jnp.sum(col_lse) - 2.0 * positive) / (2.0 * npairs)
    d_sims = 0.5 * (jnp.exp(sims - row_lse) + jnp.exp(sims - col_lse)) - jnp.where(matched, 1.0, 0.0)
    d_low = (d_sims * sim_scale).astype(low)
    first = lax.axis_index(AXIS) * own
    du = [
        nn(lax.dynamic_slice_in_dim(d_low, first, own, 0), targets),
        tn(lax.dynamic_slice_in_dim(d_low, first, own, 1), sources),
    ]
    dc = []
    for side in range(2):
        c = cls[:, side * D : (side + 1) * D]
        inv = lax.rsqrt(jnp.sum(c * c, axis=-1, keepdims=True) + pool_eps)
        dc.append(inv * du[side] - c * (inv * inv * inv * jnp.sum(du[side] * c, axis=-1, keepdims=True)))
    return loss, jnp.concatenate(dc, axis=1)


def every(v):
    return lax.all_gather(v, AXIS, axis=0, tiled=True)


def scatter(v):
    return lax.psum_scatter(v, AXIS, scatter_dimension=0, tiled=True)


def local(
    tokens,
    lengths,
    partners,
    out_cotangent,
    w_query,
    w_key,
    w_value,
    w_output,
    b_query,
    b_value,
    b_output,
    gain_attn,
    shift_attn,
    w_inner,
    b_inner,
    w_outer,
    b_outer,
    gain_ffn,
    shift_ffn,
):
    cube = lax.axis_size(AXIS) == CUBE
    count = tokens.shape[0]
    x = tokens.reshape(count * LEN, D)
    vectors = (b_query, b_value, b_output, gain_attn, shift_attn, b_outer, gain_ffn, shift_ffn, b_inner)
    blocks = count * LEN // ROWS
    lower, higher = blocks // 2, blocks - blocks // 2
    if cube:
        place = Place()
        qkv = pack(w_query, w_key, w_value)
        vec = vector_table(vectors, partners, place)
        qkv = join(qkv, send(qkv, FAR_Z), 0, place.far_z)
        vec = vec + send(vec, FAR_Z)
        qkv, vec, w_output = together(qkv, vec, w_output)
        qkv = join(qkv, send(qkv, NEAR_Z), 1, place.near_z)
        vec = vec + send(vec, NEAR_Z)
        prj = join(w_output, send(w_output, FAR_Z), 0, place.far_z)
        qkv, vec, prj, w_inner = together(qkv, vec, prj, w_inner)
        qkv = join(qkv, send(qkv, FIRST), 2, place.first).reshape(4, 2, 72, D)
        vec = vec + send(vec, FIRST)
        prj = join(prj, send(prj, NEAR_Z), 1, place.near_z)
        inn = join(w_inner, send(w_inner, FAR_Z), 0, place.far_z)
        qkv, vec, prj, inn = together(qkv, vec, prj, inn)
        far = send(qkv, SECOND)
        other = send(qkv, CORE)
        vec = vec + send(vec, SECOND)
        prj = join(prj, send(prj, FIRST), 2, place.first).reshape(4, 2, 24, D)
        inn = join(inn, send(inn, NEAR_Z), 1, place.near_z)
        far, other, vec, prj, inn = together(far, other, vec, prj, inn)
        qkv_parts = (qkv, far, other, send(far, CORE))
        vec = vec + send(vec, CORE)
        qkv_parts, vec, prj, inn, w_outer = together(qkv_parts, vec, prj, inn, w_outer)
        inn = join(inn, send(inn, FIRST), 2, place.first).reshape(4, 2, 24, FF)
        prj_far = send(prj, SECOND)
        out = join(w_outer, send(w_outer, FAR_Z), 0, place.far_z)
        queries, keys, values, full = project(x, vec, qkv_parts, cube)
        queries, prj_far, inn, out = together(queries, prj_far, inn, out)
        inn_far = send(inn, SECOND)
        out = join(out, send(out, NEAR_Z), 1, place.near_z)
        prj_parts = (prj, prj_far, send(prj, CORE), send(prj_far, CORE))
        probs, context = attend(lengths, queries, keys, values, 0, blocks)
        context, inn, inn_far, out, prj_parts = together(context, inn, inn_far, out, prj_parts)
        inn_parts = (inn, inn_far, send(inn, CORE), send(inn_far, CORE))
        out = join(out, send(out, FIRST), 2, place.first).reshape(4, 2, 96, D)
        hat1, inv1, normed, output_mat = close(x, context, vec, prj_parts, cube)
        normed, inn_parts, out = together(normed, inn_parts, out)
        out_far = send(out, SECOND)
        other = send(out, CORE)
        act, slope, inner_mat = inner(normed, vec, inn_parts, cube)
        act, out_far, other = together(act, out_far, other)
        out_parts = (out, out_far, other, send(out_far, CORE))
        block_out, hat2, inv2, cls, unit, outer_mat = outer(act, hat1, vec, out_parts, cube)
        loss, d_cls = pair_loss(gather_blocks(unit, place), vec, cls)
        dres, dbr, sums, *shares = outer_back(
            out_cotangent.reshape(count * LEN, D), d_cls, hat2, inv2, act, vec, cube
        )
        o = Reduction(shares, place)
        dbr, o.away = together(dbr, o.away)
        o.start(CORE)
        dh, sums, *shares = inner_back(dbr, normed, slope, outer_mat, sums, cube)
        i = Reduction(shares, place, early_z=True)
        dh, i.away = arrive([o], dh, i.away)
        i.start(CORE)
        o.settle()
        o.start(FIRST)
        dh, dres = together(dh, dres)
        d_resid, d_attn, d_context, sums = open_back(dres, dh, inner_mat, hat1, inv1, output_mat, vec, sums)
        (d_context,) = arrive([o, i], d_context)
        o.settle()
        o.start(SECOND)
        i.settle()
        i.start(NEAR_Z)
        d_queries, d_keys, d_values, *shares = heads_back(
            queries, keys, values, d_context, probs, x, sums, context, d_attn, cube
        )
        a = Reduction(shares, place)
        d_queries, a.away = arrive([o, i], d_queries, a.away)
        a.start(CORE)
        o.settle()
        i.settle()
        o.away, i.away = arrive([a], o.away, i.away)
        a.settle()
        a.start(FIRST)
        o.start(NEAR_Z)
        i.start(FIRST)
        grad_rows = token_grad(d_resid, d_queries, d_keys, d_values, full)
        (grad_rows,) = arrive([o, i, a], grad_rows)
        a.settle()
        a.start(SECOND)
        o.settle()
        o.start(FAR_Z)
        i.settle()
        i.start(SECOND)
        arrive([i, a])
        a.settle()
        a.start(NEAR_Z)
        i.settle()
        i.start(FAR_Z)
        grad_w_outer = o.total()
        (grad_w_outer,) = arrive([a], grad_w_outer)
        a.settle()
        a.start(FAR_Z)
        grad_w_inner = i.total()
        g_attn = a.total()
        g_mats = [g_attn[24 * n : 24 * (n + 1)] for n in range(4)]
        small, inner_part = g_attn[96:, D - WIDE :], g_attn[96, D - WIDE // 2 :]
        grads = [small[n, : D // CUBE] for n in range(B_INNER)] + [inner_part[: FF // CUBE]]
    else:
        rows = [every(v).reshape(-1, D) for v in vectors]
        vec = jnp.concatenate(rows + [jnp.zeros((4, D), low)], axis=0)
        qkv_parts = (jnp.stack([every(w) for w in (w_query, w_key, w_value)]),)
        queries, keys, values, full = project(x, vec, qkv_parts, cube)
        probs, context = attend(lengths, queries, keys, values, 0, blocks)
        hat1, inv1, normed, output_mat = close(x, context, vec, (every(w_output),), cube)
        act, slope, inner_mat = inner(normed, vec, (every(w_inner),), cube)
        block_out, hat2, inv2, cls, unit, outer_mat = outer(act, hat1, vec, (every(w_outer),), cube)
        loss, d_cls = plain_loss(every(unit), every(partners), cls)
        dres, dbr, sums, d_outer = outer_back(
            out_cotangent.reshape(count * LEN, D), d_cls, hat2, inv2, act, vec, cube
        )
        dh, sums, d_inner = inner_back(dbr, normed, slope, outer_mat, sums, cube)
        d_resid, d_attn, d_context, sums = open_back(dres, dh, inner_mat, hat1, inv1, output_mat, vec, sums)
        d_queries, d_keys, d_values, sums, d_mats = heads_back(
            queries, keys, values, d_context, probs, x, sums, context, d_attn, cube
        )
        grad_rows = token_grad(d_resid, d_queries, d_keys, d_values, full)
        grad_w_outer, grad_w_inner = scatter(d_outer), scatter(d_inner)
        g_mats = [scatter(d_mats[n]) for n in range(4)]
        grads = [scatter(sums[n]) for n in range(B_INNER)] + [scatter(sums[B_INNER:CODES].reshape(-1))]
    (
        grad_b_query,
        grad_b_value,
        grad_b_output,
        grad_gain_attn,
        grad_shift_attn,
        grad_b_outer,
        grad_gain_ffn,
        grad_shift_ffn,
        grad_b_inner,
    ) = grads
    return (
        loss,
        block_out.reshape(count, LEN, D),
        grad_rows.reshape(count, LEN, D),
        g_mats[0],
        g_mats[1],
        g_mats[2],
        g_mats[3],
        grad_b_query,
        grad_b_value,
        grad_b_output,
        grad_gain_attn,
        grad_shift_attn,
        grad_w_inner,
        grad_b_inner,
        grad_w_outer,
        grad_b_outer,
        grad_gain_ffn,
        grad_shift_ffn,
    )


def solution(mesh):
    rows, cols = P(AXIS), P(AXIS, None)
    cube = P(AXIS, None, None)
    in_specs = (cube, rows, rows, cube) + (cols,) * 4 + (rows,) * 5 + (cols, rows, cols) + (rows,) * 3
    out_specs = (P(), cube, cube) + (cols,) * 4 + (rows,) * 5 + (cols, rows, cols) + (rows,) * 3
    return jax.shard_map(local, mesh=mesh, in_specs=in_specs, out_specs=out_specs, check_vma=False)
```

```python
import jax
import jax.numpy as jnp
from jax import lax
from jax.experimental import pallas as pl
from jax.experimental.pallas import tpu as pltpu
from jax.sharding import PartitionSpec as P

D = 768
HEADS = 12
HEAD_DIM = 64
LEN = 64
FF = 3072
QUAD = 4
WIDE = QUAD * HEAD_DIM
GROUPS = HEADS // QUAD
ROWS = 256
BLOCK = 768
AXIS = "fsdp"
CUBE = 32
norm_eps = 1e-12
pool_eps = 1e-06
sim_scale = 50.0
sim_margin = 0.3
f32, low = jnp.float32, jnp.bfloat16
S = jax.ShapeDtypeStruct

B_QUERY, B_VALUE, B_OUTPUT, G_ATTN, S_ATTN, B_OUTER, G_FFN, S_FFN, B_INNER = range(9)
CODES = B_INNER + FF // D


def nn(a, b):
    return lax.dot_general(a, b, (((1,), (0,)), ((), ())), preferred_element_type=f32)


def nt(a, b):
    return lax.dot_general(a, b, (((1,), (1,)), ((), ())), preferred_element_type=f32)


def tn(a, b):
    return lax.dot_general(a, b, (((0,), (0,)), ((), ())), preferred_element_type=f32)


def whole(shape):
    return pl.BlockSpec(shape, lambda *_: (0,) * len(shape), pipeline_mode=pl.Buffered(1))


def row_block(width, rows=ROWS):
    return pl.BlockSpec((rows, width), lambda i, *_: (i, 0))


def params(flops, nbytes, exps=0, room=60):
    return dict(
        compiler_params=pltpu.CompilerParams(vmem_limit_bytes=room << 20),
        cost_estimate=pl.CostEstimate(flops=int(flops), bytes_accessed=int(nbytes), transcendentals=int(exps)),
    )


ANY = pl.BlockSpec(memory_space=pl.ANY)


def part_copies(parts, target, sems, cut):
    me = lax.axis_index(AXIS)
    core, x, y = me & 1, (me >> 1) & 1, (me >> 2) & 1

    def start(zero, one):
        for i in range(2):
            pltpu.make_async_copy(cut(zero[i]), target.at[:, (y + i) & 1, :, 0], sems.at[2 * i]).start()
            pltpu.make_async_copy(cut(one[i]), target.at[:, :, (x + i) & 1, 1], sems.at[2 * i + 1]).start()

    @pl.when(core == 0)
    def _():
        start(parts[:2], parts[2:])

    @pl.when(core == 1)
    def _():
        start(parts[2:], parts[:2])


def part_waits(parts, target, sems, cut):
    for i in range(2):
        pltpu.make_async_copy(cut(parts[i]), target.at[:, i, :, 0], sems.at[2 * i]).wait()
        pltpu.make_async_copy(cut(parts[i]), target.at[:, :, i, 1], sems.at[2 * i + 1]).wait()


def everything(ref):
    return ref


def project_body(cube, count, biases, x_ref, vec_ref, *refs):
    outs = len(biases)
    parts, out_refs, (full_ref, w_ref, sems, out_sem) = refs[: -outs - 4], refs[-outs - 4 : -4], refs[-4:]
    step = pl.program_id(0)
    onward = pltpu.make_async_copy(w_ref, full_ref, out_sem)

    @pl.when(step == 0)
    def _():
        if cube:

            def cut(m):
                return lambda ref: ref.at[:, :, pl.ds(m * 24, 24), :]

            for m in range(count):
                part_copies(parts, w_ref.at[m], sems.at[m], cut(m))
            for m in range(count):
                part_waits(parts, w_ref.at[m], sems.at[m], cut(m))
        else:
            copy = pltpu.make_async_copy(parts[0], w_ref, sems.at[0, 0])
            copy.start()
            copy.wait()
        onward.start()

    x = x_ref[...]
    for m, (bias, out) in enumerate(zip(biases, out_refs)):
        product = nn(x, w_ref.at[m].reshape(D, D)[...] if cube else w_ref[m])
        if bias is not None:
            product += vec_ref[bias : bias + 1].astype(f32)
        out[...] = product.astype(low)

    @pl.when(step == pl.num_programs(0) - 1)
    def _():
        onward.wait()


def project(x, vec, parts, count, biases, cube):
    t = x.shape[0]
    shape = (count, 4, 2, 2, 2, 24, D) if cube else (count, D, D)
    outs = len(biases)
    *products, full = pl.pallas_call(
        lambda *refs: project_body(cube, count, biases, *refs),
        grid=(t // (2 * ROWS),),
        in_specs=[row_block(D, 2 * ROWS), whole(vec.shape)] + [ANY] * len(parts),
        out_specs=[row_block(D, 2 * ROWS)] * outs + [ANY],
        out_shape=[S((t, D), low)] * outs + [S(shape, low)],
        scratch_shapes=[pltpu.VMEM(shape, low), pltpu.SemaphoreType.DMA((count, 4)), pltpu.SemaphoreType.DMA],
        name="project",
        **params(2 * outs * t * D * D, 2 * (outs + 1) * t * D + 4 * count * D * D, room=60),
    )(x, vec, *parts)
    return *products, full.reshape(count, D, D)


def assemble(cube, parts, w_ref, full_ref, sems, out_sem):
    onward = pltpu.make_async_copy(w_ref, full_ref, out_sem)

    @pl.when(pl.program_id(0) == 0)
    def _():
        if cube:
            part_copies(parts, w_ref, sems, everything)
            part_waits(parts, w_ref, sems, everything)
        else:
            copy = pltpu.make_async_copy(parts[0], w_ref, sems.at[0])
            copy.start()
            copy.wait()
        onward.start()

    return onward


def scratch_for(shape):
    return [pltpu.VMEM(shape, low), pltpu.SemaphoreType.DMA((4,)), pltpu.SemaphoreType.DMA]


def head_masks(dtype):
    lane = lax.broadcasted_iota(jnp.int32, (1, WIDE), 1) // HEAD_DIM
    return [jnp.where(lane == h, 1.0, 0.0).astype(dtype) for h in range(QUAD)]


def stacked(rows, masks):
    return jnp.concatenate([rows * m for m in masks], axis=0)


def unstacked(full, masks):
    return sum(full[LEN * h : LEN * (h + 1)] * m for h, m in enumerate(masks))


def layer_norm(resid):
    centred = resid - jnp.mean(resid, axis=-1, keepdims=True)
    inv = lax.rsqrt(jnp.mean(centred * centred, axis=-1, keepdims=True) + norm_eps)
    return centred * inv, inv


def layer_norm_back(grad, gain, hat, inv):
    grad = grad * gain
    mean = jnp.mean(grad, axis=-1, keepdims=True)
    along = jnp.mean(grad * hat, axis=-1, keepdims=True)
    return (grad - mean - hat * along) * inv


def attend_body(len_ref, q_ref, k_ref, v_ref, p_ref, c_ref):
    masks, masks32 = head_masks(low), head_masks(f32)
    per = q_ref.shape[0] // LEN
    first = pl.program_id(0) * per
    key_at = lax.broadcasted_iota(jnp.int32, (LEN, WIDE), 0)

    def sentence(s):
        rows = pl.ds(pl.multiple_of(s * LEN, LEN), LEN)
        seen = key_at < len_ref[first + s]
        for g in range(GROUPS):
            cols = pl.ds(g * WIDE, WIDE)
            q, k, v = q_ref[rows, cols], k_ref[rows, cols], v_ref[rows, cols]
            scores = nt(k, stacked(q, masks)) * HEAD_DIM ** (-0.5)
            scores = jnp.where(seen, scores, -1e30)
            expd = jnp.exp(scores - jnp.max(scores, axis=0, keepdims=True))
            probs = expd * (1.0 / jnp.sum(expd, axis=0, keepdims=True))
            p_ref[g, rows, :] = probs
            c_ref[rows, cols] = unstacked(tn(probs.astype(low), v), masks32).astype(low)

    pl.loop(0, per, unroll=UNROLL)(sentence)


UNROLL = 8


def mat_of(m):
    return pl.BlockSpec((1, D, D), lambda *_: (m, 0, 0), pipeline_mode=pl.Buffered(1))


def attend(lengths, q, k, v):
    t = q.shape[0]
    rows = row_block(D, 2 * ROWS)
    return pl.pallas_call(
        attend_body,
        grid_spec=pltpu.PrefetchScalarGridSpec(
            num_scalar_prefetch=1,
            grid=(t // (2 * ROWS),),
            in_specs=[rows] * 3,
            out_specs=[pl.BlockSpec((GROUPS, 2 * ROWS, WIDE), lambda i, *_: (0, i, 0)), rows],
        ),
        out_shape=[S((GROUPS, t, WIDE), f32), S((t, D), low)],
        name="attend",
        **params(10 * t * D * D, 20 * t * D, t * D, room=60),
    )(lengths, q, k, v)


def halves(ref):
    return [slice(i * ROWS, (i + 1) * ROWS) for i in range(ref.shape[0] // ROWS)]


def close_body(x_ref, c_ref, w_ref, vec_ref, hat_ref, inv_ref, n_ref):
    w = w_ref[0]
    branches = [nn(c_ref[r, :], w) + vec_ref[B_OUTPUT : B_OUTPUT + 1].astype(f32) for r in halves(x_ref)]
    for r, branch in zip(halves(x_ref), branches):
        hat, inv = layer_norm(x_ref[r, :].astype(f32) + branch)
        hat_ref[r, :] = hat
        inv_ref[r, :] = inv
        n_ref[r, :] = (hat * vec_ref[G_ATTN : G_ATTN + 1].astype(f32) + vec_ref[S_ATTN : S_ATTN + 1].astype(f32)).astype(low)


def close(x, c, full, vec):
    t = x.shape[0]
    rows = row_block(D, 2 * ROWS)
    return pl.pallas_call(
        close_body,
        grid=(t // (2 * ROWS),),
        in_specs=[rows, rows, mat_of(1), whole(vec.shape)],
        out_specs=[rows, row_block(1, 2 * ROWS), rows],
        out_shape=[S((t, D), f32), S((t, 1), f32), S((t, D), low)],
        name="close",
        **params(2 * t * D * D, 10 * t * D + 2 * D * D, room=60),
    )(x, c, full, vec)


def open_back_body(dres_ref, dh_ref, wi_ref, hat_ref, inv_ref, wo_ref, vec_ref, before_ref, dr_ref, da_ref, dc_ref, sums_ref):
    @pl.when(pl.program_id(0) == 0)
    def _():
        sums_ref[...] = before_ref[...]

    grads = [dres_ref[r, :] + nt(dh_ref[r, :], wi_ref[...]) for r in halves(dres_ref)]
    for r, dn in zip(halves(dres_ref), grads):
        hat = hat_ref[r, :]
        dres = layer_norm_back(dn, vec_ref[G_ATTN : G_ATTN + 1].astype(f32), hat, inv_ref[r, :])
        dr_ref[r, :] = dres
        dao = dres.astype(low)
        da_ref[r, :] = dao
        dc_ref[r, :] = nt(dao, wo_ref[0]).astype(low)
        sums_ref[B_OUTPUT : B_OUTPUT + 1] += jnp.sum(dao.astype(f32), axis=0, keepdims=True)
        sums_ref[G_ATTN : G_ATTN + 1] += jnp.sum(dn * hat, axis=0, keepdims=True)
        sums_ref[S_ATTN : S_ATTN + 1] += jnp.sum(dn, axis=0, keepdims=True)


def open_back(dres, dh, wi, hat, inv, full, vec, sums):
    t = dres.shape[0]
    return pl.pallas_call(
        open_back_body,
        grid=(t // (2 * ROWS),),
        in_specs=[row_block(D, 2 * ROWS), row_block(FF, 2 * ROWS), whole(wi.shape), row_block(D, 2 * ROWS), row_block(1, 2 * ROWS), mat_of(1), whole(vec.shape), whole((16, D))],
        out_specs=[row_block(D, 2 * ROWS)] * 3 + [whole((16, D))],
        out_shape=[S((t, D), f32), S((t, D), low), S((t, D), low), S((16, D), f32)],
        name="open_back",
        **params(10 * t * D * D, 20 * t * D + 10 * D * D, room=60),
    )(dres, dh, wi, hat, inv, full, vec, sums)


def device_rows(table):
    rows = 8 * CUBE
    row, lane = (lax.broadcasted_iota(jnp.int32, (rows, D), axis) for axis in range(2))
    out = []
    for values, r in (
        (jnp.concatenate([table[:8]] * CUBE, axis=0), D // CUBE),
        (jnp.concatenate([jnp.broadcast_to(table[B_INNER + j : B_INNER + j + 1], (rows * D // FF, D)) for j in range(FF // D)], axis=0), FF // CUBE),
    ):
        own = jnp.where(lane // r == (row // 8) % (D // r), values, 0.0).astype(low)
        at, to = (lax.broadcasted_iota(jnp.int32, (D, WIDE // 2), axis) for axis in range(2))
        out.append(nn(own, jnp.where(at % r == to, 1.0, 0.0).astype(low)))
    return jnp.concatenate(out, axis=1)


def heads_back_body(cube, q_ref, k_ref, v_ref, dc_ref, p_ref, x_ref, before_ref, c_ref, da_ref, *refs):
    dq_ref, dk_ref, dv_ref, *shares = refs[:-1]
    table_ref = refs[-1]
    step = pl.program_id(0)
    masks, masks32 = head_masks(low), head_masks(f32)

    def sentence(s):
        rows = pl.ds(pl.multiple_of(s * LEN, LEN), LEN)
        q, k, v, dc, p = q_ref[rows, :], k_ref[rows, :], v_ref[rows, :], dc_ref[rows, :], p_ref[0, rows, :]
        dcs = stacked(dc, masks)
        dp = nt(v, dcs)
        dv_ref[rows, :] = nn(p.astype(low), dcs).astype(low)
        ds = (p * (dp - jnp.sum(p * dp, axis=0, keepdims=True))).astype(low)
        dk_ref[rows, :] = (nn(ds, stacked(q, masks)) * HEAD_DIM ** (-0.5)).astype(low)
        dq_ref[rows, :] = (unstacked(tn(ds, k), masks32) * HEAD_DIM ** (-0.5)).astype(low)

    @pl.when(step == 0)
    def _():
        table_ref[...] = before_ref[...]

    pl.loop(0, q_ref.shape[0] // LEN, unroll=BACK_UNROLL)(sentence)
    cols = pl.ds(pl.multiple_of(step * WIDE, WIDE), WIDE)
    table_ref[B_QUERY : B_QUERY + 1, cols] = jnp.sum(dq_ref[...].astype(f32), axis=0, keepdims=True)
    table_ref[B_VALUE : B_VALUE + 1, cols] = jnp.sum(dv_ref[...].astype(f32), axis=0, keepdims=True)
    for m, (rows, grad) in enumerate(((x_ref, dq_ref), (x_ref, dk_ref), (x_ref, dv_ref), (c_ref, da_ref))):
        full = tn(rows[...], grad[...])
        if cube:
            full = full.reshape(4, 2, 2, 2, 24, WIDE)

            def put(ref, p, q, value, m=m):
                ref[:, p, q, 24 * m : 24 * (m + 1)] = value.astype(ref.dtype)

            write_shares(lambda y, x, c: full[:, y, x, c], *shares, put)
        else:
            shares[1][m] = full
    if cube:

        def put_rows(ref, p, q, value):
            ref[:, p, q, 96:] = value.astype(ref.dtype)

        @pl.when(step < GROUPS - 1)
        def _():
            write_shares(lambda y, x, c: jnp.zeros((4, 8, WIDE), f32), *shares, put_rows)

        @pl.when(step == GROUPS - 1)
        def _():
            values = device_rows(table_ref[...]).reshape(4, 2, 2, 2, 8, WIDE)
            write_shares(lambda y, x, c: values[:, y, x, c], *shares, put_rows)
    else:
        shares[0][...] = table_ref[...]


BACK_UNROLL = 16


def heads_back(q, k, v, dc, p, x, sums, c, da, cube):
    t = q.shape[0]
    col = pl.BlockSpec((t, WIDE), lambda i: (0, i))
    if cube:
        spec = pl.BlockSpec((4, 2, 2, 104, WIDE), lambda i: (0, 0, 0, 0, i))
        shape = (4, 2, 2, 104, D)
        specs, shapes = [spec] * 2, [S(shape, KEEP), S(shape, low)]
    else:
        specs = [whole((16, D)), pl.BlockSpec((4, D, WIDE), lambda i: (0, 0, i))]
        shapes = [S((16, D), f32), S((4, D, D), f32)]
    return pl.pallas_call(
        lambda *refs: heads_back_body(cube, *refs),
        grid=(GROUPS,),
        in_specs=[col] * 4
        + [pl.BlockSpec((1, t, WIDE), lambda i: (i, 0, 0)), whole((t, D)), whole((16, D)), whole((t, D)), col],
        out_specs=[col] * 3 + specs,
        out_shape=[S((t, D), low)] * 3 + shapes,
        scratch_shapes=[pltpu.VMEM((16, D), f32)],
        name="heads_back",
        **params(t * D * 24000, t * D * 20, room=60),
    )(q, k, v, dc, p, x, sums, c, da)


def gelu_parts(h):
    d = 1.0 + (0.3275911 * 0.7071067811865476) * jnp.abs(h)
    t = pl.reciprocal(d, approx=True)
    t = t * (2.0 - d * t)
    poly = t * (0.127414796 + t * (-0.142248368 + t * (0.7107068705 + t * (-0.7265760135 + t * 0.5307027145))))
    bell = jnp.exp(-0.5 * (h * h))
    tail = poly * bell
    cdf = jnp.where(h >= 0, 1.0 - tail, tail)
    return h * cdf, cdf + h * (bell * 0.3989422804014327)


def inner_body(cube, n_ref, vec_ref, *refs):
    parts, (a_ref, gp_ref, full_ref, w_ref, sems, out_sem) = refs[:-6], refs[-6:]
    onward = assemble(cube, parts, w_ref, full_ref, sems, out_sem)
    n = n_ref[...]
    w = w_ref.reshape(D, FF) if cube else w_ref
    for j in range(FF // BLOCK):
        cols = pl.ds(j * BLOCK, BLOCK)
        h = nn(n, w[:, cols]) + vec_ref[B_INNER + j : B_INNER + j + 1].astype(f32)
        act, slope = gelu_parts(h)
        a_ref[:, cols] = act.astype(low)
        gp_ref[:, cols] = slope.astype(low)

    @pl.when(pl.program_id(0) == pl.num_programs(0) - 1)
    def _():
        onward.wait()


def inner(n, vec, parts, cube):
    t = n.shape[0]
    shape = (4, 2, 2, 2, 24, FF) if cube else (D, FF)
    act, slope, full = pl.pallas_call(
        lambda *refs: inner_body(cube, *refs),
        grid=(t // ROWS,),
        in_specs=[row_block(D), whole(vec.shape)] + [ANY] * len(parts),
        out_specs=[row_block(FF), row_block(FF), ANY],
        out_shape=[S((t, FF), low), S((t, FF), low), S(shape, low)],
        scratch_shapes=[pltpu.VMEM(shape, low), pltpu.SemaphoreType.DMA((4,)), pltpu.SemaphoreType.DMA],
        name="inner",
        **params(6 * t * D * FF, 2 * t * D + 4 * t * FF + 4 * D * FF, 2 * t * FF, room=60),
    )(n, vec, *parts)
    return act, slope, full.reshape(D, FF)


def outer_body(cube, a_ref, hat_ref, vec_ref, *refs):
    parts = refs[:-9]
    out_ref, hat2_ref, inv_ref, cls_ref, unit_ref, full_ref, w_ref, sems, out_sem = refs[-9:]
    onward = assemble(cube, parts, w_ref, full_ref, sems, out_sem)
    step = pl.program_id(0)
    w = w_ref.reshape(FF, D) if cube else w_ref
    branch = nn(a_ref[...], w[...]) + vec_ref[B_OUTER : B_OUTER + 1].astype(f32)
    normed = hat_ref[...] * vec_ref[G_ATTN : G_ATTN + 1].astype(f32) + vec_ref[S_ATTN : S_ATTN + 1].astype(f32)
    hat, inv = layer_norm(normed + branch)
    hat2_ref[...] = hat
    inv_ref[...] = inv
    rows = hat * vec_ref[G_FFN : G_FFN + 1].astype(f32) + vec_ref[S_FFN : S_FFN + 1].astype(f32)
    out_ref[...] = rows.astype(low)
    pairs = rows.shape[0] // LEN // 2
    for s in range(pairs):
        at = pl.ds(step * pairs + s, 1)
        for side in range(2):
            cols = pl.ds(side * D, D)
            cls = rows[LEN * (2 * s + side) : LEN * (2 * s + side) + 1]
            cls_ref[at, cols] = cls

    @pl.when(step == pl.num_programs(0) - 1)
    def _():
        for side in range(2):
            cls = cls_ref[:, side * D : (side + 1) * D]
            unit = cls * lax.rsqrt(jnp.sum(cls * cls, axis=-1, keepdims=True) + pool_eps)
            unit_ref[:, side * D : (side + 1) * D] = unit.astype(low)
        onward.wait()


def outer(act, hat, vec, parts, cube):
    t = hat.shape[0]
    shape = (4, 2, 2, 2, 96, D) if cube else (FF, D)
    pairs = t // LEN // 2
    once = pl.BlockSpec((pairs, 2 * D), lambda i: (0, 0))
    *outs, full = pl.pallas_call(
        lambda *refs: outer_body(cube, *refs),
        grid=(t // ROWS,),
        in_specs=[row_block(FF), row_block(D), whole(vec.shape)] + [ANY] * len(parts),
        out_specs=[row_block(D), row_block(D), row_block(1), once, once, ANY],
        out_shape=[S((t, D), low), S((t, D), f32), S((t, 1), f32), S((pairs, 2 * D), f32), S((pairs, 2 * D), low), S(shape, low)],
        scratch_shapes=[pltpu.VMEM(shape, low), pltpu.SemaphoreType.DMA((4,)), pltpu.SemaphoreType.DMA],
        name="outer",
        **params(2 * t * D * FF, 10 * t * D + 2 * t * FF + 4 * D * FF, room=60),
    )(act, hat, vec, *parts)
    return *outs, full.reshape(FF, D)


def write_shares(full, keep_ref, away_ref, put):
    core = lax.axis_index(AXIS) & 1

    def write(zero, one):
        for y in range(2):
            for x in range(2):
                put(zero, x, y, full(y, x, 0))
                put(one, y, x, full(y, x, 1))

    @pl.when(core == 0)
    def _():
        write(keep_ref, away_ref)

    @pl.when(core == 1)
    def _():
        write(away_ref, keep_ref)


def outer_back_body(cube, cot_ref, dc_ref, hat2_ref, inv2_ref, a_ref, vec_ref, dres_ref, dbr_ref, sums_ref, *refs):
    j = pl.program_id(0)

    def write(dw):
        if cube:
            dw = dw.reshape(2, 2, 2, 96, D)

            def put(ref, p, q, value):
                ref[0, p, q] = value.astype(ref.dtype)

            write_shares(lambda y, x, c: dw[y, x, c], *refs, put)
        else:
            refs[0][...] = dw

    @pl.when(j == 0)
    def _():
        dw = jnp.zeros((BLOCK, D), f32)
        dgain = jnp.zeros((1, D), f32)
        dshift = jnp.zeros((1, D), f32)
        dbias = jnp.zeros((1, D), f32)
        at = lax.broadcasted_iota(jnp.int32, (ROWS, D), 0)
        for b in range(cot_ref.shape[0] // ROWS):
            rows = pl.ds(b * ROWS, ROWS)
            d = cot_ref[rows, :].astype(f32)
            hat = hat2_ref[rows, :]
            for s in range(ROWS // LEN):
                whose = b * (ROWS // LEN) + s
                extra = dc_ref[whose // 2 : whose // 2 + 1, (whose % 2) * D : (whose % 2 + 1) * D]
                d += jnp.where(at == LEN * s, extra, 0.0)
            dgain += jnp.sum(d * hat, axis=0, keepdims=True)
            dshift += jnp.sum(d, axis=0, keepdims=True)
            dres = layer_norm_back(d, vec_ref[G_FFN : G_FFN + 1].astype(f32), hat, inv2_ref[rows, :])
            dres_ref[rows, :] = dres
            dbr = dres.astype(low)
            dbr_ref[rows, :] = dbr
            dbias += jnp.sum(dbr.astype(f32), axis=0, keepdims=True)
            dw += tn(a_ref[rows, :], dbr)
        write(dw)
        sums_ref[...] = jnp.zeros_like(sums_ref)
        sums_ref[B_OUTER : B_OUTER + 1] = dbias
        sums_ref[G_FFN : G_FFN + 1] = dgain
        sums_ref[S_FFN : S_FFN + 1] = dshift

    @pl.when(j > 0)
    def _():
        write(tn(a_ref[...], dbr_ref[...]))


def outer_back(cot, dc, hat2, inv2, a, vec, cube):
    t = cot.shape[0]
    if cube:
        spec = pl.BlockSpec((1, 2, 2, 96, D), lambda j: (j, 0, 0, 0, 0))
        specs, shapes = [spec] * 2, [S((4, 2, 2, 96, D), KEEP), S((4, 2, 2, 96, D), low)]
    else:
        specs, shapes = [pl.BlockSpec((BLOCK, D), lambda j: (j, 0))], [S((FF, D), f32)]
    return pl.pallas_call(
        lambda *refs: outer_back_body(cube, *refs),
        grid=(FF // BLOCK,),
        in_specs=[whole((t, D)), whole(dc.shape), whole((t, D)), whole((t, 1)), pl.BlockSpec((t, BLOCK), lambda j: (0, j)),
                  whole(vec.shape)],
        out_specs=[whole((t, D)), whole((t, D)), whole((16, D))] + specs,
        out_shape=[S((t, D), f32), S((t, D), low), S((16, D), f32)] + shapes,
        name="outer_back",
        **params(4 * t * D * FF, 14 * t * D + 2 * t * FF + 8 * D * FF, room=60),
    )(cot, dc, hat2, inv2, a, vec)


def inner_back_body(cube, dbr_ref, n_ref, gp_ref, wo_ref, before_ref, dh_ref, sums_ref, *refs):
    @pl.when(pl.program_id(0) == 0)
    def _():
        sums_ref[...] = before_ref[...]

    dh = (gp_ref[...].astype(f32) * nt(dbr_ref[...], wo_ref[...])).astype(low)
    dh_ref[...] = dh
    sums_ref[pl.ds(B_INNER + pl.program_id(0), 1), :] = jnp.sum(dh.astype(f32), axis=0, keepdims=True)
    dw = tn(n_ref[...], dh)
    if cube:
        dw = dw.reshape(4, 2, 2, 2, 24, BLOCK)

        def put(ref, p, q, value):
            ref[:, p, q] = value.astype(ref.dtype)

        write_shares(lambda y, x, c: dw[:, y, x, c], *refs, put)
    else:
        refs[0][...] = dw


def inner_back(dbr, n, gp, wo, sums, cube):
    t = n.shape[0]
    fblk = pl.BlockSpec((t, BLOCK), lambda j: (0, j))
    if cube:
        spec = pl.BlockSpec((4, 2, 2, 24, BLOCK), lambda j: (0, 0, 0, 0, j))
        specs, shapes = [spec] * 2, [S((4, 2, 2, 24, FF), KEEP), S((4, 2, 2, 24, FF), low)]
    else:
        specs, shapes = [pl.BlockSpec((D, BLOCK), lambda j: (0, j))], [S((D, FF), f32)]
    return pl.pallas_call(
        lambda *refs: inner_back_body(cube, *refs),
        grid=(FF // BLOCK,),
        in_specs=[whole((t, D)), whole((t, D)), fblk, pl.BlockSpec((BLOCK, D), lambda j: (j, 0)), whole((16, D))],
        out_specs=[fblk, whole((16, D))] + specs,
        out_shape=[S((t, FF), low), S((16, D), f32)] + shapes,
        name="inner_back",
        **params(4 * t * D * FF, 4 * t * D + 4 * t * FF + 8 * D * FF, room=60),
    )(dbr, n, gp, wo, sums)


KEEP = low


def token_grad_body(dr_ref, dq_ref, dk_ref, dv_ref, wq_ref, wk_ref, wv_ref, o_ref):
    o_ref[...] = (
        dr_ref[...] + nt(dq_ref[...], wq_ref[0]) + nt(dk_ref[...], wk_ref[0]) + nt(dv_ref[...], wv_ref[0])
    )


def token_grad(dr, dq, dk, dv, qk, vo):
    t = dr.shape[0]

    return pl.pallas_call(
        token_grad_body,
        grid=(t // ROWS,),
        in_specs=[row_block(D)] * 4 + [mat_of(0), mat_of(1), mat_of(0)],
        out_specs=row_block(D),
        out_shape=S((t, D), f32),
        name="token_grad",
        **params(6 * t * D * D, 14 * t * D + 6 * D * D, room=60),
    )(dr, dq, dk, dv, qk, qk, vo)


def loss_body(near, far, near_other, far_other, codes_ref, cls_ref, loss_ref, dc_ref, table_ref, ds_ref, units_ref, sems):
    parts = (near, far, near_other, far_other)
    part_copies(parts, units_ref, sems, everything)
    part_waits(parts, units_ref, sems, everything)
    own = cls_ref.shape[0]
    pairs = CUBE * own
    units = units_ref.reshape(pairs, 2 * D)
    sources, targets = units[:, :D], units[:, D:]
    codes = codes_ref[CODES : CODES + 2, :pairs].astype(f32)
    partner = (codes[0:1] + 64.0 * codes[1:2]).astype(jnp.int32)
    matched = lax.broadcasted_iota(jnp.int32, (pairs, pairs), 0) == partner
    sims = nt(targets, sources) * sim_scale - jnp.where(matched, sim_scale * sim_margin, 0.0)
    row_top = jnp.max(sims, axis=0, keepdims=True)
    row_lse = row_top + jnp.log(jnp.sum(jnp.exp(sims - row_top), axis=0, keepdims=True))
    col_top = jnp.max(sims, axis=1, keepdims=True)
    col_lse = col_top + jnp.log(jnp.sum(jnp.exp(sims - col_top), axis=1, keepdims=True))
    total = (
        jnp.sum(row_lse, axis=1, keepdims=True)
        + jnp.sum(col_lse, axis=0, keepdims=True)
        - 2.0 * jnp.sum(jnp.sum(jnp.where(matched, sims, 0.0), axis=1, keepdims=True), axis=0, keepdims=True)
    )
    loss_ref[...] = jnp.broadcast_to(total * (0.5 / pairs), loss_ref.shape)
    d_sims = 0.5 * (jnp.exp(sims - row_lse) + jnp.exp(sims - col_lse)) - jnp.where(matched, 1.0, 0.0)
    d_low = (d_sims * sim_scale).astype(low)
    table_ref[...] = nn(d_low, sources)
    ds_ref[...] = tn(d_low, targets)
    mine = pl.ds(pl.multiple_of(lax.axis_index(AXIS) * own, own), own)
    for side, ref in enumerate((ds_ref, table_ref)):
        cols = pl.ds(side * D, D)
        cls, du = cls_ref[:, cols], ref[mine, :]
        inv = lax.rsqrt(jnp.sum(cls * cls, axis=-1, keepdims=True) + pool_eps)
        dc_ref[:, cols] = inv * du - cls * (inv * inv * inv * jnp.sum(du * cls, axis=-1, keepdims=True))


def pair_loss(parts, vec, cls):
    own = cls.shape[0]
    pairs = CUBE * own
    loss, dc = pl.pallas_call(
        loss_body,
        in_specs=[ANY] * 4 + [whole(vec.shape), whole(cls.shape)],
        out_specs=[whole((8, 128)), whole(cls.shape)],
        out_shape=[S((8, 128), f32), S(cls.shape, f32)],
        scratch_shapes=[pltpu.VMEM((pairs, D), f32), pltpu.VMEM((pairs, D), f32),
                        pltpu.VMEM((4, 2, 2, 2, own, 2 * D), low), pltpu.SemaphoreType.DMA((4,))],
        grid=(1,),
        name="pair_loss",
        **params(6 * pairs * pairs * D, 4 * pairs * D, 4 * pairs * pairs, room=60),
    )(*parts, vec, cls)
    return loss[0, 0], dc


CORE = [(i, i ^ 1) for i in range(CUBE)]
FAR_Z = [(i, i ^ 16) for i in range(CUBE)]
NEAR_Z = [(i, i ^ 8) for i in range(CUBE)]
FIRST = [(i, i ^ (4 if i & 1 else 2)) for i in range(CUBE)]
SECOND = [(i, i ^ (2 if i & 1 else 4)) for i in range(CUBE)]
ROUTES = (CORE, FIRST, SECOND, NEAR_Z, FAR_Z)


class Place:
    def __init__(self):
        self.me = lax.axis_index(AXIS)
        self.core = self.me & 1
        x, y = (self.me >> 1) & 1, (self.me >> 2) & 1
        self.near_z, self.far_z = (self.me >> 3) & 1, (self.me >> 4) & 1
        self.first = jnp.where(self.core == 0, x, y)
        self.second = jnp.where(self.core == 0, y, x)
        self.bits = [b.reshape(1) for b in (self.first, self.second, self.near_z, self.far_z)]


def join(own, other, axis, bit):
    shape = own.shape[:axis] + (2,) + own.shape[axis:]
    where = lax.broadcasted_iota(jnp.int32, shape, axis)
    return jnp.where(where == bit, jnp.expand_dims(own, axis), jnp.expand_dims(other, axis))


def pick(field, axis, bit):
    return lax.dynamic_index_in_dim(field, bit, axis, keepdims=False)


def send(field, route):
    return lax.ppermute(field, AXIS, route)


def spread(block, place):
    block = join(block, send(block, FAR_Z), 0, place.far_z)
    block = join(block, send(block, NEAR_Z), 1, place.near_z)
    return join(block, send(block, FIRST), 2, place.first)


def together(*values):
    return lax.optimization_barrier(values)


class Reduction:
    def __init__(self, shares, place, early_z=False):
        keep, self.away = shares
        self.terms = [keep.reshape(2, 2, *keep.shape[1:])]
        self.left = [(2, place.first), (2, place.second), (1, place.near_z), (0, place.far_z)]
        if early_z:
            self.left = [(1, place.near_z), (1, place.first), (1, place.second), (0, place.far_z)]
        self.came = None

    def start(self, route):
        self.came, self.away = send(self.away, route), None

    def settle(self):
        self.terms.append(self.came.reshape(self.terms[0].shape))
        axis, bit = self.left.pop(0)
        self.away = sum(pick(term, axis, 1 - bit).astype(f32) for term in self.terms).astype(low)
        self.terms = [pick(term, axis, bit) for term in self.terms]

    def total(self):
        return sum(term.astype(f32) for term in (*self.terms, self.came))


def arrive(sums, *values):
    done = together(*values, *[s.came for s in sums])
    for s, came in zip(sums, done[len(values) :]):
        s.came = came
    return done[: len(values)]


def spread_rows(rows, at, count):
    r = rows.shape[1]
    lane = lax.broadcasted_iota(jnp.int32, (r, D), 1)
    copies = nn(rows, jnp.where(lane % r == lax.broadcasted_iota(jnp.int32, (r, D), 0), 1.0, 0.0).astype(low))
    lane = lax.broadcasted_iota(jnp.int32, (count, D), 1)
    row = lax.broadcasted_iota(jnp.int32, (count, D), 0)
    return copies, lane // r, row


def vector_table(vectors, partners, place):
    *small, inner = vectors
    copies, lane, _ = spread_rows(jnp.stack(small), place.me, len(small))
    table = [jnp.where(lane == place.me, copies, 0.0)]
    fold = D // inner.shape[0]
    copies, lane, row = spread_rows(inner[None], place.me, FF // D)
    table.append(jnp.where((row == place.me // fold) & (lane == place.me % fold), copies, 0.0))
    codes = jnp.stack([partners % 64, partners // 64]).astype(low)
    copies, lane, _ = spread_rows(codes, place.me, 2)
    table.append(jnp.where(lane == place.me, copies, 0.0))
    table.append(jnp.zeros((2, D), f32))
    return jnp.concatenate(table, axis=0).astype(low)


def pack_body(*refs):
    *mats, out = refs
    r = mats[0].shape[0]
    for i, mat in enumerate(mats):
        out[i * r : (i + 1) * r, :] = mat[...]


def pack(*mats):
    r, n = mats[0].shape
    return pl.pallas_call(pack_body, out_shape=S((len(mats) * r, n), low), name="pack")(*mats)


def plain_loss(units, partners, cls):
    sources, targets = units[:, :D], units[:, D:]
    npairs, own = units.shape[0], cls.shape[0]
    sims = nt(sources, targets) * sim_scale
    matched = partners[:, None] == jnp.arange(npairs, dtype=jnp.int32)[None, :]
    sims = sims - jnp.where(matched, sim_scale * sim_margin, 0.0)
    row_top = jnp.max(sims, axis=1, keepdims=True)
    row_lse = row_top + jnp.log(jnp.sum(jnp.exp(sims - row_top), axis=1, keepdims=True))
    col_top = jnp.max(sims, axis=0, keepdims=True)
    col_lse = col_top + jnp.log(jnp.sum(jnp.exp(sims - col_top), axis=0, keepdims=True))
    positive = jnp.sum(jnp.where(matched, sims, 0.0))
    loss = (jnp.sum(row_lse) + jnp.sum(col_lse) - 2.0 * positive) / (2.0 * npairs)
    d_sims = 0.5 * (jnp.exp(sims - row_lse) + jnp.exp(sims - col_lse)) - jnp.where(matched, 1.0, 0.0)
    d_low = (d_sims * sim_scale).astype(low)
    first = lax.axis_index(AXIS) * own
    du = [
        nn(lax.dynamic_slice_in_dim(d_low, first, own, 0), targets),
        tn(lax.dynamic_slice_in_dim(d_low, first, own, 1), sources),
    ]
    dc = []
    for side in range(2):
        c = cls[:, side * D : (side + 1) * D]
        inv = lax.rsqrt(jnp.sum(c * c, axis=-1, keepdims=True) + pool_eps)
        dc.append(inv * du[side] - c * (inv * inv * inv * jnp.sum(du[side] * c, axis=-1, keepdims=True)))
    return loss, jnp.concatenate(dc, axis=1)


def every(v):
    return lax.all_gather(v, AXIS, axis=0, tiled=True)


def scatter(v):
    return lax.psum_scatter(v, AXIS, scatter_dimension=0, tiled=True)


def local(
    tokens,
    lengths,
    partners,
    out_cotangent,
    w_query,
    w_key,
    w_value,
    w_output,
    b_query,
    b_value,
    b_output,
    gain_attn,
    shift_attn,
    w_inner,
    b_inner,
    w_outer,
    b_outer,
    gain_ffn,
    shift_ffn,
):
    cube = lax.axis_size(AXIS) == CUBE
    count = tokens.shape[0]
    x = tokens.reshape(count * LEN, D)
    vectors = (b_query, b_value, b_output, gain_attn, shift_attn, b_outer, gain_ffn, shift_ffn, b_inner)
    if cube:
        place = Place()
        qk = pack(w_query, w_key)
        vo = pack(w_value, w_output)
        vec = vector_table(vectors, partners, place)
        qk = join(qk, send(qk, FAR_Z), 0, place.far_z)
        vec = vec + send(vec, FAR_Z)
        qk, vec, vo = together(qk, vec, vo)
        qk = join(qk, send(qk, NEAR_Z), 1, place.near_z)
        vec = vec + send(vec, NEAR_Z)
        vo = join(vo, send(vo, FAR_Z), 0, place.far_z)
        qk, vec, vo, w_inner = together(qk, vec, vo, w_inner)
        qk = join(qk, send(qk, FIRST), 2, place.first).reshape(4, 2, 48, D)
        vec = vec + send(vec, FIRST)
        vo = join(vo, send(vo, NEAR_Z), 1, place.near_z)
        inn = join(w_inner, send(w_inner, FAR_Z), 0, place.far_z)
        qk, vec, vo, inn = together(qk, vec, vo, inn)
        far = send(qk, SECOND)
        other = send(qk, CORE)
        vec = vec + send(vec, SECOND)
        vo = join(vo, send(vo, FIRST), 2, place.first).reshape(4, 2, 48, D)
        inn = join(inn, send(inn, NEAR_Z), 1, place.near_z)
        far, other, vec, vo, inn = together(far, other, vec, vo, inn)
        qk_parts = (qk, far, other, send(far, CORE))
        vec = vec + send(vec, CORE)
        qk_parts, vec, vo, inn, w_outer = together(qk_parts, vec, vo, inn, w_outer)
        vo_far = send(vo, SECOND)
        other = send(vo, CORE)
        inn = join(inn, send(inn, FIRST), 2, place.first).reshape(4, 2, 24, FF)
        out = join(w_outer, send(w_outer, FAR_Z), 0, place.far_z)
        queries, keys, qk = project(x, vec, qk_parts, 2, (B_QUERY, None), cube)
        queries, vo_far, other, inn, out = together(queries, vo_far, other, inn, out)
        vo_parts = (vo, vo_far, other, send(vo_far, CORE))
        inn_far = send(inn, SECOND)
        values, vo = project(x, vec, vo_parts, 2, (B_VALUE,), cube)
        values, out = together(values, out)
        out = join(out, send(out, NEAR_Z), 1, place.near_z)
        probs, context = attend(lengths, queries, keys, values)
        context, inn, inn_far, out = together(context, inn, inn_far, out)
        inn_parts = (inn, inn_far, send(inn, CORE), send(inn_far, CORE))
        out = join(out, send(out, FIRST), 2, place.first).reshape(4, 2, 96, D)
        hat1, inv1, normed = close(x, context, vo, vec)
        normed, inn_parts, out = together(normed, inn_parts, out)
        out_far = send(out, SECOND)
        other = send(out, CORE)
        act, slope, inner_mat = inner(normed, vec, inn_parts, cube)
        act, out_far, other = together(act, out_far, other)
        out_parts = (out, out_far, other, send(out_far, CORE))
        block_out, hat2, inv2, cls, unit, outer_mat = outer(act, hat1, vec, out_parts, cube)
        near = spread(unit, place).reshape(4, 2, *unit.shape)
        far = send(near, SECOND)
        loss, d_cls = pair_loss((near, far, send(near, CORE), send(far, CORE)), vec, cls)
        dres, dbr, sums, *shares = outer_back(
            out_cotangent.reshape(count * LEN, D), d_cls, hat2, inv2, act, vec, cube
        )
        o = Reduction(shares, place)
        dbr, o.away = together(dbr, o.away)
        o.start(CORE)
        dh, sums, *shares = inner_back(dbr, normed, slope, outer_mat, sums, cube)
        i = Reduction(shares, place, early_z=True)
        dh, i.away = arrive([o], dh, i.away)
        i.start(CORE)
        o.settle()
        o.start(FIRST)
        dh, dres = together(dh, dres)
        d_resid, d_attn, d_context, sums = open_back(dres, dh, inner_mat, hat1, inv1, vo, vec, sums)
        (d_context,) = arrive([o, i], d_context)
        o.settle()
        o.start(SECOND)
        i.settle()
        i.start(NEAR_Z)
        d_queries, d_keys, d_values, *shares = heads_back(
            queries, keys, values, d_context, probs, x, sums, context, d_attn, cube
        )
        a = Reduction(shares, place)
        d_queries, a.away = arrive([o, i], d_queries, a.away)
        a.start(CORE)
        o.settle()
        i.settle()
        o.away, i.away = arrive([a], o.away, i.away)
        a.settle()
        a.start(FIRST)
        o.start(NEAR_Z)
        i.start(FIRST)
        grad_rows = token_grad(d_resid, d_queries, d_keys, d_values, qk, vo)
        (grad_rows,) = arrive([o, i, a], grad_rows)
        a.settle()
        a.start(SECOND)
        o.settle()
        o.start(FAR_Z)
        i.settle()
        i.start(SECOND)
        arrive([i, a])
        a.settle()
        a.start(NEAR_Z)
        i.settle()
        i.start(FAR_Z)
        grad_w_outer = o.total()
        (grad_w_outer,) = arrive([a], grad_w_outer)
        a.settle()
        a.start(FAR_Z)
        grad_w_inner = i.total()
        g_attn = a.total()
        g_mats = [g_attn[24 * n : 24 * (n + 1)] for n in range(4)]
        small, inner_part = g_attn[96:, D - WIDE :], g_attn[96, D - WIDE // 2 :]
        grads = [small[n, : D // CUBE] for n in range(B_INNER)] + [inner_part[: FF // CUBE]]
    else:
        rows = [every(v).reshape(-1, D) for v in vectors]
        vec = jnp.concatenate(rows + [jnp.zeros((4, D), low)], axis=0)
        qk_parts, vo_parts = ((jnp.stack([every(w) for w in ws]),) for ws in ((w_query, w_key), (w_value, w_output)))
        queries, keys, qk = project(x, vec, qk_parts, 2, (B_QUERY, None), cube)
        values, vo = project(x, vec, vo_parts, 2, (B_VALUE,), cube)
        probs, context = attend(lengths, queries, keys, values)
        hat1, inv1, normed = close(x, context, vo, vec)
        act, slope, inner_mat = inner(normed, vec, (every(w_inner),), cube)
        block_out, hat2, inv2, cls, unit, outer_mat = outer(act, hat1, vec, (every(w_outer),), cube)
        loss, d_cls = plain_loss(every(unit), every(partners), cls)
        dres, dbr, sums, d_outer = outer_back(
            out_cotangent.reshape(count * LEN, D), d_cls, hat2, inv2, act, vec, cube
        )
        dh, sums, d_inner = inner_back(dbr, normed, slope, outer_mat, sums, cube)
        d_resid, d_attn, d_context, sums = open_back(dres, dh, inner_mat, hat1, inv1, vo, vec, sums)
        d_queries, d_keys, d_values, sums, d_mats = heads_back(
            queries, keys, values, d_context, probs, x, sums, context, d_attn, cube
        )
        grad_rows = token_grad(d_resid, d_queries, d_keys, d_values, qk, vo)
        grad_w_outer, grad_w_inner = scatter(d_outer), scatter(d_inner)
        g_mats = [scatter(d_mats[n]) for n in range(4)]
        grads = [scatter(sums[n]) for n in range(B_INNER)] + [scatter(sums[B_INNER:CODES].reshape(-1))]
    (
        grad_b_query,
        grad_b_value,
        grad_b_output,
        grad_gain_attn,
        grad_shift_attn,
        grad_b_outer,
        grad_gain_ffn,
        grad_shift_ffn,
        grad_b_inner,
    ) = grads
    return (
        loss,
        block_out.reshape(count, LEN, D),
        grad_rows.reshape(count, LEN, D),
        g_mats[0],
        g_mats[1],
        g_mats[2],
        g_mats[3],
        grad_b_query,
        grad_b_value,
        grad_b_output,
        grad_gain_attn,
        grad_shift_attn,
        grad_w_inner,
        grad_b_inner,
        grad_w_outer,
        grad_b_outer,
        grad_gain_ffn,
        grad_shift_ffn,
    )


def solution(mesh):
    rows, cols = P(AXIS), P(AXIS, None)
    cube = P(AXIS, None, None)
    in_specs = (cube, rows, rows, cube) + (cols,) * 4 + (rows,) * 5 + (cols, rows, cols) + (rows,) * 3
    out_specs = (P(), cube, cube) + (cols,) * 4 + (rows,) * 5 + (cols, rows, cols) + (rows,) * 3
    return jax.shard_map(local, mesh=mesh, in_specs=in_specs, out_specs=out_specs, check_vma=False)
```

```python
import jax
import jax.numpy as jnp
from jax import lax
from jax.experimental import pallas as pl
from jax.experimental.pallas import tpu as pltpu
from jax.sharding import PartitionSpec as P

D = 768
HEADS = 12
HEAD_DIM = 64
LEN = 64
FF = 3072
QUAD = 4
WIDE = QUAD * HEAD_DIM
GROUPS = HEADS // QUAD
ROWS = 256
BLOCK = 768
AXIS = "fsdp"
CUBE = 32
norm_eps = 1e-12
pool_eps = 1e-06
sim_scale = 50.0
sim_margin = 0.3
f32, low = jnp.float32, jnp.bfloat16
S = jax.ShapeDtypeStruct

B_QUERY, B_VALUE, B_OUTPUT, G_ATTN, S_ATTN, B_OUTER, G_FFN, S_FFN, B_INNER = range(9)
CODES = B_INNER + FF // D


def nn(a, b):
    return lax.dot_general(a, b, (((1,), (0,)), ((), ())), preferred_element_type=f32)


def nt(a, b):
    return lax.dot_general(a, b, (((1,), (1,)), ((), ())), preferred_element_type=f32)


def tn(a, b):
    return lax.dot_general(a, b, (((0,), (0,)), ((), ())), preferred_element_type=f32)


def whole(shape):
    return pl.BlockSpec(shape, lambda *_: (0,) * len(shape), pipeline_mode=pl.Buffered(1))


def row_block(width, rows=ROWS):
    return pl.BlockSpec((rows, width), lambda i, *_: (i, 0))


def params(flops, nbytes, exps=0, room=60):
    return dict(
        compiler_params=pltpu.CompilerParams(vmem_limit_bytes=room << 20),
        cost_estimate=pl.CostEstimate(flops=int(flops), bytes_accessed=int(nbytes), transcendentals=int(exps)),
    )


ANY = pl.BlockSpec(memory_space=pl.ANY)


def part_copies(parts, target, sems, cut):
    me = lax.axis_index(AXIS)
    core, x, y = me & 1, (me >> 1) & 1, (me >> 2) & 1

    def start(zero, one):
        for i in range(2):
            pltpu.make_async_copy(cut(zero[i]), target.at[:, (y + i) & 1, :, 0], sems.at[2 * i]).start()
            pltpu.make_async_copy(cut(one[i]), target.at[:, :, (x + i) & 1, 1], sems.at[2 * i + 1]).start()

    @pl.when(core == 0)
    def _():
        start(parts[:2], parts[2:])

    @pl.when(core == 1)
    def _():
        start(parts[2:], parts[:2])


def part_waits(parts, target, sems, cut):
    for i in range(2):
        pltpu.make_async_copy(cut(parts[i]), target.at[:, i, :, 0], sems.at[2 * i]).wait()
        pltpu.make_async_copy(cut(parts[i]), target.at[:, :, i, 1], sems.at[2 * i + 1]).wait()


def everything(ref):
    return ref


def project_body(cube, count, biases, x_ref, vec_ref, *refs):
    outs = len(biases)
    parts, out_refs, (full_ref, w_ref, sems, out_sem) = refs[: -outs - 4], refs[-outs - 4 : -4], refs[-4:]
    step = pl.program_id(0)
    onward = pltpu.make_async_copy(w_ref, full_ref, out_sem)

    @pl.when(step == 0)
    def _():
        if cube:

            def cut(m):
                return lambda ref: ref.at[:, :, pl.ds(m * 24, 24), :]

            for m in range(count):
                part_copies(parts, w_ref.at[m], sems.at[m], cut(m))
            for m in range(count):
                part_waits(parts, w_ref.at[m], sems.at[m], cut(m))
        else:
            copy = pltpu.make_async_copy(parts[0], w_ref, sems.at[0, 0])
            copy.start()
            copy.wait()
        onward.start()

    x = x_ref[...]
    for m, (bias, out) in enumerate(zip(biases, out_refs)):
        product = nn(x, w_ref.at[m].reshape(D, D)[...] if cube else w_ref[m])
        if bias is not None:
            product += vec_ref[bias : bias + 1].astype(f32)
        out[...] = product.astype(low)

    @pl.when(step == pl.num_programs(0) - 1)
    def _():
        onward.wait()


def project(x, vec, parts, count, biases, cube):
    t = x.shape[0]
    shape = (count, 4, 2, 2, 2, 24, D) if cube else (count, D, D)
    outs = len(biases)
    *products, full = pl.pallas_call(
        lambda *refs: project_body(cube, count, biases, *refs),
        grid=(t // (2 * ROWS),),
        in_specs=[row_block(D, 2 * ROWS), whole(vec.shape)] + [ANY] * len(parts),
        out_specs=[row_block(D, 2 * ROWS)] * outs + [ANY],
        out_shape=[S((t, D), low)] * outs + [S(shape, low)],
        scratch_shapes=[pltpu.VMEM(shape, low), pltpu.SemaphoreType.DMA((count, 4)), pltpu.SemaphoreType.DMA],
        name="project",
        **params(2 * outs * t * D * D, 2 * (outs + 1) * t * D + 4 * count * D * D, room=16),
    )(x, vec, *parts)
    return *products, full.reshape(count, D, D)


def assemble(cube, parts, w_ref, full_ref, sems, out_sem):
    onward = pltpu.make_async_copy(w_ref, full_ref, out_sem)

    @pl.when(pl.program_id(0) == 0)
    def _():
        if cube:
            part_copies(parts, w_ref, sems, everything)
            part_waits(parts, w_ref, sems, everything)
        else:
            copy = pltpu.make_async_copy(parts[0], w_ref, sems.at[0])
            copy.start()
            copy.wait()
        onward.start()

    return onward


def scratch_for(shape):
    return [pltpu.VMEM(shape, low), pltpu.SemaphoreType.DMA((4,)), pltpu.SemaphoreType.DMA]


def head_masks(dtype):
    lane = lax.broadcasted_iota(jnp.int32, (1, WIDE), 1) // HEAD_DIM
    return [jnp.where(lane == h, 1.0, 0.0).astype(dtype) for h in range(QUAD)]


def stacked(rows, masks):
    return jnp.concatenate([rows * m for m in masks], axis=0)


def unstacked(full, masks):
    return sum(full[LEN * h : LEN * (h + 1)] * m for h, m in enumerate(masks))


def layer_norm(resid):
    centred = resid - jnp.mean(resid, axis=-1, keepdims=True)
    inv = lax.rsqrt(jnp.mean(centred * centred, axis=-1, keepdims=True) + norm_eps)
    return centred * inv, inv


def layer_norm_back(grad, gain, hat, inv):
    grad = grad * gain
    mean = jnp.mean(grad, axis=-1, keepdims=True)
    along = jnp.mean(grad * hat, axis=-1, keepdims=True)
    return (grad - mean - hat * along) * inv


def attend_body(len_ref, q_ref, k_ref, v_ref, p_ref, c_ref):
    masks, masks32 = head_masks(low), head_masks(f32)
    per = q_ref.shape[0] // LEN
    first = pl.program_id(0) * per
    key_at = lax.broadcasted_iota(jnp.int32, (LEN, WIDE), 0)

    def sentence(s):
        rows = pl.ds(pl.multiple_of(s * LEN, LEN), LEN)
        seen = key_at < len_ref[first + s]
        for g in range(GROUPS):
            cols = pl.ds(g * WIDE, WIDE)
            q, k, v = q_ref[rows, cols], k_ref[rows, cols], v_ref[rows, cols]
            scores = nt(k, stacked(q, masks)) * HEAD_DIM ** (-0.5)
            scores = jnp.where(seen, scores, -1e30)
            expd = jnp.exp(scores - jnp.max(scores, axis=0, keepdims=True))
            probs = expd * (1.0 / jnp.sum(expd, axis=0, keepdims=True))
            p_ref[g, rows, :] = probs
            c_ref[rows, cols] = unstacked(tn(probs.astype(low), v), masks32).astype(low)

    pl.loop(0, per, unroll=UNROLL)(sentence)


UNROLL = 8


def mat_of(m):
    return pl.BlockSpec((1, D, D), lambda *_: (m, 0, 0), pipeline_mode=pl.Buffered(1))


def attend(lengths, q, k, v):
    t = q.shape[0]
    rows = row_block(D, 2 * ROWS)
    return pl.pallas_call(
        attend_body,
        grid_spec=pltpu.PrefetchScalarGridSpec(
            num_scalar_prefetch=1,
            grid=(t // (2 * ROWS),),
            in_specs=[rows] * 3,
            out_specs=[pl.BlockSpec((GROUPS, 2 * ROWS, WIDE), lambda i, *_: (0, i, 0)), rows],
        ),
        out_shape=[S((GROUPS, t, WIDE), f32), S((t, D), low)],
        name="attend",
        **params(10 * t * D * D, 20 * t * D, t * D, room=60),
    )(lengths, q, k, v)


def halves(ref):
    return [slice(i * ROWS, (i + 1) * ROWS) for i in range(ref.shape[0] // ROWS)]


def close_body(x_ref, c_ref, w_ref, vec_ref, hat_ref, inv_ref, n_ref):
    w = w_ref[0]
    branches = [nn(c_ref[r, :], w) + vec_ref[B_OUTPUT : B_OUTPUT + 1].astype(f32) for r in halves(x_ref)]
    for r, branch in zip(halves(x_ref), branches):
        hat, inv = layer_norm(x_ref[r, :].astype(f32) + branch)
        hat_ref[r, :] = hat
        inv_ref[r, :] = inv
        n_ref[r, :] = (hat * vec_ref[G_ATTN : G_ATTN + 1].astype(f32) + vec_ref[S_ATTN : S_ATTN + 1].astype(f32)).astype(low)


def close(x, c, full, vec):
    t = x.shape[0]
    rows = row_block(D, 2 * ROWS)
    return pl.pallas_call(
        close_body,
        grid=(t // (2 * ROWS),),
        in_specs=[rows, rows, mat_of(1), whole(vec.shape)],
        out_specs=[rows, row_block(1, 2 * ROWS), rows],
        out_shape=[S((t, D), f32), S((t, 1), f32), S((t, D), low)],
        name="close",
        **params(2 * t * D * D, 10 * t * D + 2 * D * D, room=60),
    )(x, c, full, vec)


def open_back_body(dres_ref, dh_ref, wi_ref, hat_ref, inv_ref, wo_ref, vec_ref, before_ref, dr_ref, da_ref, dc_ref, sums_ref):
    @pl.when(pl.program_id(0) == 0)
    def _():
        sums_ref[...] = before_ref[...]

    grads = [dres_ref[r, :] + nt(dh_ref[r, :], wi_ref[...]) for r in halves(dres_ref)]
    for r, dn in zip(halves(dres_ref), grads):
        hat = hat_ref[r, :]
        dres = layer_norm_back(dn, vec_ref[G_ATTN : G_ATTN + 1].astype(f32), hat, inv_ref[r, :])
        dr_ref[r, :] = dres
        dao = dres.astype(low)
        da_ref[r, :] = dao
        dc_ref[r, :] = nt(dao, wo_ref[0]).astype(low)
        sums_ref[B_OUTPUT : B_OUTPUT + 1] += jnp.sum(dao.astype(f32), axis=0, keepdims=True)
        sums_ref[G_ATTN : G_ATTN + 1] += jnp.sum(dn * hat, axis=0, keepdims=True)
        sums_ref[S_ATTN : S_ATTN + 1] += jnp.sum(dn, axis=0, keepdims=True)


def open_back(dres, dh, wi, hat, inv, full, vec, sums):
    t = dres.shape[0]
    return pl.pallas_call(
        open_back_body,
        grid=(t // (2 * ROWS),),
        in_specs=[row_block(D, 2 * ROWS), row_block(FF, 2 * ROWS), whole(wi.shape), row_block(D, 2 * ROWS), row_block(1, 2 * ROWS), mat_of(1), whole(vec.shape), whole((16, D))],
        out_specs=[row_block(D, 2 * ROWS)] * 3 + [whole((16, D))],
        out_shape=[S((t, D), f32), S((t, D), low), S((t, D), low), S((16, D), f32)],
        name="open_back",
        **params(10 * t * D * D, 20 * t * D + 10 * D * D, room=60),
    )(dres, dh, wi, hat, inv, full, vec, sums)


def device_rows(table):
    rows = 8 * CUBE
    row, lane = (lax.broadcasted_iota(jnp.int32, (rows, D), axis) for axis in range(2))
    out = []
    for values, r in (
        (jnp.concatenate([table[:8]] * CUBE, axis=0), D // CUBE),
        (jnp.concatenate([jnp.broadcast_to(table[B_INNER + j : B_INNER + j + 1], (rows * D // FF, D)) for j in range(FF // D)], axis=0), FF // CUBE),
    ):
        own = jnp.where(lane // r == (row // 8) % (D // r), values, 0.0).astype(low)
        at, to = (lax.broadcasted_iota(jnp.int32, (D, WIDE // 2), axis) for axis in range(2))
        out.append(nn(own, jnp.where(at % r == to, 1.0, 0.0).astype(low)))
    return jnp.concatenate(out, axis=1)


def heads_back_body(cube, q_ref, k_ref, v_ref, dc_ref, p_ref, x_ref, before_ref, c_ref, da_ref, *refs):
    dq_ref, dk_ref, dv_ref, *shares = refs[:-1]
    table_ref = refs[-1]
    step = pl.program_id(0)
    masks, masks32 = head_masks(low), head_masks(f32)

    def sentence(s):
        rows = pl.ds(pl.multiple_of(s * LEN, LEN), LEN)
        q, k, v, dc, p = q_ref[rows, :], k_ref[rows, :], v_ref[rows, :], dc_ref[rows, :], p_ref[0, rows, :]
        dcs = stacked(dc, masks)
        dp = nt(v, dcs)
        dv_ref[rows, :] = nn(p.astype(low), dcs).astype(low)
        ds = (p * (dp - jnp.sum(p * dp, axis=0, keepdims=True))).astype(low)
        dk_ref[rows, :] = (nn(ds, stacked(q, masks)) * HEAD_DIM ** (-0.5)).astype(low)
        dq_ref[rows, :] = (unstacked(tn(ds, k), masks32) * HEAD_DIM ** (-0.5)).astype(low)

    @pl.when(step == 0)
    def _():
        table_ref[...] = before_ref[...]

    pl.loop(0, q_ref.shape[0] // LEN, unroll=BACK_UNROLL)(sentence)
    cols = pl.ds(pl.multiple_of(step * WIDE, WIDE), WIDE)
    table_ref[B_QUERY : B_QUERY + 1, cols] = jnp.sum(dq_ref[...].astype(f32), axis=0, keepdims=True)
    table_ref[B_VALUE : B_VALUE + 1, cols] = jnp.sum(dv_ref[...].astype(f32), axis=0, keepdims=True)
    for m, (rows, grad) in enumerate(((x_ref, dq_ref), (x_ref, dk_ref), (x_ref, dv_ref), (c_ref, da_ref))):
        full = tn(rows[...], grad[...])
        if cube:
            full = full.reshape(4, 2, 2, 2, 24, WIDE)

            def put(ref, p, q, value, m=m):
                ref[:, p, q, 24 * m : 24 * (m + 1)] = value.astype(ref.dtype)

            write_shares(lambda y, x, c: full[:, y, x, c], *shares, put)
        else:
            shares[1][m] = full
    if cube:

        def put_rows(ref, p, q, value):
            ref[:, p, q, 96:] = value.astype(ref.dtype)

        @pl.when(step < GROUPS - 1)
        def _():
            write_shares(lambda y, x, c: jnp.zeros((4, 8, WIDE), f32), *shares, put_rows)

        @pl.when(step == GROUPS - 1)
        def _():
            values = device_rows(table_ref[...]).reshape(4, 2, 2, 2, 8, WIDE)
            write_shares(lambda y, x, c: values[:, y, x, c], *shares, put_rows)
    else:
        shares[0][...] = table_ref[...]


BACK_UNROLL = 16


def heads_back(q, k, v, dc, p, x, sums, c, da, cube):
    t = q.shape[0]
    col = pl.BlockSpec((t, WIDE), lambda i: (0, i))
    if cube:
        spec = pl.BlockSpec((4, 2, 2, 104, WIDE), lambda i: (0, 0, 0, 0, i))
        shape = (4, 2, 2, 104, D)
        specs, shapes = [spec] * 2, [S(shape, KEEP), S(shape, low)]
    else:
        specs = [whole((16, D)), pl.BlockSpec((4, D, WIDE), lambda i: (0, 0, i))]
        shapes = [S((16, D), f32), S((4, D, D), f32)]
    return pl.pallas_call(
        lambda *refs: heads_back_body(cube, *refs),
        grid=(GROUPS,),
        in_specs=[col] * 4
        + [pl.BlockSpec((1, t, WIDE), lambda i: (i, 0, 0)), whole((t, D)), whole((16, D)), whole((t, D)), col],
        out_specs=[col] * 3 + specs,
        out_shape=[S((t, D), low)] * 3 + shapes,
        scratch_shapes=[pltpu.VMEM((16, D), f32)],
        name="heads_back",
        **params(t * D * 24000, t * D * 20, room=60),
    )(q, k, v, dc, p, x, sums, c, da)


def gelu_parts(h):
    d = 1.0 + (0.3275911 * 0.7071067811865476) * jnp.abs(h)
    t = pl.reciprocal(d, approx=True)
    t = t * (2.0 - d * t)
    poly = t * (0.127414796 + t * (-0.142248368 + t * (0.7107068705 + t * (-0.7265760135 + t * 0.5307027145))))
    bell = jnp.exp(-0.5 * (h * h))
    tail = poly * bell
    cdf = jnp.where(h >= 0, 1.0 - tail, tail)
    return h * cdf, cdf + h * (bell * 0.3989422804014327)


def inner_body(cube, n_ref, vec_ref, *refs):
    parts, (a_ref, gp_ref, full_ref, w_ref, sems, out_sem, bias_ref) = refs[:-7], refs[-7:]
    onward = assemble(cube, parts, w_ref, full_ref, sems, out_sem)

    @pl.when(pl.program_id(0) == 0)
    def _():
        bias_ref[...] = vec_ref[...].astype(f32)

    w = w_ref.reshape(D, FF) if cube else w_ref

    @pl.loop(0, FF // BLOCK)
    def _(j):
        cols = pl.ds(pl.multiple_of(j * BLOCK, BLOCK), BLOCK)
        h = nn(n_ref[...], w[:, cols]) + bias_ref[pl.ds(B_INNER + j, 1), :]
        act, slope = gelu_parts(h)
        a_ref[:, cols] = act.astype(low)
        gp_ref[:, cols] = slope.astype(low)

    @pl.when(pl.program_id(0) == pl.num_programs(0) - 1)
    def _():
        onward.wait()


def inner(n, vec, parts, cube):
    t = n.shape[0]
    shape = (4, 2, 2, 2, 24, FF) if cube else (D, FF)
    act, slope, full = pl.pallas_call(
        lambda *refs: inner_body(cube, *refs),
        grid=(t // ROWS,),
        in_specs=[row_block(D), whole(vec.shape)] + [ANY] * len(parts),
        out_specs=[row_block(FF), row_block(FF), ANY],
        out_shape=[S((t, FF), low), S((t, FF), low), S(shape, low)],
        scratch_shapes=[*scratch_for(shape), pltpu.VMEM((16, D), f32)],
        name="inner",
        **params(6 * t * D * FF, 2 * t * D + 4 * t * FF + 4 * D * FF, 2 * t * FF, room=60),
    )(n, vec, *parts)
    return act, slope, full.reshape(D, FF)


def outer_body(cube, a_ref, hat_ref, vec_ref, *refs):
    parts = refs[:-9]
    out_ref, hat2_ref, inv_ref, cls_ref, unit_ref, full_ref, w_ref, sems, out_sem = refs[-9:]
    onward = assemble(cube, parts, w_ref, full_ref, sems, out_sem)
    step = pl.program_id(0)
    w = w_ref.reshape(FF, D) if cube else w_ref
    branch = nn(a_ref[...], w[...]) + vec_ref[B_OUTER : B_OUTER + 1].astype(f32)
    normed = hat_ref[...] * vec_ref[G_ATTN : G_ATTN + 1].astype(f32) + vec_ref[S_ATTN : S_ATTN + 1].astype(f32)
    hat, inv = layer_norm(normed + branch)
    hat2_ref[...] = hat
    inv_ref[...] = inv
    rows = hat * vec_ref[G_FFN : G_FFN + 1].astype(f32) + vec_ref[S_FFN : S_FFN + 1].astype(f32)
    out_ref[...] = rows.astype(low)
    pairs = rows.shape[0] // LEN // 2
    for s in range(pairs):
        at = pl.ds(step * pairs + s, 1)
        for side in range(2):
            cols = pl.ds(side * D, D)
            cls = rows[LEN * (2 * s + side) : LEN * (2 * s + side) + 1]
            cls_ref[at, cols] = cls

    @pl.when(step == pl.num_programs(0) - 1)
    def _():
        for side in range(2):
            cls = cls_ref[:, side * D : (side + 1) * D]
            unit = cls * lax.rsqrt(jnp.sum(cls * cls, axis=-1, keepdims=True) + pool_eps)
            unit_ref[:, side * D : (side + 1) * D] = unit.astype(low)
        onward.wait()


def outer(act, hat, vec, parts, cube):
    t = hat.shape[0]
    shape = (4, 2, 2, 2, 96, D) if cube else (FF, D)
    pairs = t // LEN // 2
    once = pl.BlockSpec((pairs, 2 * D), lambda i: (0, 0))
    *outs, full = pl.pallas_call(
        lambda *refs: outer_body(cube, *refs),
        grid=(t // ROWS,),
        in_specs=[row_block(FF), row_block(D), whole(vec.shape)] + [ANY] * len(parts),
        out_specs=[row_block(D), row_block(D), row_block(1), once, once, ANY],
        out_shape=[S((t, D), low), S((t, D), f32), S((t, 1), f32), S((pairs, 2 * D), f32), S((pairs, 2 * D), low), S(shape, low)],
        scratch_shapes=[pltpu.VMEM(shape, low), pltpu.SemaphoreType.DMA((4,)), pltpu.SemaphoreType.DMA],
        name="outer",
        **params(2 * t * D * FF, 10 * t * D + 2 * t * FF + 4 * D * FF, room=60),
    )(act, hat, vec, *parts)
    return *outs, full.reshape(FF, D)


def write_shares(full, keep_ref, away_ref, put):
    core = lax.axis_index(AXIS) & 1

    def write(zero, one):
        for y in range(2):
            for x in range(2):
                put(zero, x, y, full(y, x, 0))
                put(one, y, x, full(y, x, 1))

    @pl.when(core == 0)
    def _():
        write(keep_ref, away_ref)

    @pl.when(core == 1)
    def _():
        write(away_ref, keep_ref)


def outer_back_body(cube, cot_ref, dc_ref, hat2_ref, inv2_ref, a_ref, vec_ref, dres_ref, dbr_ref, sums_ref, *refs):
    j = pl.program_id(0)

    def write(dw):
        if cube:
            dw = dw.reshape(2, 2, 2, 96, D)

            def put(ref, p, q, value):
                ref[0, p, q] = value.astype(ref.dtype)

            write_shares(lambda y, x, c: dw[y, x, c], *refs, put)
        else:
            refs[0][...] = dw

    @pl.when(j == 0)
    def _():
        dw = jnp.zeros((BLOCK, D), f32)
        dgain = jnp.zeros((1, D), f32)
        dshift = jnp.zeros((1, D), f32)
        dbias = jnp.zeros((1, D), f32)
        at = lax.broadcasted_iota(jnp.int32, (ROWS, D), 0)
        for b in range(cot_ref.shape[0] // ROWS):
            rows = pl.ds(b * ROWS, ROWS)
            d = cot_ref[rows, :].astype(f32)
            hat = hat2_ref[rows, :]
            for s in range(ROWS // LEN):
                whose = b * (ROWS // LEN) + s
                extra = dc_ref[whose // 2 : whose // 2 + 1, (whose % 2) * D : (whose % 2 + 1) * D]
                d += jnp.where(at == LEN * s, extra, 0.0)
            dgain += jnp.sum(d * hat, axis=0, keepdims=True)
            dshift += jnp.sum(d, axis=0, keepdims=True)
            dres = layer_norm_back(d, vec_ref[G_FFN : G_FFN + 1].astype(f32), hat, inv2_ref[rows, :])
            dres_ref[rows, :] = dres
            dbr = dres.astype(low)
            dbr_ref[rows, :] = dbr
            dbias += jnp.sum(dbr.astype(f32), axis=0, keepdims=True)
            dw += tn(a_ref[rows, :], dbr)
        write(dw)
        sums_ref[...] = jnp.zeros_like(sums_ref)
        sums_ref[B_OUTER : B_OUTER + 1] = dbias
        sums_ref[G_FFN : G_FFN + 1] = dgain
        sums_ref[S_FFN : S_FFN + 1] = dshift

    @pl.when(j > 0)
    def _():
        write(tn(a_ref[...], dbr_ref[...]))


def outer_back(cot, dc, hat2, inv2, a, vec, cube):
    t = cot.shape[0]
    if cube:
        spec = pl.BlockSpec((1, 2, 2, 96, D), lambda j: (j, 0, 0, 0, 0))
        specs, shapes = [spec] * 2, [S((4, 2, 2, 96, D), KEEP), S((4, 2, 2, 96, D), low)]
    else:
        specs, shapes = [pl.BlockSpec((BLOCK, D), lambda j: (j, 0))], [S((FF, D), f32)]
    return pl.pallas_call(
        lambda *refs: outer_back_body(cube, *refs),
        grid=(FF // BLOCK,),
        in_specs=[whole((t, D)), whole(dc.shape), whole((t, D)), whole((t, 1)), pl.BlockSpec((t, BLOCK), lambda j: (0, j)),
                  whole(vec.shape)],
        out_specs=[whole((t, D)), whole((t, D)), whole((16, D))] + specs,
        out_shape=[S((t, D), f32), S((t, D), low), S((16, D), f32)] + shapes,
        name="outer_back",
        **params(4 * t * D * FF, 14 * t * D + 2 * t * FF + 8 * D * FF, room=60),
    )(cot, dc, hat2, inv2, a, vec)


def inner_back_body(cube, dbr_ref, n_ref, gp_ref, wo_ref, before_ref, dh_ref, sums_ref, *refs):
    @pl.when(pl.program_id(0) == 0)
    def _():
        sums_ref[...] = before_ref[...]

    dh = (gp_ref[...].astype(f32) * nt(dbr_ref[...], wo_ref[...])).astype(low)
    dh_ref[...] = dh
    sums_ref[pl.ds(B_INNER + pl.program_id(0), 1), :] = jnp.sum(dh.astype(f32), axis=0, keepdims=True)
    dw = tn(n_ref[...], dh)
    if cube:
        dw = dw.reshape(4, 2, 2, 2, 24, BLOCK)

        def put(ref, p, q, value):
            ref[:, p, q] = value.astype(ref.dtype)

        write_shares(lambda y, x, c: dw[:, y, x, c], *refs, put)
    else:
        refs[0][...] = dw


def inner_back(dbr, n, gp, wo, sums, cube):
    t = n.shape[0]
    fblk = pl.BlockSpec((t, BLOCK), lambda j: (0, j))
    if cube:
        spec = pl.BlockSpec((4, 2, 2, 24, BLOCK), lambda j: (0, 0, 0, 0, j))
        specs, shapes = [spec] * 2, [S((4, 2, 2, 24, FF), KEEP), S((4, 2, 2, 24, FF), low)]
    else:
        specs, shapes = [pl.BlockSpec((D, BLOCK), lambda j: (0, j))], [S((D, FF), f32)]
    return pl.pallas_call(
        lambda *refs: inner_back_body(cube, *refs),
        grid=(FF // BLOCK,),
        in_specs=[whole((t, D)), whole((t, D)), fblk, pl.BlockSpec((BLOCK, D), lambda j: (j, 0)), whole((16, D))],
        out_specs=[fblk, whole((16, D))] + specs,
        out_shape=[S((t, FF), low), S((16, D), f32)] + shapes,
        name="inner_back",
        **params(4 * t * D * FF, 4 * t * D + 4 * t * FF + 8 * D * FF, room=60),
    )(dbr, n, gp, wo, sums)


KEEP = low


def token_grad_body(dr_ref, dq_ref, dk_ref, dv_ref, wq_ref, wk_ref, wv_ref, o_ref):
    o_ref[...] = (
        dr_ref[...] + nt(dq_ref[...], wq_ref[0]) + nt(dk_ref[...], wk_ref[0]) + nt(dv_ref[...], wv_ref[0])
    )


def token_grad(dr, dq, dk, dv, qk, vo):
    t = dr.shape[0]

    return pl.pallas_call(
        token_grad_body,
        grid=(t // ROWS,),
        in_specs=[row_block(D)] * 4 + [mat_of(0), mat_of(1), mat_of(0)],
        out_specs=row_block(D),
        out_shape=S((t, D), f32),
        name="token_grad",
        **params(6 * t * D * D, 14 * t * D + 6 * D * D, room=60),
    )(dr, dq, dk, dv, qk, qk, vo)


def loss_body(near, far, near_other, far_other, codes_ref, cls_ref, loss_ref, dc_ref, table_ref, ds_ref, units_ref, sems):
    parts = (near, far, near_other, far_other)
    part_copies(parts, units_ref, sems, everything)
    part_waits(parts, units_ref, sems, everything)
    own = cls_ref.shape[0]
    pairs = CUBE * own
    units = units_ref.reshape(pairs, 2 * D)
    sources, targets = units[:, :D], units[:, D:]
    codes = codes_ref[CODES : CODES + 2, :pairs].astype(f32)
    partner = (codes[0:1] + 64.0 * codes[1:2]).astype(jnp.int32)
    matched = lax.broadcasted_iota(jnp.int32, (pairs, pairs), 0) == partner
    sims = nt(targets, sources) * sim_scale - jnp.where(matched, sim_scale * sim_margin, 0.0)
    row_top = jnp.max(sims, axis=0, keepdims=True)
    row_lse = row_top + jnp.log(jnp.sum(jnp.exp(sims - row_top), axis=0, keepdims=True))
    col_top = jnp.max(sims, axis=1, keepdims=True)
    col_lse = col_top + jnp.log(jnp.sum(jnp.exp(sims - col_top), axis=1, keepdims=True))
    total = (
        jnp.sum(row_lse, axis=1, keepdims=True)
        + jnp.sum(col_lse, axis=0, keepdims=True)
        - 2.0 * jnp.sum(jnp.sum(jnp.where(matched, sims, 0.0), axis=1, keepdims=True), axis=0, keepdims=True)
    )
    loss_ref[...] = jnp.broadcast_to(total * (0.5 / pairs), loss_ref.shape)
    d_sims = 0.5 * (jnp.exp(sims - row_lse) + jnp.exp(sims - col_lse)) - jnp.where(matched, 1.0, 0.0)
    d_low = (d_sims * sim_scale).astype(low)
    table_ref[...] = nn(d_low, sources)
    ds_ref[...] = tn(d_low, targets)
    mine = pl.ds(pl.multiple_of(lax.axis_index(AXIS) * own, own), own)
    for side, ref in enumerate((ds_ref, table_ref)):
        cols = pl.ds(side * D, D)
        cls, du = cls_ref[:, cols], ref[mine, :]
        inv = lax.rsqrt(jnp.sum(cls * cls, axis=-1, keepdims=True) + pool_eps)
        dc_ref[:, cols] = inv * du - cls * (inv * inv * inv * jnp.sum(du * cls, axis=-1, keepdims=True))


def pair_loss(parts, vec, cls):
    own = cls.shape[0]
    pairs = CUBE * own
    loss, dc = pl.pallas_call(
        loss_body,
        in_specs=[ANY] * 4 + [whole(vec.shape), whole(cls.shape)],
        out_specs=[whole((8, 128)), whole(cls.shape)],
        out_shape=[S((8, 128), f32), S(cls.shape, f32)],
        scratch_shapes=[pltpu.VMEM((pairs, D), f32), pltpu.VMEM((pairs, D), f32),
                        pltpu.VMEM((4, 2, 2, 2, own, 2 * D), low), pltpu.SemaphoreType.DMA((4,))],
        grid=(1,),
        name="pair_loss",
        **params(6 * pairs * pairs * D, 4 * pairs * D, 4 * pairs * pairs, room=12),
    )(*parts, vec, cls)
    return loss[0, 0], dc


CORE = [(i, i ^ 1) for i in range(CUBE)]
FAR_Z = [(i, i ^ 16) for i in range(CUBE)]
NEAR_Z = [(i, i ^ 8) for i in range(CUBE)]
FIRST = [(i, i ^ (4 if i & 1 else 2)) for i in range(CUBE)]
SECOND = [(i, i ^ (2 if i & 1 else 4)) for i in range(CUBE)]
ROUTES = (CORE, FIRST, SECOND, NEAR_Z, FAR_Z)


class Place:
    def __init__(self):
        self.me = lax.axis_index(AXIS)
        self.core = self.me & 1
        x, y = (self.me >> 1) & 1, (self.me >> 2) & 1
        self.near_z, self.far_z = (self.me >> 3) & 1, (self.me >> 4) & 1
        self.first = jnp.where(self.core == 0, x, y)
        self.second = jnp.where(self.core == 0, y, x)
        self.bits = [b.reshape(1) for b in (self.first, self.second, self.near_z, self.far_z)]


def join(own, other, axis, bit):
    shape = own.shape[:axis] + (2,) + own.shape[axis:]
    where = lax.broadcasted_iota(jnp.int32, shape, axis)
    return jnp.where(where == bit, jnp.expand_dims(own, axis), jnp.expand_dims(other, axis))


def pick(field, axis, bit):
    return lax.dynamic_index_in_dim(field, bit, axis, keepdims=False)


def send(field, route):
    return lax.ppermute(field, AXIS, route)


def spread(block, place):
    block = join(block, send(block, FAR_Z), 0, place.far_z)
    block = join(block, send(block, NEAR_Z), 1, place.near_z)
    return join(block, send(block, FIRST), 2, place.first)


def together(*values):
    return lax.optimization_barrier(values)


class Reduction:
    def __init__(self, shares, place, early_z=False):
        keep, self.away = shares
        self.terms = [keep.reshape(2, 2, *keep.shape[1:])]
        self.left = [(2, place.first), (2, place.second), (1, place.near_z), (0, place.far_z)]
        if early_z:
            self.left = [(1, place.near_z), (1, place.first), (1, place.second), (0, place.far_z)]
        self.came = None

    def start(self, route):
        self.came, self.away = send(self.away, route), None

    def settle(self):
        self.terms.append(self.came.reshape(self.terms[0].shape))
        axis, bit = self.left.pop(0)
        self.away = sum(pick(term, axis, 1 - bit).astype(f32) for term in self.terms).astype(low)
        self.terms = [pick(term, axis, bit) for term in self.terms]

    def total(self):
        return sum(term.astype(f32) for term in (*self.terms, self.came))


def arrive(sums, *values):
    done = together(*values, *[s.came for s in sums])
    for s, came in zip(sums, done[len(values) :]):
        s.came = came
    return done[: len(values)]


def spread_rows(rows, at, count):
    r = rows.shape[1]
    lane = lax.broadcasted_iota(jnp.int32, (r, D), 1)
    copies = nn(rows, jnp.where(lane % r == lax.broadcasted_iota(jnp.int32, (r, D), 0), 1.0, 0.0).astype(low))
    lane = lax.broadcasted_iota(jnp.int32, (count, D), 1)
    row = lax.broadcasted_iota(jnp.int32, (count, D), 0)
    return copies, lane // r, row


def vector_table(vectors, partners, place):
    *small, inner = vectors
    copies, lane, _ = spread_rows(jnp.stack(small), place.me, len(small))
    table = [jnp.where(lane == place.me, copies, 0.0)]
    fold = D // inner.shape[0]
    copies, lane, row = spread_rows(inner[None], place.me, FF // D)
    table.append(jnp.where((row == place.me // fold) & (lane == place.me % fold), copies, 0.0))
    codes = jnp.stack([partners % 64, partners // 64]).astype(low)
    copies, lane, _ = spread_rows(codes, place.me, 2)
    table.append(jnp.where(lane == place.me, copies, 0.0))
    table.append(jnp.zeros((2, D), f32))
    return jnp.concatenate(table, axis=0).astype(low)


def pack_body(*refs):
    *mats, out = refs
    r = mats[0].shape[0]
    for i, mat in enumerate(mats):
        out[i * r : (i + 1) * r, :] = mat[...]


def pack(*mats):
    r, n = mats[0].shape
    return pl.pallas_call(pack_body, out_shape=S((len(mats) * r, n), low), name="pack")(*mats)


def plain_loss(units, partners, cls):
    sources, targets = units[:, :D], units[:, D:]
    npairs, own = units.shape[0], cls.shape[0]
    sims = nt(sources, targets) * sim_scale
    matched = partners[:, None] == jnp.arange(npairs, dtype=jnp.int32)[None, :]
    sims = sims - jnp.where(matched, sim_scale * sim_margin, 0.0)
    row_top = jnp.max(sims, axis=1, keepdims=True)
    row_lse = row_top + jnp.log(jnp.sum(jnp.exp(sims - row_top), axis=1, keepdims=True))
    col_top = jnp.max(sims, axis=0, keepdims=True)
    col_lse = col_top + jnp.log(jnp.sum(jnp.exp(sims - col_top), axis=0, keepdims=True))
    positive = jnp.sum(jnp.where(matched, sims, 0.0))
    loss = (jnp.sum(row_lse) + jnp.sum(col_lse) - 2.0 * positive) / (2.0 * npairs)
    d_sims = 0.5 * (jnp.exp(sims - row_lse) + jnp.exp(sims - col_lse)) - jnp.where(matched, 1.0, 0.0)
    d_low = (d_sims * sim_scale).astype(low)
    first = lax.axis_index(AXIS) * own
    du = [
        nn(lax.dynamic_slice_in_dim(d_low, first, own, 0), targets),
        tn(lax.dynamic_slice_in_dim(d_low, first, own, 1), sources),
    ]
    dc = []
    for side in range(2):
        c = cls[:, side * D : (side + 1) * D]
        inv = lax.rsqrt(jnp.sum(c * c, axis=-1, keepdims=True) + pool_eps)
        dc.append(inv * du[side] - c * (inv * inv * inv * jnp.sum(du[side] * c, axis=-1, keepdims=True)))
    return loss, jnp.concatenate(dc, axis=1)


def every(v):
    return lax.all_gather(v, AXIS, axis=0, tiled=True)


def scatter(v):
    return lax.psum_scatter(v, AXIS, scatter_dimension=0, tiled=True)


def local(
    tokens,
    lengths,
    partners,
    out_cotangent,
    w_query,
    w_key,
    w_value,
    w_output,
    b_query,
    b_value,
    b_output,
    gain_attn,
    shift_attn,
    w_inner,
    b_inner,
    w_outer,
    b_outer,
    gain_ffn,
    shift_ffn,
):
    cube = lax.axis_size(AXIS) == CUBE
    count = tokens.shape[0]
    x = tokens.reshape(count * LEN, D)
    vectors = (b_query, b_value, b_output, gain_attn, shift_attn, b_outer, gain_ffn, shift_ffn, b_inner)
    if cube:
        place = Place()
        qk = pack(w_query, w_key)
        vo = pack(w_value, w_output)
        vec = vector_table(vectors, partners, place)
        qk = join(qk, send(qk, FAR_Z), 0, place.far_z)
        vec = vec + send(vec, FAR_Z)
        qk, vec, vo = together(qk, vec, vo)
        qk = join(qk, send(qk, NEAR_Z), 1, place.near_z)
        vec = vec + send(vec, NEAR_Z)
        vo = join(vo, send(vo, FAR_Z), 0, place.far_z)
        qk, vec, vo, w_inner = together(qk, vec, vo, w_inner)
        qk = join(qk, send(qk, FIRST), 2, place.first).reshape(4, 2, 48, D)
        vec = vec + send(vec, FIRST)
        vo = join(vo, send(vo, NEAR_Z), 1, place.near_z)
        inn = join(w_inner, send(w_inner, FAR_Z), 0, place.far_z)
        qk, vec, vo, inn = together(qk, vec, vo, inn)
        far = send(qk, SECOND)
        other = send(qk, CORE)
        vec = vec + send(vec, SECOND)
        vo = join(vo, send(vo, FIRST), 2, place.first).reshape(4, 2, 48, D)
        inn = join(inn, send(inn, NEAR_Z), 1, place.near_z)
        far, other, vec, vo, inn = together(far, other, vec, vo, inn)
        qk_parts = (qk, far, other, send(far, CORE))
        vec = vec + send(vec, CORE)
        qk_parts, vec, vo, inn, w_outer = together(qk_parts, vec, vo, inn, w_outer)
        vo_far = send(vo, SECOND)
        other = send(vo, CORE)
        inn = join(inn, send(inn, FIRST), 2, place.first).reshape(4, 2, 24, FF)
        out = join(w_outer, send(w_outer, FAR_Z), 0, place.far_z)
        queries, keys, qk = project(x, vec, qk_parts, 2, (B_QUERY, None), cube)
        queries, vo_far, other, inn, out = together(queries, vo_far, other, inn, out)
        vo_parts = (vo, vo_far, other, send(vo_far, CORE))
        inn_far = send(inn, SECOND)
        values, vo = project(x, vec, vo_parts, 2, (B_VALUE,), cube)
        values, out = together(values, out)
        out = join(out, send(out, NEAR_Z), 1, place.near_z)
        probs, context = attend(lengths, queries, keys, values)
        context, inn, inn_far, out = together(context, inn, inn_far, out)
        inn_parts = (inn, inn_far, send(inn, CORE), send(inn_far, CORE))
        out = join(out, send(out, FIRST), 2, place.first).reshape(4, 2, 96, D)
        hat1, inv1, normed = close(x, context, vo, vec)
        normed, inn_parts, out = together(normed, inn_parts, out)
        out_far = send(out, SECOND)
        other = send(out, CORE)
        act, slope, inner_mat = inner(normed, vec, inn_parts, cube)
        act, out_far, other = together(act, out_far, other)
        out_parts = (out, out_far, other, send(out_far, CORE))
        block_out, hat2, inv2, cls, unit, outer_mat = outer(act, hat1, vec, out_parts, cube)
        near = spread(unit, place).reshape(4, 2, *unit.shape)
        far = send(near, SECOND)
        loss, d_cls = pair_loss((near, far, send(near, CORE), send(far, CORE)), vec, cls)
        dres, dbr, sums, *shares = outer_back(
            out_cotangent.reshape(count * LEN, D), d_cls, hat2, inv2, act, vec, cube
        )
        o = Reduction(shares, place)
        dbr, o.away = together(dbr, o.away)
        o.start(CORE)
        dh, sums, *shares = inner_back(dbr, normed, slope, outer_mat, sums, cube)
        i = Reduction(shares, place, early_z=True)
        dh, i.away = arrive([o], dh, i.away)
        i.start(CORE)
        o.settle()
        o.start(FIRST)
        dh, dres = together(dh, dres)
        d_resid, d_attn, d_context, sums = open_back(dres, dh, inner_mat, hat1, inv1, vo, vec, sums)
        (d_context,) = arrive([o, i], d_context)
        o.settle()
        o.start(SECOND)
        i.settle()
        i.start(NEAR_Z)
        d_queries, d_keys, d_values, *shares = heads_back(
            queries, keys, values, d_context, probs, x, sums, context, d_attn, cube
        )
        a = Reduction(shares, place)
        d_queries, a.away = arrive([o, i], d_queries, a.away)
        a.start(CORE)
        o.settle()
        i.settle()
        o.away, i.away = arrive([a], o.away, i.away)
        a.settle()
        a.start(FIRST)
        o.start(NEAR_Z)
        i.start(FIRST)
        grad_rows = token_grad(d_resid, d_queries, d_keys, d_values, qk, vo)
        (grad_rows,) = arrive([o, i, a], grad_rows)
        a.settle()
        a.start(SECOND)
        o.settle()
        o.start(FAR_Z)
        i.settle()
        i.start(SECOND)
        arrive([i, a])
        a.settle()
        a.start(NEAR_Z)
        i.settle()
        i.start(FAR_Z)
        grad_w_outer = o.total()
        (grad_w_outer,) = arrive([a], grad_w_outer)
        a.settle()
        a.start(FAR_Z)
        grad_w_inner = i.total()
        g_attn = a.total()
        g_mats = [g_attn[24 * n : 24 * (n + 1)] for n in range(4)]
        small, inner_part = g_attn[96:, D - WIDE :], g_attn[96, D - WIDE // 2 :]
        grads = [small[n, : D // CUBE] for n in range(B_INNER)] + [inner_part[: FF // CUBE]]
    else:
        rows = [every(v).reshape(-1, D) for v in vectors]
        vec = jnp.concatenate(rows + [jnp.zeros((4, D), low)], axis=0)
        qk_parts, vo_parts = ((jnp.stack([every(w) for w in ws]),) for ws in ((w_query, w_key), (w_value, w_output)))
        queries, keys, qk = project(x, vec, qk_parts, 2, (B_QUERY, None), cube)
        values, vo = project(x, vec, vo_parts, 2, (B_VALUE,), cube)
        probs, context = attend(lengths, queries, keys, values)
        hat1, inv1, normed = close(x, context, vo, vec)
        act, slope, inner_mat = inner(normed, vec, (every(w_inner),), cube)
        block_out, hat2, inv2, cls, unit, outer_mat = outer(act, hat1, vec, (every(w_outer),), cube)
        loss, d_cls = plain_loss(every(unit), every(partners), cls)
        dres, dbr, sums, d_outer = outer_back(
            out_cotangent.reshape(count * LEN, D), d_cls, hat2, inv2, act, vec, cube
        )
        dh, sums, d_inner = inner_back(dbr, normed, slope, outer_mat, sums, cube)
        d_resid, d_attn, d_context, sums = open_back(dres, dh, inner_mat, hat1, inv1, vo, vec, sums)
        d_queries, d_keys, d_values, sums, d_mats = heads_back(
            queries, keys, values, d_context, probs, x, sums, context, d_attn, cube
        )
        grad_rows = token_grad(d_resid, d_queries, d_keys, d_values, qk, vo)
        grad_w_outer, grad_w_inner = scatter(d_outer), scatter(d_inner)
        g_mats = [scatter(d_mats[n]) for n in range(4)]
        grads = [scatter(sums[n]) for n in range(B_INNER)] + [scatter(sums[B_INNER:CODES].reshape(-1))]
    (
        grad_b_query,
        grad_b_value,
        grad_b_output,
        grad_gain_attn,
        grad_shift_attn,
        grad_b_outer,
        grad_gain_ffn,
        grad_shift_ffn,
        grad_b_inner,
    ) = grads
    return (
        loss,
        block_out.reshape(count, LEN, D),
        grad_rows.reshape(count, LEN, D),
        g_mats[0],
        g_mats[1],
        g_mats[2],
        g_mats[3],
        grad_b_query,
        grad_b_value,
        grad_b_output,
        grad_gain_attn,
        grad_shift_attn,
        grad_w_inner,
        grad_b_inner,
        grad_w_outer,
        grad_b_outer,
        grad_gain_ffn,
        grad_shift_ffn,
    )


def solution(mesh):
    rows, cols = P(AXIS), P(AXIS, None)
    cube = P(AXIS, None, None)
    in_specs = (cube, rows, rows, cube) + (cols,) * 4 + (rows,) * 5 + (cols, rows, cols) + (rows,) * 3
    out_specs = (P(), cube, cube) + (cols,) * 4 + (rows,) * 5 + (cols, rows, cols) + (rows,) * 3
    return jax.shard_map(local, mesh=mesh, in_specs=in_specs, out_specs=out_specs, check_vma=False)
```

```python
import jax
import jax.numpy as jnp
from jax import lax
from jax.experimental import pallas as pl
from jax.experimental.pallas import tpu as pltpu
from jax.sharding import PartitionSpec as P

D = 768
HEADS = 12
HEAD_DIM = 64
LEN = 64
FF = 3072
QUAD = 4
WIDE = QUAD * HEAD_DIM
GROUPS = HEADS // QUAD
ROWS = 256
BLOCK = 768
AXIS = "fsdp"
CUBE = 32
norm_eps = 1e-12
pool_eps = 1e-06
sim_scale = 50.0
sim_margin = 0.3
f32, low = jnp.float32, jnp.bfloat16
S = jax.ShapeDtypeStruct

B_QUERY, B_VALUE, B_OUTPUT, G_ATTN, S_ATTN, B_OUTER, G_FFN, S_FFN, B_INNER = range(9)
CODES = B_INNER + FF // D


def nn(a, b):
    return lax.dot_general(a, b, (((1,), (0,)), ((), ())), preferred_element_type=f32)


def nt(a, b):
    return lax.dot_general(a, b, (((1,), (1,)), ((), ())), preferred_element_type=f32)


def tn(a, b):
    return lax.dot_general(a, b, (((0,), (0,)), ((), ())), preferred_element_type=f32)


def whole(shape):
    return pl.BlockSpec(shape, lambda *_: (0,) * len(shape), pipeline_mode=pl.Buffered(1))


def row_block(width, rows=ROWS):
    return pl.BlockSpec((rows, width), lambda i, *_: (i, 0))


def params(flops, nbytes, exps=0, room=60):
    return dict(
        compiler_params=pltpu.CompilerParams(vmem_limit_bytes=room << 20),
        cost_estimate=pl.CostEstimate(flops=int(flops), bytes_accessed=int(nbytes), transcendentals=int(exps)),
    )


ANY = pl.BlockSpec(memory_space=pl.ANY)


def part_copies(parts, target, sems, cut):
    me = lax.axis_index(AXIS)
    core, x, y = me & 1, (me >> 1) & 1, (me >> 2) & 1

    def start(zero, one):
        for i in range(2):
            pltpu.make_async_copy(cut(zero[i]), target.at[:, (y + i) & 1, :, 0], sems.at[2 * i]).start()
            pltpu.make_async_copy(cut(one[i]), target.at[:, :, (x + i) & 1, 1], sems.at[2 * i + 1]).start()

    @pl.when(core == 0)
    def _():
        start(parts[:2], parts[2:])

    @pl.when(core == 1)
    def _():
        start(parts[2:], parts[:2])


def part_waits(parts, target, sems, cut):
    for i in range(2):
        pltpu.make_async_copy(cut(parts[i]), target.at[:, i, :, 0], sems.at[2 * i]).wait()
        pltpu.make_async_copy(cut(parts[i]), target.at[:, :, i, 1], sems.at[2 * i + 1]).wait()


def everything(ref):
    return ref


def project_body(cube, count, biases, x_ref, vec_ref, *refs):
    outs = len(biases)
    parts, out_refs, (full_ref, w_ref, sems, out_sem) = refs[: -outs - 4], refs[-outs - 4 : -4], refs[-4:]
    step = pl.program_id(0)
    onward = pltpu.make_async_copy(w_ref, full_ref, out_sem)

    @pl.when(step == 0)
    def _():
        if cube:

            def cut(m):
                return lambda ref: ref.at[:, :, pl.ds(m * 24, 24), :]

            for m in range(count):
                part_copies(parts, w_ref.at[m], sems.at[m], cut(m))
            for m in range(count):
                part_waits(parts, w_ref.at[m], sems.at[m], cut(m))
        else:
            copy = pltpu.make_async_copy(parts[0], w_ref, sems.at[0, 0])
            copy.start()
            copy.wait()
        onward.start()

    x = x_ref[...]
    for m, (bias, out) in enumerate(zip(biases, out_refs)):
        product = nn(x, w_ref.at[m].reshape(D, D)[...] if cube else w_ref[m])
        if bias is not None:
            product += vec_ref[bias : bias + 1].astype(f32)
        out[...] = product.astype(low)

    @pl.when(step == pl.num_programs(0) - 1)
    def _():
        onward.wait()


def project(x, vec, parts, count, biases, cube):
    t = x.shape[0]
    shape = (count, 4, 2, 2, 2, 24, D) if cube else (count, D, D)
    outs = len(biases)
    *products, full = pl.pallas_call(
        lambda *refs: project_body(cube, count, biases, *refs),
        grid=(t // (2 * ROWS),),
        in_specs=[row_block(D, 2 * ROWS), whole(vec.shape)] + [ANY] * len(parts),
        out_specs=[row_block(D, 2 * ROWS)] * outs + [ANY],
        out_shape=[S((t, D), low)] * outs + [S(shape, low)],
        scratch_shapes=[pltpu.VMEM(shape, low), pltpu.SemaphoreType.DMA((count, 4)), pltpu.SemaphoreType.DMA],
        name="project",
        **params(2 * outs * t * D * D, 2 * (outs + 1) * t * D + 4 * count * D * D, room=16),
    )(x, vec, *parts)
    return *products, full.reshape(count, D, D)


def assemble(cube, parts, w_ref, full_ref, sems, out_sem):
    onward = pltpu.make_async_copy(w_ref, full_ref, out_sem)

    @pl.when(pl.program_id(0) == 0)
    def _():
        if cube:
            part_copies(parts, w_ref, sems, everything)
            part_waits(parts, w_ref, sems, everything)
        else:
            copy = pltpu.make_async_copy(parts[0], w_ref, sems.at[0])
            copy.start()
            copy.wait()
        onward.start()

    return onward


def scratch_for(shape):
    return [pltpu.VMEM(shape, low), pltpu.SemaphoreType.DMA((4,)), pltpu.SemaphoreType.DMA]


def head_masks(dtype):
    lane = lax.broadcasted_iota(jnp.int32, (1, WIDE), 1) // HEAD_DIM
    return [jnp.where(lane == h, 1.0, 0.0).astype(dtype) for h in range(QUAD)]


def stacked(rows, masks):
    return jnp.concatenate([rows * m for m in masks], axis=0)


def unstacked(full, masks):
    return sum(full[LEN * h : LEN * (h + 1)] * m for h, m in enumerate(masks))


def layer_norm(resid):
    centred = resid - jnp.mean(resid, axis=-1, keepdims=True)
    inv = lax.rsqrt(jnp.mean(centred * centred, axis=-1, keepdims=True) + norm_eps)
    return centred * inv, inv


def layer_norm_back(grad, gain, hat, inv):
    grad = grad * gain
    mean = jnp.mean(grad, axis=-1, keepdims=True)
    along = jnp.mean(grad * hat, axis=-1, keepdims=True)
    return (grad - mean - hat * along) * inv


def attend_body(len_ref, q_ref, k_ref, v_ref, p_ref, c_ref):
    masks, masks32 = head_masks(low), head_masks(f32)
    per = q_ref.shape[0] // LEN
    first = pl.program_id(0) * per
    key_at = lax.broadcasted_iota(jnp.int32, (LEN, WIDE), 0)

    def sentence(s):
        rows = pl.ds(pl.multiple_of(s * LEN, LEN), LEN)
        seen = key_at < len_ref[first + s]
        for g in range(GROUPS):
            cols = pl.ds(g * WIDE, WIDE)
            q, k, v = q_ref[rows, cols], k_ref[rows, cols], v_ref[rows, cols]
            scores = nt(k, stacked(q, masks)) * HEAD_DIM ** (-0.5)
            scores = jnp.where(seen, scores, -1e30)
            expd = jnp.exp(scores - jnp.max(scores, axis=0, keepdims=True))
            probs = expd * (1.0 / jnp.sum(expd, axis=0, keepdims=True))
            p_ref[g, rows, :] = probs
            c_ref[rows, cols] = unstacked(tn(probs.astype(low), v), masks32).astype(low)

    pl.loop(0, per, unroll=UNROLL)(sentence)


UNROLL = 8


def mat_of(m):
    return pl.BlockSpec((1, D, D), lambda *_: (m, 0, 0), pipeline_mode=pl.Buffered(1))


def attend(lengths, q, k, v):
    t = q.shape[0]
    rows = row_block(D, 2 * ROWS)
    return pl.pallas_call(
        attend_body,
        grid_spec=pltpu.PrefetchScalarGridSpec(
            num_scalar_prefetch=1,
            grid=(t // (2 * ROWS),),
            in_specs=[rows] * 3,
            out_specs=[pl.BlockSpec((GROUPS, 2 * ROWS, WIDE), lambda i, *_: (0, i, 0)), rows],
        ),
        out_shape=[S((GROUPS, t, WIDE), f32), S((t, D), low)],
        name="attend",
        **params(10 * t * D * D, 20 * t * D, t * D, room=60),
    )(lengths, q, k, v)


def halves(ref):
    return [slice(i * ROWS, (i + 1) * ROWS) for i in range(ref.shape[0] // ROWS)]


def close_body(x_ref, c_ref, w_ref, vec_ref, hat_ref, inv_ref, n_ref):
    w = w_ref[0]
    branches = [nn(c_ref[r, :], w) + vec_ref[B_OUTPUT : B_OUTPUT + 1].astype(f32) for r in halves(x_ref)]
    for r, branch in zip(halves(x_ref), branches):
        hat, inv = layer_norm(x_ref[r, :].astype(f32) + branch)
        hat_ref[r, :] = hat
        inv_ref[r, :] = inv
        n_ref[r, :] = (hat * vec_ref[G_ATTN : G_ATTN + 1].astype(f32) + vec_ref[S_ATTN : S_ATTN + 1].astype(f32)).astype(low)


def close(x, c, full, vec):
    t = x.shape[0]
    rows = row_block(D, 2 * ROWS)
    return pl.pallas_call(
        close_body,
        grid=(t // (2 * ROWS),),
        in_specs=[rows, rows, mat_of(1), whole(vec.shape)],
        out_specs=[rows, row_block(1, 2 * ROWS), rows],
        out_shape=[S((t, D), f32), S((t, 1), f32), S((t, D), low)],
        name="close",
        **params(2 * t * D * D, 10 * t * D + 2 * D * D, room=60),
    )(x, c, full, vec)


def open_back_body(dres_ref, dh_ref, wi_ref, hat_ref, inv_ref, wo_ref, vec_ref, before_ref, dr_ref, da_ref, dc_ref, sums_ref):
    @pl.when(pl.program_id(0) == 0)
    def _():
        sums_ref[...] = before_ref[...]

    grads = [dres_ref[r, :] + nt(dh_ref[r, :], wi_ref[...]) for r in halves(dres_ref)]
    for r, dn in zip(halves(dres_ref), grads):
        hat = hat_ref[r, :]
        dres = layer_norm_back(dn, vec_ref[G_ATTN : G_ATTN + 1].astype(f32), hat, inv_ref[r, :])
        dr_ref[r, :] = dres
        dao = dres.astype(low)
        da_ref[r, :] = dao
        dc_ref[r, :] = nt(dao, wo_ref[0]).astype(low)
        sums_ref[B_OUTPUT : B_OUTPUT + 1] += jnp.sum(dao.astype(f32), axis=0, keepdims=True)
        sums_ref[G_ATTN : G_ATTN + 1] += jnp.sum(dn * hat, axis=0, keepdims=True)
        sums_ref[S_ATTN : S_ATTN + 1] += jnp.sum(dn, axis=0, keepdims=True)


def open_back(dres, dh, wi, hat, inv, full, vec, sums):
    t = dres.shape[0]
    return pl.pallas_call(
        open_back_body,
        grid=(t // (2 * ROWS),),
        in_specs=[row_block(D, 2 * ROWS), row_block(FF, 2 * ROWS), whole(wi.shape), row_block(D, 2 * ROWS), row_block(1, 2 * ROWS), mat_of(1), whole(vec.shape), whole((16, D))],
        out_specs=[row_block(D, 2 * ROWS)] * 3 + [whole((16, D))],
        out_shape=[S((t, D), f32), S((t, D), low), S((t, D), low), S((16, D), f32)],
        name="open_back",
        **params(10 * t * D * D, 20 * t * D + 10 * D * D, room=60),
    )(dres, dh, wi, hat, inv, full, vec, sums)


def device_rows(table):
    rows = 8 * CUBE
    row, lane = (lax.broadcasted_iota(jnp.int32, (rows, D), axis) for axis in range(2))
    out = []
    for values, r in (
        (jnp.concatenate([table[:8]] * CUBE, axis=0), D // CUBE),
        (jnp.concatenate([jnp.broadcast_to(table[B_INNER + j : B_INNER + j + 1], (rows * D // FF, D)) for j in range(FF // D)], axis=0), FF // CUBE),
    ):
        own = jnp.where(lane // r == (row // 8) % (D // r), values, 0.0).astype(low)
        at, to = (lax.broadcasted_iota(jnp.int32, (D, WIDE // 2), axis) for axis in range(2))
        out.append(nn(own, jnp.where(at % r == to, 1.0, 0.0).astype(low)))
    return jnp.concatenate(out, axis=1)


def heads_back_body(cube, q_ref, k_ref, v_ref, dc_ref, p_ref, x_ref, before_ref, c_ref, da_ref, *refs):
    dq_ref, dk_ref, dv_ref, *shares = refs[:-1]
    table_ref = refs[-1]
    step = pl.program_id(0)
    masks, masks32 = head_masks(low), head_masks(f32)

    def sentence(s):
        rows = pl.ds(pl.multiple_of(s * LEN, LEN), LEN)
        q, k, v, dc, p = q_ref[rows, :], k_ref[rows, :], v_ref[rows, :], dc_ref[rows, :], p_ref[0, rows, :]
        dcs = stacked(dc, masks)
        dp = nt(v, dcs)
        dv_ref[rows, :] = nn(p.astype(low), dcs).astype(low)
        ds = (p * (dp - jnp.sum(p * dp, axis=0, keepdims=True))).astype(low)
        dk_ref[rows, :] = (nn(ds, stacked(q, masks)) * HEAD_DIM ** (-0.5)).astype(low)
        dq_ref[rows, :] = (unstacked(tn(ds, k), masks32) * HEAD_DIM ** (-0.5)).astype(low)

    @pl.when(step == 0)
    def _():
        table_ref[...] = before_ref[...]

    pl.loop(0, q_ref.shape[0] // LEN, unroll=BACK_UNROLL)(sentence)
    cols = pl.ds(pl.multiple_of(step * WIDE, WIDE), WIDE)
    table_ref[B_QUERY : B_QUERY + 1, cols] = jnp.sum(dq_ref[...].astype(f32), axis=0, keepdims=True)
    table_ref[B_VALUE : B_VALUE + 1, cols] = jnp.sum(dv_ref[...].astype(f32), axis=0, keepdims=True)
    for m, (rows, grad) in enumerate(((x_ref, dq_ref), (x_ref, dk_ref), (x_ref, dv_ref), (c_ref, da_ref))):
        full = tn(rows[...], grad[...])
        if cube:
            full = full.reshape(4, 2, 2, 2, 24, WIDE)

            def put(ref, p, q, value, m=m):
                ref[:, p, q, 24 * m : 24 * (m + 1)] = value.astype(ref.dtype)

            write_shares(lambda y, x, c: full[:, y, x, c], *shares, put)
        else:
            shares[1][m] = full
    if cube:

        def put_rows(ref, p, q, value):
            ref[:, p, q, 96:] = value.astype(ref.dtype)

        @pl.when(step < GROUPS - 1)
        def _():
            write_shares(lambda y, x, c: jnp.zeros((4, 8, WIDE), f32), *shares, put_rows)

        @pl.when(step == GROUPS - 1)
        def _():
            values = device_rows(table_ref[...]).reshape(4, 2, 2, 2, 8, WIDE)
            write_shares(lambda y, x, c: values[:, y, x, c], *shares, put_rows)
    else:
        shares[0][...] = table_ref[...]


BACK_UNROLL = 16


def heads_back(q, k, v, dc, p, x, sums, c, da, cube):
    t = q.shape[0]
    col = pl.BlockSpec((t, WIDE), lambda i: (0, i))
    if cube:
        spec = pl.BlockSpec((4, 2, 2, 104, WIDE), lambda i: (0, 0, 0, 0, i))
        shape = (4, 2, 2, 104, D)
        specs, shapes = [spec] * 2, [S(shape, KEEP), S(shape, low)]
    else:
        specs = [whole((16, D)), pl.BlockSpec((4, D, WIDE), lambda i: (0, 0, i))]
        shapes = [S((16, D), f32), S((4, D, D), f32)]
    return pl.pallas_call(
        lambda *refs: heads_back_body(cube, *refs),
        grid=(GROUPS,),
        in_specs=[col] * 4
        + [pl.BlockSpec((1, t, WIDE), lambda i: (i, 0, 0)), whole((t, D)), whole((16, D)), whole((t, D)), col],
        out_specs=[col] * 3 + specs,
        out_shape=[S((t, D), low)] * 3 + shapes,
        scratch_shapes=[pltpu.VMEM((16, D), f32)],
        name="heads_back",
        **params(t * D * 24000, t * D * 20, room=60),
    )(q, k, v, dc, p, x, sums, c, da)


def gelu_parts(h):
    d = 1.0 + (0.3275911 * 0.7071067811865476) * jnp.abs(h)
    t = pl.reciprocal(d, approx=True)
    t = t * (2.0 - d * t)
    poly = t * (0.127414796 + t * (-0.142248368 + t * (0.7107068705 + t * (-0.7265760135 + t * 0.5307027145))))
    bell = jnp.exp(-0.5 * (h * h))
    tail = poly * bell
    cdf = jnp.where(h >= 0, 1.0 - tail, tail)
    return h * cdf, cdf + h * (bell * 0.3989422804014327)


def inner_body(cube, n_ref, vec_ref, *refs):
    parts, (a_ref, gp_ref, full_ref, w_ref, sems, out_sem, bias_ref) = refs[:-7], refs[-7:]
    onward = assemble(cube, parts, w_ref, full_ref, sems, out_sem)

    @pl.when(pl.program_id(0) == 0)
    def _():
        bias_ref[...] = vec_ref[...].astype(f32)

    w = w_ref.reshape(D, FF) if cube else w_ref

    @pl.loop(0, FF // BLOCK)
    def _(j):
        cols = pl.ds(pl.multiple_of(j * BLOCK, BLOCK), BLOCK)
        h = nn(n_ref[...], w[:, cols]) + bias_ref[pl.ds(B_INNER + j, 1), :]
        act, slope = gelu_parts(h)
        a_ref[:, cols] = act.astype(low)
        gp_ref[:, cols] = slope.astype(low)

    @pl.when(pl.program_id(0) == pl.num_programs(0) - 1)
    def _():
        onward.wait()


def inner(n, vec, parts, cube):
    t = n.shape[0]
    shape = (4, 2, 2, 2, 24, FF) if cube else (D, FF)
    act, slope, full = pl.pallas_call(
        lambda *refs: inner_body(cube, *refs),
        grid=(t // ROWS,),
        in_specs=[row_block(D), whole(vec.shape)] + [ANY] * len(parts),
        out_specs=[row_block(FF), row_block(FF), ANY],
        out_shape=[S((t, FF), low), S((t, FF), low), S(shape, low)],
        scratch_shapes=[*scratch_for(shape), pltpu.VMEM((16, D), f32)],
        name="inner",
        **params(6 * t * D * FF, 2 * t * D + 4 * t * FF + 4 * D * FF, 2 * t * FF, room=60),
    )(n, vec, *parts)
    return act, slope, full.reshape(D, FF)


def outer_body(cube, a_ref, hat_ref, vec_ref, *refs):
    parts = refs[:-9]
    out_ref, hat2_ref, inv_ref, cls_ref, unit_ref, full_ref, w_ref, sems, out_sem = refs[-9:]
    onward = assemble(cube, parts, w_ref, full_ref, sems, out_sem)
    step = pl.program_id(0)
    w = w_ref.reshape(FF, D) if cube else w_ref
    branch = nn(a_ref[...], w[...]) + vec_ref[B_OUTER : B_OUTER + 1].astype(f32)
    normed = hat_ref[...] * vec_ref[G_ATTN : G_ATTN + 1].astype(f32) + vec_ref[S_ATTN : S_ATTN + 1].astype(f32)
    hat, inv = layer_norm(normed + branch)
    hat2_ref[...] = hat
    inv_ref[...] = inv
    rows = hat * vec_ref[G_FFN : G_FFN + 1].astype(f32) + vec_ref[S_FFN : S_FFN + 1].astype(f32)
    out_ref[...] = rows.astype(low)
    pairs = rows.shape[0] // LEN // 2
    for s in range(pairs):
        at = pl.ds(step * pairs + s, 1)
        for side in range(2):
            cols = pl.ds(side * D, D)
            cls = rows[LEN * (2 * s + side) : LEN * (2 * s + side) + 1]
            cls_ref[at, cols] = cls

    @pl.when(step == pl.num_programs(0) - 1)
    def _():
        for side in range(2):
            cls = cls_ref[:, side * D : (side + 1) * D]
            unit = cls * lax.rsqrt(jnp.sum(cls * cls, axis=-1, keepdims=True) + pool_eps)
            unit_ref[:, side * D : (side + 1) * D] = unit.astype(low)
        onward.wait()


def outer(act, hat, vec, parts, cube):
    t = hat.shape[0]
    shape = (4, 2, 2, 2, 96, D) if cube else (FF, D)
    pairs = t // LEN // 2
    once = pl.BlockSpec((pairs, 2 * D), lambda i: (0, 0))
    *outs, full = pl.pallas_call(
        lambda *refs: outer_body(cube, *refs),
        grid=(t // ROWS,),
        in_specs=[row_block(FF), row_block(D), whole(vec.shape)] + [ANY] * len(parts),
        out_specs=[row_block(D), row_block(D), row_block(1), once, once, ANY],
        out_shape=[S((t, D), low), S((t, D), f32), S((t, 1), f32), S((pairs, 2 * D), f32), S((pairs, 2 * D), low), S(shape, low)],
        scratch_shapes=[pltpu.VMEM(shape, low), pltpu.SemaphoreType.DMA((4,)), pltpu.SemaphoreType.DMA],
        name="outer",
        **params(2 * t * D * FF, 10 * t * D + 2 * t * FF + 4 * D * FF, room=60),
    )(act, hat, vec, *parts)
    return *outs, full.reshape(FF, D)


def write_shares(full, keep_ref, away_ref, put):
    core = lax.axis_index(AXIS) & 1

    def write(zero, one):
        for y in range(2):
            for x in range(2):
                put(zero, x, y, full(y, x, 0))
                put(one, y, x, full(y, x, 1))

    @pl.when(core == 0)
    def _():
        write(keep_ref, away_ref)

    @pl.when(core == 1)
    def _():
        write(away_ref, keep_ref)


def outer_back_body(cube, cot_ref, dc_ref, hat2_ref, inv2_ref, a_ref, vec_ref, dres_ref, dbr_ref, sums_ref, *refs):
    j = pl.program_id(0)

    def write(dw):
        if cube:
            dw = dw.reshape(2, 2, 2, 96, D)

            def put(ref, p, q, value):
                ref[0, p, q] = value.astype(ref.dtype)

            write_shares(lambda y, x, c: dw[y, x, c], *refs, put)
        else:
            refs[0][...] = dw

    @pl.when(j == 0)
    def _():
        dw = jnp.zeros((BLOCK, D), f32)
        dgain = jnp.zeros((1, D), f32)
        dshift = jnp.zeros((1, D), f32)
        dbias = jnp.zeros((1, D), f32)
        at = lax.broadcasted_iota(jnp.int32, (ROWS, D), 0)
        for b in range(cot_ref.shape[0] // ROWS):
            rows = pl.ds(b * ROWS, ROWS)
            d = cot_ref[rows, :].astype(f32)
            hat = hat2_ref[rows, :]
            for s in range(ROWS // LEN):
                whose = b * (ROWS // LEN) + s
                extra = dc_ref[whose // 2 : whose // 2 + 1, (whose % 2) * D : (whose % 2 + 1) * D]
                d += jnp.where(at == LEN * s, extra, 0.0)
            dgain += jnp.sum(d * hat, axis=0, keepdims=True)
            dshift += jnp.sum(d, axis=0, keepdims=True)
            dres = layer_norm_back(d, vec_ref[G_FFN : G_FFN + 1].astype(f32), hat, inv2_ref[rows, :])
            dres_ref[rows, :] = dres
            dbr = dres.astype(low)
            dbr_ref[rows, :] = dbr
            dbias += jnp.sum(dbr.astype(f32), axis=0, keepdims=True)
            dw += tn(a_ref[rows, :], dbr)
        write(dw)
        sums_ref[...] = jnp.zeros_like(sums_ref)
        sums_ref[B_OUTER : B_OUTER + 1] = dbias
        sums_ref[G_FFN : G_FFN + 1] = dgain
        sums_ref[S_FFN : S_FFN + 1] = dshift

    @pl.when(j > 0)
    def _():
        write(tn(a_ref[...], dbr_ref[...]))


def outer_back(cot, dc, hat2, inv2, a, vec, cube):
    t = cot.shape[0]
    if cube:
        spec = pl.BlockSpec((1, 2, 2, 96, D), lambda j: (j, 0, 0, 0, 0))
        specs, shapes = [spec] * 2, [S((4, 2, 2, 96, D), KEEP), S((4, 2, 2, 96, D), low)]
    else:
        specs, shapes = [pl.BlockSpec((BLOCK, D), lambda j: (j, 0))], [S((FF, D), f32)]
    return pl.pallas_call(
        lambda *refs: outer_back_body(cube, *refs),
        grid=(FF // BLOCK,),
        in_specs=[whole((t, D)), whole(dc.shape), whole((t, D)), whole((t, 1)), pl.BlockSpec((t, BLOCK), lambda j: (0, j)),
                  whole(vec.shape)],
        out_specs=[whole((t, D)), whole((t, D)), whole((16, D))] + specs,
        out_shape=[S((t, D), f32), S((t, D), low), S((16, D), f32)] + shapes,
        name="outer_back",
        **params(4 * t * D * FF, 14 * t * D + 2 * t * FF + 8 * D * FF, room=60),
    )(cot, dc, hat2, inv2, a, vec)


def inner_back_body(cube, dbr_ref, n_ref, gp_ref, wo_ref, before_ref, dh_ref, sums_ref, *refs):
    @pl.when(pl.program_id(0) == 0)
    def _():
        sums_ref[...] = before_ref[...]

    dh = (gp_ref[...].astype(f32) * nt(dbr_ref[...], wo_ref[...])).astype(low)
    dh_ref[...] = dh
    sums_ref[pl.ds(B_INNER + pl.program_id(0), 1), :] = jnp.sum(dh.astype(f32), axis=0, keepdims=True)
    dw = tn(n_ref[...], dh)
    if cube:
        dw = dw.reshape(4, 2, 2, 2, 24, BLOCK)

        def put(ref, p, q, value):
            ref[:, p, q] = value.astype(ref.dtype)

        write_shares(lambda y, x, c: dw[:, y, x, c], *refs, put)
    else:
        refs[0][...] = dw


def inner_back(dbr, n, gp, wo, sums, cube):
    t = n.shape[0]
    fblk = pl.BlockSpec((t, BLOCK), lambda j: (0, j))
    if cube:
        spec = pl.BlockSpec((4, 2, 2, 24, BLOCK), lambda j: (0, 0, 0, 0, j))
        specs, shapes = [spec] * 2, [S((4, 2, 2, 24, FF), KEEP), S((4, 2, 2, 24, FF), low)]
    else:
        specs, shapes = [pl.BlockSpec((D, BLOCK), lambda j: (0, j))], [S((D, FF), f32)]
    return pl.pallas_call(
        lambda *refs: inner_back_body(cube, *refs),
        grid=(FF // BLOCK,),
        in_specs=[whole((t, D)), whole((t, D)), fblk, pl.BlockSpec((BLOCK, D), lambda j: (j, 0)), whole((16, D))],
        out_specs=[fblk, whole((16, D))] + specs,
        out_shape=[S((t, FF), low), S((16, D), f32)] + shapes,
        name="inner_back",
        **params(4 * t * D * FF, 4 * t * D + 4 * t * FF + 8 * D * FF, room=60),
    )(dbr, n, gp, wo, sums)


KEEP = low


def token_grad_body(dr_ref, dq_ref, dk_ref, dv_ref, wq_ref, wk_ref, wv_ref, o_ref):
    o_ref[...] = (
        dr_ref[...] + nt(dq_ref[...], wq_ref[0]) + nt(dk_ref[...], wk_ref[0]) + nt(dv_ref[...], wv_ref[0])
    )


def token_grad(dr, dq, dk, dv, qk, vo):
    t = dr.shape[0]

    return pl.pallas_call(
        token_grad_body,
        grid=(t // ROWS,),
        in_specs=[row_block(D)] * 4 + [mat_of(0), mat_of(1), mat_of(0)],
        out_specs=row_block(D),
        out_shape=S((t, D), f32),
        name="token_grad",
        **params(6 * t * D * D, 14 * t * D + 6 * D * D, room=60),
    )(dr, dq, dk, dv, qk, qk, vo)


def loss_body(near, far, near_other, far_other, codes_ref, cls_ref, loss_ref, dc_ref, table_ref, ds_ref, units_ref, sems):
    parts = (near, far, near_other, far_other)
    part_copies(parts, units_ref, sems, everything)
    part_waits(parts, units_ref, sems, everything)
    own = cls_ref.shape[0]
    pairs = CUBE * own
    units = units_ref.reshape(pairs, 2 * D)
    sources, targets = units[:, :D], units[:, D:]
    codes = codes_ref[CODES : CODES + 2, :pairs].astype(f32)
    partner = (codes[0:1] + 64.0 * codes[1:2]).astype(jnp.int32)
    matched = lax.broadcasted_iota(jnp.int32, (pairs, pairs), 0) == partner
    sims = nt(targets, sources) * sim_scale - jnp.where(matched, sim_scale * sim_margin, 0.0)
    row_top = jnp.max(sims, axis=0, keepdims=True)
    row_lse = row_top + jnp.log(jnp.sum(jnp.exp(sims - row_top), axis=0, keepdims=True))
    col_top = jnp.max(sims, axis=1, keepdims=True)
    col_lse = col_top + jnp.log(jnp.sum(jnp.exp(sims - col_top), axis=1, keepdims=True))
    total = (
        jnp.sum(row_lse, axis=1, keepdims=True)
        + jnp.sum(col_lse, axis=0, keepdims=True)
        - 2.0 * jnp.sum(jnp.sum(jnp.where(matched, sims, 0.0), axis=1, keepdims=True), axis=0, keepdims=True)
    )
    loss_ref[...] = jnp.broadcast_to(total * (0.5 / pairs), loss_ref.shape)
    d_sims = 0.5 * (jnp.exp(sims - row_lse) + jnp.exp(sims - col_lse)) - jnp.where(matched, 1.0, 0.0)
    d_low = (d_sims * sim_scale).astype(low)
    table_ref[...] = nn(d_low, sources)
    ds_ref[...] = tn(d_low, targets)
    mine = pl.ds(pl.multiple_of(lax.axis_index(AXIS) * own, own), own)
    for side, ref in enumerate((ds_ref, table_ref)):
        cols = pl.ds(side * D, D)
        cls, du = cls_ref[:, cols], ref[mine, :]
        inv = lax.rsqrt(jnp.sum(cls * cls, axis=-1, keepdims=True) + pool_eps)
        dc_ref[:, cols] = inv * du - cls * (inv * inv * inv * jnp.sum(du * cls, axis=-1, keepdims=True))


def pair_loss(parts, vec, cls):
    own = cls.shape[0]
    pairs = CUBE * own
    loss, dc = pl.pallas_call(
        loss_body,
        in_specs=[ANY] * 4 + [whole(vec.shape), whole(cls.shape)],
        out_specs=[whole((8, 128)), whole(cls.shape)],
        out_shape=[S((8, 128), f32), S(cls.shape, f32)],
        scratch_shapes=[pltpu.VMEM((pairs, D), f32), pltpu.VMEM((pairs, D), f32),
                        pltpu.VMEM((4, 2, 2, 2, own, 2 * D), low), pltpu.SemaphoreType.DMA((4,))],
        grid=(1,),
        name="pair_loss",
        **params(6 * pairs * pairs * D, 4 * pairs * D, 4 * pairs * pairs, room=12),
    )(*parts, vec, cls)
    return loss[0, 0], dc


CORE = [(i, i ^ 1) for i in range(CUBE)]
FAR_Z = [(i, i ^ 16) for i in range(CUBE)]
NEAR_Z = [(i, i ^ 8) for i in range(CUBE)]
FIRST = [(i, i ^ (4 if i & 1 else 2)) for i in range(CUBE)]
SECOND = [(i, i ^ (2 if i & 1 else 4)) for i in range(CUBE)]
ROUTES = (CORE, FIRST, SECOND, NEAR_Z, FAR_Z)


class Place:
    def __init__(self):
        self.me = lax.axis_index(AXIS)
        self.core = self.me & 1
        x, y = (self.me >> 1) & 1, (self.me >> 2) & 1
        self.near_z, self.far_z = (self.me >> 3) & 1, (self.me >> 4) & 1
        self.first = jnp.where(self.core == 0, x, y)
        self.second = jnp.where(self.core == 0, y, x)
        self.bits = [b.reshape(1) for b in (self.first, self.second, self.near_z, self.far_z)]


def join(own, other, axis, bit):
    shape = own.shape[:axis] + (2,) + own.shape[axis:]
    where = lax.broadcasted_iota(jnp.int32, shape, axis)
    return jnp.where(where == bit, jnp.expand_dims(own, axis), jnp.expand_dims(other, axis))


def pick(field, axis, bit):
    return lax.dynamic_index_in_dim(field, bit, axis, keepdims=False)


def send(field, route):
    return lax.ppermute(field, AXIS, route)


def spread(block, place):
    block = join(block, send(block, FAR_Z), 0, place.far_z)
    block = join(block, send(block, NEAR_Z), 1, place.near_z)
    return join(block, send(block, FIRST), 2, place.first)


def together(*values):
    return lax.optimization_barrier(values)


class Reduction:
    def __init__(self, shares, place, early_z=False):
        keep, self.away = shares
        self.terms = [keep.reshape(2, 2, *keep.shape[1:])]
        self.left = [(2, place.first), (2, place.second), (1, place.near_z), (0, place.far_z)]
        if early_z:
            self.left = [(1, place.near_z), (1, place.first), (1, place.second), (0, place.far_z)]
        self.came = None

    def start(self, route):
        self.came, self.away = send(self.away, route), None

    def settle(self):
        self.terms.append(self.came.reshape(self.terms[0].shape))
        axis, bit = self.left.pop(0)
        self.away = sum(pick(term, axis, 1 - bit).astype(f32) for term in self.terms).astype(low)
        self.terms = [pick(term, axis, bit) for term in self.terms]

    def total(self):
        return sum(term.astype(f32) for term in (*self.terms, self.came))


def arrive(sums, *values):
    done = together(*values, *[s.came for s in sums])
    for s, came in zip(sums, done[len(values) :]):
        s.came = came
    return done[: len(values)]


def spread_rows(rows, at, count):
    r = rows.shape[1]
    lane = lax.broadcasted_iota(jnp.int32, (r, D), 1)
    copies = nn(rows, jnp.where(lane % r == lax.broadcasted_iota(jnp.int32, (r, D), 0), 1.0, 0.0).astype(low))
    lane = lax.broadcasted_iota(jnp.int32, (count, D), 1)
    row = lax.broadcasted_iota(jnp.int32, (count, D), 0)
    return copies, lane // r, row


def vector_table(vectors, partners, place):
    *small, inner = vectors
    copies, lane, _ = spread_rows(jnp.stack(small), place.me, len(small))
    table = [jnp.where(lane == place.me, copies, 0.0)]
    fold = D // inner.shape[0]
    copies, lane, row = spread_rows(inner[None], place.me, FF // D)
    table.append(jnp.where((row == place.me // fold) & (lane == place.me % fold), copies, 0.0))
    codes = jnp.stack([partners % 64, partners // 64]).astype(low)
    copies, lane, _ = spread_rows(codes, place.me, 2)
    table.append(jnp.where(lane == place.me, copies, 0.0))
    table.append(jnp.zeros((2, D), f32))
    return jnp.concatenate(table, axis=0).astype(low)


def pack_body(*refs):
    *mats, out = refs
    r = mats[0].shape[0]
    for i, mat in enumerate(mats):
        out[i * r : (i + 1) * r, :] = mat[...]


def pack(*mats):
    r, n = mats[0].shape
    return pl.pallas_call(pack_body, out_shape=S((len(mats) * r, n), low), name="pack")(*mats)


def plain_loss(units, partners, cls):
    sources, targets = units[:, :D], units[:, D:]
    npairs, own = units.shape[0], cls.shape[0]
    sims = nt(sources, targets) * sim_scale
    matched = partners[:, None] == jnp.arange(npairs, dtype=jnp.int32)[None, :]
    sims = sims - jnp.where(matched, sim_scale * sim_margin, 0.0)
    row_top = jnp.max(sims, axis=1, keepdims=True)
    row_lse = row_top + jnp.log(jnp.sum(jnp.exp(sims - row_top), axis=1, keepdims=True))
    col_top = jnp.max(sims, axis=0, keepdims=True)
    col_lse = col_top + jnp.log(jnp.sum(jnp.exp(sims - col_top), axis=0, keepdims=True))
    positive = jnp.sum(jnp.where(matched, sims, 0.0))
    loss = (jnp.sum(row_lse) + jnp.sum(col_lse) - 2.0 * positive) / (2.0 * npairs)
    d_sims = 0.5 * (jnp.exp(sims - row_lse) + jnp.exp(sims - col_lse)) - jnp.where(matched, 1.0, 0.0)
    d_low = (d_sims * sim_scale).astype(low)
    first = lax.axis_index(AXIS) * own
    du = [
        nn(lax.dynamic_slice_in_dim(d_low, first, own, 0), targets),
        tn(lax.dynamic_slice_in_dim(d_low, first, own, 1), sources),
    ]
    dc = []
    for side in range(2):
        c = cls[:, side * D : (side + 1) * D]
        inv = lax.rsqrt(jnp.sum(c * c, axis=-1, keepdims=True) + pool_eps)
        dc.append(inv * du[side] - c * (inv * inv * inv * jnp.sum(du[side] * c, axis=-1, keepdims=True)))
    return loss, jnp.concatenate(dc, axis=1)


def every(v):
    return lax.all_gather(v, AXIS, axis=0, tiled=True)


def scatter(v):
    return lax.psum_scatter(v, AXIS, scatter_dimension=0, tiled=True)


def local(
    tokens,
    lengths,
    partners,
    out_cotangent,
    w_query,
    w_key,
    w_value,
    w_output,
    b_query,
    b_value,
    b_output,
    gain_attn,
    shift_attn,
    w_inner,
    b_inner,
    w_outer,
    b_outer,
    gain_ffn,
    shift_ffn,
):
    cube = lax.axis_size(AXIS) == CUBE
    count = tokens.shape[0]
    x = tokens.reshape(count * LEN, D)
    vectors = (b_query, b_value, b_output, gain_attn, shift_attn, b_outer, gain_ffn, shift_ffn, b_inner)
    if cube:
        place = Place()
        qk = pack(w_query, w_key)
        vo = pack(w_value, w_output)
        vec = vector_table(vectors, partners, place)
        qk = join(qk, send(qk, FAR_Z), 0, place.far_z)
        vec = vec + send(vec, FAR_Z)
        qk, vec, vo = together(qk, vec, vo)
        qk = join(qk, send(qk, NEAR_Z), 1, place.near_z)
        vec = vec + send(vec, NEAR_Z)
        vo = join(vo, send(vo, FAR_Z), 0, place.far_z)
        qk, vec, vo, w_inner = together(qk, vec, vo, w_inner)
        qk = join(qk, send(qk, FIRST), 2, place.first).reshape(4, 2, 48, D)
        vec = vec + send(vec, FIRST)
        vo = join(vo, send(vo, NEAR_Z), 1, place.near_z)
        inn = join(w_inner, send(w_inner, FAR_Z), 0, place.far_z)
        qk, vec, vo, inn = together(qk, vec, vo, inn)
        far = send(qk, SECOND)
        other = send(qk, CORE)
        vec = vec + send(vec, SECOND)
        vo = join(vo, send(vo, FIRST), 2, place.first).reshape(4, 2, 48, D)
        inn = join(inn, send(inn, NEAR_Z), 1, place.near_z)
        far, other, vec, vo, inn = together(far, other, vec, vo, inn)
        qk_parts = (qk, far, other, send(far, CORE))
        vec = vec + send(vec, CORE)
        qk_parts, vec, vo, inn, w_outer = together(qk_parts, vec, vo, inn, w_outer)
        vo_far = send(vo, SECOND)
        other = send(vo, CORE)
        inn = join(inn, send(inn, FIRST), 2, place.first).reshape(4, 2, 24, FF)
        out = join(w_outer, send(w_outer, FAR_Z), 0, place.far_z)
        queries, keys, qk = project(x, vec, qk_parts, 2, (B_QUERY, None), cube)
        queries, vo_far, other, inn, out = together(queries, vo_far, other, inn, out)
        vo_parts = (vo, vo_far, other, send(vo_far, CORE))
        inn_far = send(inn, SECOND)
        came = send(out, NEAR_Z)
        values, vo = project(x, vec, vo_parts, 2, (B_VALUE,), cube)
        values, came = together(values, came)
        out = join(out, came, 1, place.near_z)
        came = send(out, FIRST)
        probs, context = attend(lengths, queries, keys, values)
        context, inn, inn_far, came = together(context, inn, inn_far, came)
        inn_parts = (inn, inn_far, send(inn, CORE), send(inn_far, CORE))
        out = join(out, came, 2, place.first).reshape(4, 2, 96, D)
        out_far = send(out, SECOND)
        other = send(out, CORE)
        hat1, inv1, normed = close(x, context, vo, vec)
        normed, inn_parts = together(normed, inn_parts)
        act, slope, inner_mat = inner(normed, vec, inn_parts, cube)
        act, out_far, other = together(act, out_far, other)
        out_parts = (out, out_far, other, send(out_far, CORE))
        block_out, hat2, inv2, cls, unit, outer_mat = outer(act, hat1, vec, out_parts, cube)
        near = spread(unit, place).reshape(4, 2, *unit.shape)
        far = send(near, SECOND)
        loss, d_cls = pair_loss((near, far, send(near, CORE), send(far, CORE)), vec, cls)
        dres, dbr, sums, *shares = outer_back(
            out_cotangent.reshape(count * LEN, D), d_cls, hat2, inv2, act, vec, cube
        )
        o = Reduction(shares, place)
        dbr, o.away = together(dbr, o.away)
        o.start(CORE)
        dh, sums, *shares = inner_back(dbr, normed, slope, outer_mat, sums, cube)
        i = Reduction(shares, place, early_z=True)
        dh, i.away = arrive([o], dh, i.away)
        i.start(CORE)
        o.settle()
        o.start(FIRST)
        dh, dres = together(dh, dres)
        d_resid, d_attn, d_context, sums = open_back(dres, dh, inner_mat, hat1, inv1, vo, vec, sums)
        (d_context,) = arrive([o, i], d_context)
        o.settle()
        o.start(SECOND)
        i.settle()
        i.start(NEAR_Z)
        d_queries, d_keys, d_values, *shares = heads_back(
            queries, keys, values, d_context, probs, x, sums, context, d_attn, cube
        )
        a = Reduction(shares, place)
        d_queries, a.away = arrive([o, i], d_queries, a.away)
        a.start(CORE)
        o.settle()
        i.settle()
        o.away, i.away = arrive([a], o.away, i.away)
        a.settle()
        a.start(FIRST)
        o.start(NEAR_Z)
        i.start(FIRST)
        grad_rows = token_grad(d_resid, d_queries, d_keys, d_values, qk, vo)
        (grad_rows,) = arrive([o, i, a], grad_rows)
        a.settle()
        a.start(SECOND)
        o.settle()
        o.start(FAR_Z)
        i.settle()
        i.start(SECOND)
        arrive([i, a])
        a.settle()
        a.start(NEAR_Z)
        i.settle()
        i.start(FAR_Z)
        grad_w_outer = o.total()
        (grad_w_outer,) = arrive([a], grad_w_outer)
        a.settle()
        a.start(FAR_Z)
        grad_w_inner = i.total()
        g_attn = a.total()
        g_mats = [g_attn[24 * n : 24 * (n + 1)] for n in range(4)]
        small, inner_part = g_attn[96:, D - WIDE :], g_attn[96, D - WIDE // 2 :]
        grads = [small[n, : D // CUBE] for n in range(B_INNER)] + [inner_part[: FF // CUBE]]
    else:
        rows = [every(v).reshape(-1, D) for v in vectors]
        vec = jnp.concatenate(rows + [jnp.zeros((4, D), low)], axis=0)
        qk_parts, vo_parts = ((jnp.stack([every(w) for w in ws]),) for ws in ((w_query, w_key), (w_value, w_output)))
        queries, keys, qk = project(x, vec, qk_parts, 2, (B_QUERY, None), cube)
        values, vo = project(x, vec, vo_parts, 2, (B_VALUE,), cube)
        probs, context = attend(lengths, queries, keys, values)
        hat1, inv1, normed = close(x, context, vo, vec)
        act, slope, inner_mat = inner(normed, vec, (every(w_inner),), cube)
        block_out, hat2, inv2, cls, unit, outer_mat = outer(act, hat1, vec, (every(w_outer),), cube)
        loss, d_cls = plain_loss(every(unit), every(partners), cls)
        dres, dbr, sums, d_outer = outer_back(
            out_cotangent.reshape(count * LEN, D), d_cls, hat2, inv2, act, vec, cube
        )
        dh, sums, d_inner = inner_back(dbr, normed, slope, outer_mat, sums, cube)
        d_resid, d_attn, d_context, sums = open_back(dres, dh, inner_mat, hat1, inv1, vo, vec, sums)
        d_queries, d_keys, d_values, sums, d_mats = heads_back(
            queries, keys, values, d_context, probs, x, sums, context, d_attn, cube
        )
        grad_rows = token_grad(d_resid, d_queries, d_keys, d_values, qk, vo)
        grad_w_outer, grad_w_inner = scatter(d_outer), scatter(d_inner)
        g_mats = [scatter(d_mats[n]) for n in range(4)]
        grads = [scatter(sums[n]) for n in range(B_INNER)] + [scatter(sums[B_INNER:CODES].reshape(-1))]
    (
        grad_b_query,
        grad_b_value,
        grad_b_output,
        grad_gain_attn,
        grad_shift_attn,
        grad_b_outer,
        grad_gain_ffn,
        grad_shift_ffn,
        grad_b_inner,
    ) = grads
    return (
        loss,
        block_out.reshape(count, LEN, D),
        grad_rows.reshape(count, LEN, D),
        g_mats[0],
        g_mats[1],
        g_mats[2],
        g_mats[3],
        grad_b_query,
        grad_b_value,
        grad_b_output,
        grad_gain_attn,
        grad_shift_attn,
        grad_w_inner,
        grad_b_inner,
        grad_w_outer,
        grad_b_outer,
        grad_gain_ffn,
        grad_shift_ffn,
    )


def solution(mesh):
    rows, cols = P(AXIS), P(AXIS, None)
    cube = P(AXIS, None, None)
    in_specs = (cube, rows, rows, cube) + (cols,) * 4 + (rows,) * 5 + (cols, rows, cols) + (rows,) * 3
    out_specs = (P(), cube, cube) + (cols,) * 4 + (rows,) * 5 + (cols, rows, cols) + (rows,) * 3
    return jax.shard_map(local, mesh=mesh, in_specs=in_specs, out_specs=out_specs, check_vma=False)
```

```python
import jax
import jax.numpy as jnp
from jax import lax
from jax.experimental import pallas as pl
from jax.experimental.pallas import tpu as pltpu
from jax.sharding import PartitionSpec as P

D = 768
HEADS = 12
HEAD_DIM = 64
LEN = 64
FF = 3072
QUAD = 4
WIDE = QUAD * HEAD_DIM
GROUPS = HEADS // QUAD
ROWS = 256
BLOCK = 768
AXIS = "fsdp"
CUBE = 32
norm_eps = 1e-12
pool_eps = 1e-06
sim_scale = 50.0
sim_margin = 0.3
f32, low = jnp.float32, jnp.bfloat16
S = jax.ShapeDtypeStruct

B_QUERY, B_VALUE, B_OUTPUT, G_ATTN, S_ATTN, B_OUTER, G_FFN, S_FFN, B_INNER = range(9)
CODES = B_INNER + FF // D


def nn(a, b):
    return lax.dot_general(a, b, (((1,), (0,)), ((), ())), preferred_element_type=f32)


def nt(a, b):
    return lax.dot_general(a, b, (((1,), (1,)), ((), ())), preferred_element_type=f32)


def tn(a, b):
    return lax.dot_general(a, b, (((0,), (0,)), ((), ())), preferred_element_type=f32)


def whole(shape):
    return pl.BlockSpec(shape, lambda *_: (0,) * len(shape), pipeline_mode=pl.Buffered(1))


def row_block(width, rows=ROWS):
    return pl.BlockSpec((rows, width), lambda i, *_: (i, 0))


def params(flops, nbytes, exps=0, room=60):
    return dict(
        compiler_params=pltpu.CompilerParams(vmem_limit_bytes=room << 20),
        cost_estimate=pl.CostEstimate(flops=int(flops), bytes_accessed=int(nbytes), transcendentals=int(exps)),
    )


ANY = pl.BlockSpec(memory_space=pl.ANY)


def part_copies(parts, target, sems, cut):
    me = lax.axis_index(AXIS)
    core, x, y = me & 1, (me >> 1) & 1, (me >> 2) & 1

    def start(zero, one):
        for i in range(2):
            pltpu.make_async_copy(cut(zero[i]), target.at[:, (y + i) & 1, :, 0], sems.at[2 * i]).start()
            pltpu.make_async_copy(cut(one[i]), target.at[:, :, (x + i) & 1, 1], sems.at[2 * i + 1]).start()

    @pl.when(core == 0)
    def _():
        start(parts[:2], parts[2:])

    @pl.when(core == 1)
    def _():
        start(parts[2:], parts[:2])


def part_waits(parts, target, sems, cut):
    for i in range(2):
        pltpu.make_async_copy(cut(parts[i]), target.at[:, i, :, 0], sems.at[2 * i]).wait()
        pltpu.make_async_copy(cut(parts[i]), target.at[:, :, i, 1], sems.at[2 * i + 1]).wait()


def everything(ref):
    return ref


def project_body(cube, count, biases, x_ref, vec_ref, *refs):
    outs = len(biases)
    parts, out_refs, (full_ref, w_ref, sems, out_sem) = refs[: -outs - 4], refs[-outs - 4 : -4], refs[-4:]
    step = pl.program_id(0)
    onward = pltpu.make_async_copy(w_ref, full_ref, out_sem)

    @pl.when(step == 0)
    def _():
        if cube:

            def cut(m):
                return lambda ref: ref.at[:, :, pl.ds(m * 24, 24), :]

            for m in range(count):
                part_copies(parts, w_ref.at[m], sems.at[m], cut(m))
            for m in range(count):
                part_waits(parts, w_ref.at[m], sems.at[m], cut(m))
        else:
            copy = pltpu.make_async_copy(parts[0], w_ref, sems.at[0, 0])
            copy.start()
            copy.wait()
        onward.start()

    x = x_ref[...]
    for m, (bias, out) in enumerate(zip(biases, out_refs)):
        product = nn(x, w_ref.at[m].reshape(D, D)[...] if cube else w_ref[m])
        if bias is not None:
            product += vec_ref[bias : bias + 1].astype(f32)
        out[...] = product.astype(low)

    @pl.when(step == pl.num_programs(0) - 1)
    def _():
        onward.wait()


def project(x, vec, parts, count, biases, cube):
    t = x.shape[0]
    shape = (count, 4, 2, 2, 2, 24, D) if cube else (count, D, D)
    outs = len(biases)
    *products, full = pl.pallas_call(
        lambda *refs: project_body(cube, count, biases, *refs),
        grid=(t // (2 * ROWS),),
        in_specs=[row_block(D, 2 * ROWS), whole(vec.shape)] + [ANY] * len(parts),
        out_specs=[row_block(D, 2 * ROWS)] * outs + [ANY],
        out_shape=[S((t, D), low)] * outs + [S(shape, low)],
        scratch_shapes=[pltpu.VMEM(shape, low), pltpu.SemaphoreType.DMA((count, 4)), pltpu.SemaphoreType.DMA],
        name="project",
        **params(2 * outs * t * D * D, 2 * (outs + 1) * t * D + 4 * count * D * D, room=16),
    )(x, vec, *parts)
    return *products, full.reshape(count, D, D)


def assemble(cube, parts, w_ref, full_ref, sems, out_sem):
    onward = pltpu.make_async_copy(w_ref, full_ref, out_sem)

    @pl.when(pl.program_id(0) == 0)
    def _():
        if cube:
            part_copies(parts, w_ref, sems, everything)
            part_waits(parts, w_ref, sems, everything)
        else:
            copy = pltpu.make_async_copy(parts[0], w_ref, sems.at[0])
            copy.start()
            copy.wait()
        onward.start()

    return onward


def scratch_for(shape):
    return [pltpu.VMEM(shape, low), pltpu.SemaphoreType.DMA((4,)), pltpu.SemaphoreType.DMA]


def head_masks(dtype):
    lane = lax.broadcasted_iota(jnp.int32, (1, WIDE), 1) // HEAD_DIM
    return [jnp.where(lane == h, 1.0, 0.0).astype(dtype) for h in range(QUAD)]


def stacked(rows, masks):
    return jnp.concatenate([rows * m for m in masks], axis=0)


def unstacked(full, masks):
    return sum(full[LEN * h : LEN * (h + 1)] * m for h, m in enumerate(masks))


def layer_norm(resid):
    centred = resid - jnp.mean(resid, axis=-1, keepdims=True)
    inv = lax.rsqrt(jnp.mean(centred * centred, axis=-1, keepdims=True) + norm_eps)
    return centred * inv, inv


def layer_norm_back(grad, gain, hat, inv):
    grad = grad * gain
    mean = jnp.mean(grad, axis=-1, keepdims=True)
    along = jnp.mean(grad * hat, axis=-1, keepdims=True)
    return (grad - mean - hat * along) * inv


def attend_body(len_ref, q_ref, k_ref, v_ref, p_ref, c_ref):
    masks, masks32 = head_masks(low), head_masks(f32)
    per = q_ref.shape[0] // LEN
    first = pl.program_id(0) * per
    key_at = lax.broadcasted_iota(jnp.int32, (LEN, WIDE), 0)

    def sentence(s):
        rows = pl.ds(pl.multiple_of(s * LEN, LEN), LEN)
        seen = key_at < len_ref[first + s]
        for g in range(GROUPS):
            cols = pl.ds(g * WIDE, WIDE)
            q, k, v = q_ref[rows, cols], k_ref[rows, cols], v_ref[rows, cols]
            scores = nt(k, stacked(q, masks)) * HEAD_DIM ** (-0.5)
            scores = jnp.where(seen, scores, -1e30)
            expd = jnp.exp(scores - jnp.max(scores, axis=0, keepdims=True))
            probs = expd * (1.0 / jnp.sum(expd, axis=0, keepdims=True))
            p_ref[g, rows, :] = probs
            c_ref[rows, cols] = unstacked(tn(probs.astype(low), v), masks32).astype(low)

    pl.loop(0, per, unroll=UNROLL)(sentence)


UNROLL = 8


def mat_of(m):
    return pl.BlockSpec((1, D, D), lambda *_: (m, 0, 0), pipeline_mode=pl.Buffered(1))


def attend(lengths, q, k, v):
    t = q.shape[0]
    rows = row_block(D, 2 * ROWS)
    return pl.pallas_call(
        attend_body,
        grid_spec=pltpu.PrefetchScalarGridSpec(
            num_scalar_prefetch=1,
            grid=(t // (2 * ROWS),),
            in_specs=[rows] * 3,
            out_specs=[pl.BlockSpec((GROUPS, 2 * ROWS, WIDE), lambda i, *_: (0, i, 0)), rows],
        ),
        out_shape=[S((GROUPS, t, WIDE), f32), S((t, D), low)],
        name="attend",
        **params(10 * t * D * D, 20 * t * D, t * D, room=60),
    )(lengths, q, k, v)


def halves(ref):
    return [slice(i * ROWS, (i + 1) * ROWS) for i in range(ref.shape[0] // ROWS)]


def close_body(x_ref, c_ref, w_ref, vec_ref, hat_ref, inv_ref, n_ref):
    w = w_ref[0]
    branches = [nn(c_ref[r, :], w) + vec_ref[B_OUTPUT : B_OUTPUT + 1].astype(f32) for r in halves(x_ref)]
    for r, branch in zip(halves(x_ref), branches):
        hat, inv = layer_norm(x_ref[r, :].astype(f32) + branch)
        hat_ref[r, :] = hat
        inv_ref[r, :] = inv
        n_ref[r, :] = (hat * vec_ref[G_ATTN : G_ATTN + 1].astype(f32) + vec_ref[S_ATTN : S_ATTN + 1].astype(f32)).astype(low)


def close(x, c, full, vec):
    t = x.shape[0]
    rows = row_block(D, 2 * ROWS)
    return pl.pallas_call(
        close_body,
        grid=(t // (2 * ROWS),),
        in_specs=[rows, rows, mat_of(1), whole(vec.shape)],
        out_specs=[rows, row_block(1, 2 * ROWS), rows],
        out_shape=[S((t, D), f32), S((t, 1), f32), S((t, D), low)],
        name="close",
        **params(2 * t * D * D, 10 * t * D + 2 * D * D, room=60),
    )(x, c, full, vec)


def open_back_body(dres_ref, dh_ref, wi_ref, hat_ref, inv_ref, wo_ref, vec_ref, before_ref, dr_ref, da_ref, dc_ref, sums_ref):
    @pl.when(pl.program_id(0) == 0)
    def _():
        sums_ref[...] = before_ref[...]

    grads = [dres_ref[r, :] + nt(dh_ref[r, :], wi_ref[...]) for r in halves(dres_ref)]
    for r, dn in zip(halves(dres_ref), grads):
        hat = hat_ref[r, :]
        dres = layer_norm_back(dn, vec_ref[G_ATTN : G_ATTN + 1].astype(f32), hat, inv_ref[r, :])
        dr_ref[r, :] = dres
        dao = dres.astype(low)
        da_ref[r, :] = dao
        dc_ref[r, :] = nt(dao, wo_ref[0]).astype(low)
        sums_ref[B_OUTPUT : B_OUTPUT + 1] += jnp.sum(dao.astype(f32), axis=0, keepdims=True)
        sums_ref[G_ATTN : G_ATTN + 1] += jnp.sum(dn * hat, axis=0, keepdims=True)
        sums_ref[S_ATTN : S_ATTN + 1] += jnp.sum(dn, axis=0, keepdims=True)


def open_back(dres, dh, wi, hat, inv, full, vec, sums):
    t = dres.shape[0]
    return pl.pallas_call(
        open_back_body,
        grid=(t // (2 * ROWS),),
        in_specs=[row_block(D, 2 * ROWS), row_block(FF, 2 * ROWS), whole(wi.shape), row_block(D, 2 * ROWS), row_block(1, 2 * ROWS), mat_of(1), whole(vec.shape), whole((16, D))],
        out_specs=[row_block(D, 2 * ROWS)] * 3 + [whole((16, D))],
        out_shape=[S((t, D), f32), S((t, D), low), S((t, D), low), S((16, D), f32)],
        name="open_back",
        **params(10 * t * D * D, 20 * t * D + 10 * D * D, room=60),
    )(dres, dh, wi, hat, inv, full, vec, sums)


def device_rows(table):
    rows = 8 * CUBE
    row, lane = (lax.broadcasted_iota(jnp.int32, (rows, D), axis) for axis in range(2))
    out = []
    for values, r in (
        (jnp.concatenate([table[:8]] * CUBE, axis=0), D // CUBE),
        (jnp.concatenate([jnp.broadcast_to(table[B_INNER + j : B_INNER + j + 1], (rows * D // FF, D)) for j in range(FF // D)], axis=0), FF // CUBE),
    ):
        own = jnp.where(lane // r == (row // 8) % (D // r), values, 0.0).astype(low)
        at, to = (lax.broadcasted_iota(jnp.int32, (D, WIDE // 2), axis) for axis in range(2))
        out.append(nn(own, jnp.where(at % r == to, 1.0, 0.0).astype(low)))
    return jnp.concatenate(out, axis=1)


def heads_back_body(cube, q_ref, k_ref, v_ref, dc_ref, p_ref, x_ref, before_ref, c_ref, da_ref, *refs):
    dq_ref, dk_ref, dv_ref, *shares = refs[:-1]
    table_ref = refs[-1]
    step = pl.program_id(0)
    masks, masks32 = head_masks(low), head_masks(f32)

    def sentence(s):
        rows = pl.ds(pl.multiple_of(s * LEN, LEN), LEN)
        q, k, v, dc, p = q_ref[rows, :], k_ref[rows, :], v_ref[rows, :], dc_ref[rows, :], p_ref[0, rows, :]
        dcs = stacked(dc, masks)
        dp = nt(v, dcs)
        dv_ref[rows, :] = nn(p.astype(low), dcs).astype(low)
        ds = (p * (dp - jnp.sum(p * dp, axis=0, keepdims=True))).astype(low)
        dk_ref[rows, :] = (nn(ds, stacked(q, masks)) * HEAD_DIM ** (-0.5)).astype(low)
        dq_ref[rows, :] = (unstacked(tn(ds, k), masks32) * HEAD_DIM ** (-0.5)).astype(low)

    @pl.when(step == 0)
    def _():
        table_ref[...] = before_ref[...]

    pl.loop(0, q_ref.shape[0] // LEN, unroll=BACK_UNROLL)(sentence)
    cols = pl.ds(pl.multiple_of(step * WIDE, WIDE), WIDE)
    table_ref[B_QUERY : B_QUERY + 1, cols] = jnp.sum(dq_ref[...].astype(f32), axis=0, keepdims=True)
    table_ref[B_VALUE : B_VALUE + 1, cols] = jnp.sum(dv_ref[...].astype(f32), axis=0, keepdims=True)
    for m, (rows, grad) in enumerate(((x_ref, dq_ref), (x_ref, dk_ref), (x_ref, dv_ref), (c_ref, da_ref))):
        full = tn(rows[...], grad[...])
        if cube:
            full = full.reshape(4, 2, 2, 2, 24, WIDE)

            def put(ref, p, q, value, m=m):
                ref[:, p, q, 24 * m : 24 * (m + 1)] = value.astype(ref.dtype)

            write_shares(lambda y, x, c: full[:, y, x, c], *shares, put)
        else:
            shares[1][m] = full
    if cube:

        def put_rows(ref, p, q, value):
            ref[:, p, q, 96:] = value.astype(ref.dtype)

        @pl.when(step < GROUPS - 1)
        def _():
            write_shares(lambda y, x, c: jnp.zeros((4, 8, WIDE), f32), *shares, put_rows)

        @pl.when(step == GROUPS - 1)
        def _():
            values = device_rows(table_ref[...]).reshape(4, 2, 2, 2, 8, WIDE)
            write_shares(lambda y, x, c: values[:, y, x, c], *shares, put_rows)
    else:
        shares[0][...] = table_ref[...]


BACK_UNROLL = 16


def heads_back(q, k, v, dc, p, x, sums, c, da, cube):
    t = q.shape[0]
    col = pl.BlockSpec((t, WIDE), lambda i: (0, i))
    if cube:
        spec = pl.BlockSpec((4, 2, 2, 104, WIDE), lambda i: (0, 0, 0, 0, i))
        shape = (4, 2, 2, 104, D)
        specs, shapes = [spec] * 2, [S(shape, KEEP), S(shape, low)]
    else:
        specs = [whole((16, D)), pl.BlockSpec((4, D, WIDE), lambda i: (0, 0, i))]
        shapes = [S((16, D), f32), S((4, D, D), f32)]
    return pl.pallas_call(
        lambda *refs: heads_back_body(cube, *refs),
        grid=(GROUPS,),
        in_specs=[col] * 4
        + [pl.BlockSpec((1, t, WIDE), lambda i: (i, 0, 0)), whole((t, D)), whole((16, D)), whole((t, D)), col],
        out_specs=[col] * 3 + specs,
        out_shape=[S((t, D), low)] * 3 + shapes,
        scratch_shapes=[pltpu.VMEM((16, D), f32)],
        name="heads_back",
        **params(t * D * 24000, t * D * 20, room=60),
    )(q, k, v, dc, p, x, sums, c, da)


def gelu_parts(h):
    d = 1.0 + (0.3275911 * 0.7071067811865476) * jnp.abs(h)
    t = pl.reciprocal(d, approx=True)
    t = t * (2.0 - d * t)
    poly = t * (0.127414796 + t * (-0.142248368 + t * (0.7107068705 + t * (-0.7265760135 + t * 0.5307027145))))
    bell = jnp.exp(-0.5 * (h * h))
    tail = poly * bell
    cdf = jnp.where(h >= 0, 1.0 - tail, tail)
    return h * cdf, cdf + h * (bell * 0.3989422804014327)


def inner_body(cube, n_ref, vec_ref, *refs):
    parts, (a_ref, gp_ref, full_ref, w_ref, sems, out_sem, bias_ref) = refs[:-7], refs[-7:]
    onward = assemble(cube, parts, w_ref, full_ref, sems, out_sem)

    @pl.when(pl.program_id(0) == 0)
    def _():
        bias_ref[...] = vec_ref[...].astype(f32)

    w = w_ref.reshape(D, FF) if cube else w_ref

    @pl.loop(0, FF // BLOCK, unroll=2)
    def _(j):
        cols = pl.ds(pl.multiple_of(j * BLOCK, BLOCK), BLOCK)
        h = nn(n_ref[...], w[:, cols]) + bias_ref[pl.ds(B_INNER + j, 1), :]
        act, slope = gelu_parts(h)
        a_ref[:, cols] = act.astype(low)
        gp_ref[:, cols] = slope.astype(low)

    @pl.when(pl.program_id(0) == pl.num_programs(0) - 1)
    def _():
        onward.wait()


def inner(n, vec, parts, cube):
    t = n.shape[0]
    shape = (4, 2, 2, 2, 24, FF) if cube else (D, FF)
    act, slope, full = pl.pallas_call(
        lambda *refs: inner_body(cube, *refs),
        grid=(t // ROWS,),
        in_specs=[row_block(D), whole(vec.shape)] + [ANY] * len(parts),
        out_specs=[row_block(FF), row_block(FF), ANY],
        out_shape=[S((t, FF), low), S((t, FF), low), S(shape, low)],
        scratch_shapes=[*scratch_for(shape), pltpu.VMEM((16, D), f32)],
        name="inner",
        **params(6 * t * D * FF, 2 * t * D + 4 * t * FF + 4 * D * FF, 2 * t * FF, room=60),
    )(n, vec, *parts)
    return act, slope, full.reshape(D, FF)


def outer_body(cube, a_ref, hat_ref, vec_ref, *refs):
    parts = refs[:-9]
    out_ref, hat2_ref, inv_ref, cls_ref, unit_ref, full_ref, w_ref, sems, out_sem = refs[-9:]
    onward = assemble(cube, parts, w_ref, full_ref, sems, out_sem)
    step = pl.program_id(0)
    w = w_ref.reshape(FF, D) if cube else w_ref
    branch = nn(a_ref[...], w[...]) + vec_ref[B_OUTER : B_OUTER + 1].astype(f32)
    normed = hat_ref[...] * vec_ref[G_ATTN : G_ATTN + 1].astype(f32) + vec_ref[S_ATTN : S_ATTN + 1].astype(f32)
    hat, inv = layer_norm(normed + branch)
    hat2_ref[...] = hat
    inv_ref[...] = inv
    rows = hat * vec_ref[G_FFN : G_FFN + 1].astype(f32) + vec_ref[S_FFN : S_FFN + 1].astype(f32)
    out_ref[...] = rows.astype(low)
    pairs = rows.shape[0] // LEN // 2
    for s in range(pairs):
        at = pl.ds(step * pairs + s, 1)
        for side in range(2):
            cols = pl.ds(side * D, D)
            cls = rows[LEN * (2 * s + side) : LEN * (2 * s + side) + 1]
            cls_ref[at, cols] = cls

    @pl.when(step == pl.num_programs(0) - 1)
    def _():
        for side in range(2):
            cls = cls_ref[:, side * D : (side + 1) * D]
            unit = cls * lax.rsqrt(jnp.sum(cls * cls, axis=-1, keepdims=True) + pool_eps)
            unit_ref[:, side * D : (side + 1) * D] = unit.astype(low)
        onward.wait()


def outer(act, hat, vec, parts, cube):
    t = hat.shape[0]
    shape = (4, 2, 2, 2, 96, D) if cube else (FF, D)
    pairs = t // LEN // 2
    once = pl.BlockSpec((pairs, 2 * D), lambda i: (0, 0))
    *outs, full = pl.pallas_call(
        lambda *refs: outer_body(cube, *refs),
        grid=(t // ROWS,),
        in_specs=[row_block(FF), row_block(D), whole(vec.shape)] + [ANY] * len(parts),
        out_specs=[row_block(D), row_block(D), row_block(1), once, once, ANY],
        out_shape=[S((t, D), low), S((t, D), f32), S((t, 1), f32), S((pairs, 2 * D), f32), S((pairs, 2 * D), low), S(shape, low)],
        scratch_shapes=[pltpu.VMEM(shape, low), pltpu.SemaphoreType.DMA((4,)), pltpu.SemaphoreType.DMA],
        name="outer",
        **params(2 * t * D * FF, 10 * t * D + 2 * t * FF + 4 * D * FF, room=60),
    )(act, hat, vec, *parts)
    return *outs, full.reshape(FF, D)


def write_shares(full, keep_ref, away_ref, put):
    core = lax.axis_index(AXIS) & 1

    def write(zero, one):
        for y in range(2):
            for x in range(2):
                put(zero, x, y, full(y, x, 0))
                put(one, y, x, full(y, x, 1))

    @pl.when(core == 0)
    def _():
        write(keep_ref, away_ref)

    @pl.when(core == 1)
    def _():
        write(away_ref, keep_ref)


def outer_back_body(cube, cot_ref, dc_ref, hat2_ref, inv2_ref, a_ref, vec_ref, dres_ref, dbr_ref, sums_ref, *refs):
    j = pl.program_id(0)

    def write(dw):
        if cube:
            dw = dw.reshape(2, 2, 2, 96, D)

            def put(ref, p, q, value):
                ref[0, p, q] = value.astype(ref.dtype)

            write_shares(lambda y, x, c: dw[y, x, c], *refs, put)
        else:
            refs[0][...] = dw

    @pl.when(j == 0)
    def _():
        dw = jnp.zeros((BLOCK, D), f32)
        dgain = jnp.zeros((1, D), f32)
        dshift = jnp.zeros((1, D), f32)
        dbias = jnp.zeros((1, D), f32)
        at = lax.broadcasted_iota(jnp.int32, (ROWS, D), 0)
        for b in range(cot_ref.shape[0] // ROWS):
            rows = pl.ds(b * ROWS, ROWS)
            d = cot_ref[rows, :].astype(f32)
            hat = hat2_ref[rows, :]
            for s in range(ROWS // LEN):
                whose = b * (ROWS // LEN) + s
                extra = dc_ref[whose // 2 : whose // 2 + 1, (whose % 2) * D : (whose % 2 + 1) * D]
                d += jnp.where(at == LEN * s, extra, 0.0)
            dgain += jnp.sum(d * hat, axis=0, keepdims=True)
            dshift += jnp.sum(d, axis=0, keepdims=True)
            dres = layer_norm_back(d, vec_ref[G_FFN : G_FFN + 1].astype(f32), hat, inv2_ref[rows, :])
            dres_ref[rows, :] = dres
            dbr = dres.astype(low)
            dbr_ref[rows, :] = dbr
            dbias += jnp.sum(dbr.astype(f32), axis=0, keepdims=True)
            dw += tn(a_ref[rows, :], dbr)
        write(dw)
        sums_ref[...] = jnp.zeros_like(sums_ref)
        sums_ref[B_OUTER : B_OUTER + 1] = dbias
        sums_ref[G_FFN : G_FFN + 1] = dgain
        sums_ref[S_FFN : S_FFN + 1] = dshift

    @pl.when(j > 0)
    def _():
        write(tn(a_ref[...], dbr_ref[...]))


def outer_back(cot, dc, hat2, inv2, a, vec, cube):
    t = cot.shape[0]
    if cube:
        spec = pl.BlockSpec((1, 2, 2, 96, D), lambda j: (j, 0, 0, 0, 0))
        specs, shapes = [spec] * 2, [S((4, 2, 2, 96, D), KEEP), S((4, 2, 2, 96, D), low)]
    else:
        specs, shapes = [pl.BlockSpec((BLOCK, D), lambda j: (j, 0))], [S((FF, D), f32)]
    return pl.pallas_call(
        lambda *refs: outer_back_body(cube, *refs),
        grid=(FF // BLOCK,),
        in_specs=[whole((t, D)), whole(dc.shape), whole((t, D)), whole((t, 1)), pl.BlockSpec((t, BLOCK), lambda j: (0, j)),
                  whole(vec.shape)],
        out_specs=[whole((t, D)), whole((t, D)), whole((16, D))] + specs,
        out_shape=[S((t, D), f32), S((t, D), low), S((16, D), f32)] + shapes,
        name="outer_back",
        **params(4 * t * D * FF, 14 * t * D + 2 * t * FF + 8 * D * FF, room=60),
    )(cot, dc, hat2, inv2, a, vec)


def inner_back_body(cube, dbr_ref, n_ref, gp_ref, wo_ref, before_ref, dh_ref, sums_ref, *refs):
    @pl.when(pl.program_id(0) == 0)
    def _():
        sums_ref[...] = before_ref[...]

    dh = (gp_ref[...].astype(f32) * nt(dbr_ref[...], wo_ref[...])).astype(low)
    dh_ref[...] = dh
    sums_ref[pl.ds(B_INNER + pl.program_id(0), 1), :] = jnp.sum(dh.astype(f32), axis=0, keepdims=True)
    dw = tn(n_ref[...], dh)
    if cube:
        dw = dw.reshape(4, 2, 2, 2, 24, BLOCK)

        def put(ref, p, q, value):
            ref[:, p, q] = value.astype(ref.dtype)

        write_shares(lambda y, x, c: dw[:, y, x, c], *refs, put)
    else:
        refs[0][...] = dw


def inner_back(dbr, n, gp, wo, sums, cube):
    t = n.shape[0]
    fblk = pl.BlockSpec((t, BLOCK), lambda j: (0, j))
    if cube:
        spec = pl.BlockSpec((4, 2, 2, 24, BLOCK), lambda j: (0, 0, 0, 0, j))
        specs, shapes = [spec] * 2, [S((4, 2, 2, 24, FF), KEEP), S((4, 2, 2, 24, FF), low)]
    else:
        specs, shapes = [pl.BlockSpec((D, BLOCK), lambda j: (0, j))], [S((D, FF), f32)]
    return pl.pallas_call(
        lambda *refs: inner_back_body(cube, *refs),
        grid=(FF // BLOCK,),
        in_specs=[whole((t, D)), whole((t, D)), fblk, pl.BlockSpec((BLOCK, D), lambda j: (j, 0)), whole((16, D))],
        out_specs=[fblk, whole((16, D))] + specs,
        out_shape=[S((t, FF), low), S((16, D), f32)] + shapes,
        name="inner_back",
        **params(4 * t * D * FF, 4 * t * D + 4 * t * FF + 8 * D * FF, room=60),
    )(dbr, n, gp, wo, sums)


KEEP = low


def token_grad_body(dr_ref, dq_ref, dk_ref, dv_ref, wq_ref, wk_ref, wv_ref, o_ref):
    o_ref[...] = (
        dr_ref[...] + nt(dq_ref[...], wq_ref[0]) + nt(dk_ref[...], wk_ref[0]) + nt(dv_ref[...], wv_ref[0])
    )


def token_grad(dr, dq, dk, dv, qk, vo):
    t = dr.shape[0]

    return pl.pallas_call(
        token_grad_body,
        grid=(t // ROWS,),
        in_specs=[row_block(D)] * 4 + [mat_of(0), mat_of(1), mat_of(0)],
        out_specs=row_block(D),
        out_shape=S((t, D), f32),
        name="token_grad",
        **params(6 * t * D * D, 14 * t * D + 6 * D * D, room=60),
    )(dr, dq, dk, dv, qk, qk, vo)


def loss_body(near, far, near_other, far_other, codes_ref, cls_ref, loss_ref, dc_ref, table_ref, ds_ref, units_ref, sems):
    parts = (near, far, near_other, far_other)
    part_copies(parts, units_ref, sems, everything)
    part_waits(parts, units_ref, sems, everything)
    own = cls_ref.shape[0]
    pairs = CUBE * own
    units = units_ref.reshape(pairs, 2 * D)
    sources, targets = units[:, :D], units[:, D:]
    codes = codes_ref[CODES : CODES + 2, :pairs].astype(f32)
    partner = (codes[0:1] + 64.0 * codes[1:2]).astype(jnp.int32)
    matched = lax.broadcasted_iota(jnp.int32, (pairs, pairs), 0) == partner
    sims = nt(targets, sources) * sim_scale - jnp.where(matched, sim_scale * sim_margin, 0.0)
    row_top = jnp.max(sims, axis=0, keepdims=True)
    row_lse = row_top + jnp.log(jnp.sum(jnp.exp(sims - row_top), axis=0, keepdims=True))
    col_top = jnp.max(sims, axis=1, keepdims=True)
    col_lse = col_top + jnp.log(jnp.sum(jnp.exp(sims - col_top), axis=1, keepdims=True))
    total = (
        jnp.sum(row_lse, axis=1, keepdims=True)
        + jnp.sum(col_lse, axis=0, keepdims=True)
        - 2.0 * jnp.sum(jnp.sum(jnp.where(matched, sims, 0.0), axis=1, keepdims=True), axis=0, keepdims=True)
    )
    loss_ref[...] = jnp.broadcast_to(total * (0.5 / pairs), loss_ref.shape)
    d_sims = 0.5 * (jnp.exp(sims - row_lse) + jnp.exp(sims - col_lse)) - jnp.where(matched, 1.0, 0.0)
    d_low = (d_sims * sim_scale).astype(low)
    table_ref[...] = nn(d_low, sources)
    ds_ref[...] = tn(d_low, targets)
    mine = pl.ds(pl.multiple_of(lax.axis_index(AXIS) * own, own), own)
    for side, ref in enumerate((ds_ref, table_ref)):
        cols = pl.ds(side * D, D)
        cls, du = cls_ref[:, cols], ref[mine, :]
        inv = lax.rsqrt(jnp.sum(cls * cls, axis=-1, keepdims=True) + pool_eps)
        dc_ref[:, cols] = inv * du - cls * (inv * inv * inv * jnp.sum(du * cls, axis=-1, keepdims=True))


def pair_loss(parts, vec, cls):
    own = cls.shape[0]
    pairs = CUBE * own
    loss, dc = pl.pallas_call(
        loss_body,
        in_specs=[ANY] * 4 + [whole(vec.shape), whole(cls.shape)],
        out_specs=[whole((8, 128)), whole(cls.shape)],
        out_shape=[S((8, 128), f32), S(cls.shape, f32)],
        scratch_shapes=[pltpu.VMEM((pairs, D), f32), pltpu.VMEM((pairs, D), f32),
                        pltpu.VMEM((4, 2, 2, 2, own, 2 * D), low), pltpu.SemaphoreType.DMA((4,))],
        grid=(1,),
        name="pair_loss",
        **params(6 * pairs * pairs * D, 4 * pairs * D, 4 * pairs * pairs, room=12),
    )(*parts, vec, cls)
    return loss[0, 0], dc


CORE = [(i, i ^ 1) for i in range(CUBE)]
FAR_Z = [(i, i ^ 16) for i in range(CUBE)]
NEAR_Z = [(i, i ^ 8) for i in range(CUBE)]
FIRST = [(i, i ^ (4 if i & 1 else 2)) for i in range(CUBE)]
SECOND = [(i, i ^ (2 if i & 1 else 4)) for i in range(CUBE)]
ROUTES = (CORE, FIRST, SECOND, NEAR_Z, FAR_Z)


class Place:
    def __init__(self):
        self.me = lax.axis_index(AXIS)
        self.core = self.me & 1
        x, y = (self.me >> 1) & 1, (self.me >> 2) & 1
        self.near_z, self.far_z = (self.me >> 3) & 1, (self.me >> 4) & 1
        self.first = jnp.where(self.core == 0, x, y)
        self.second = jnp.where(self.core == 0, y, x)
        self.bits = [b.reshape(1) for b in (self.first, self.second, self.near_z, self.far_z)]


def join(own, other, axis, bit):
    shape = own.shape[:axis] + (2,) + own.shape[axis:]
    where = lax.broadcasted_iota(jnp.int32, shape, axis)
    return jnp.where(where == bit, jnp.expand_dims(own, axis), jnp.expand_dims(other, axis))


def pick(field, axis, bit):
    return lax.dynamic_index_in_dim(field, bit, axis, keepdims=False)


def send(field, route):
    return lax.ppermute(field, AXIS, route)


def spread(block, place):
    block = join(block, send(block, FAR_Z), 0, place.far_z)
    block = join(block, send(block, NEAR_Z), 1, place.near_z)
    return join(block, send(block, FIRST), 2, place.first)


def together(*values):
    return lax.optimization_barrier(values)


class Reduction:
    def __init__(self, shares, place, early_z=False):
        keep, self.away = shares
        self.terms = [keep.reshape(2, 2, *keep.shape[1:])]
        self.left = [(2, place.first), (2, place.second), (1, place.near_z), (0, place.far_z)]
        if early_z:
            self.left = [(1, place.near_z), (1, place.first), (1, place.second), (0, place.far_z)]
        self.came = None

    def start(self, route):
        self.came, self.away = send(self.away, route), None

    def settle(self):
        self.terms.append(self.came.reshape(self.terms[0].shape))
        axis, bit = self.left.pop(0)
        self.away = sum(pick(term, axis, 1 - bit).astype(f32) for term in self.terms).astype(low)
        self.terms = [pick(term, axis, bit) for term in self.terms]

    def total(self):
        return sum(term.astype(f32) for term in (*self.terms, self.came))


def arrive(sums, *values):
    done = together(*values, *[s.came for s in sums])
    for s, came in zip(sums, done[len(values) :]):
        s.came = came
    return done[: len(values)]


def spread_rows(rows, at, count):
    r = rows.shape[1]
    lane = lax.broadcasted_iota(jnp.int32, (r, D), 1)
    copies = nn(rows, jnp.where(lane % r == lax.broadcasted_iota(jnp.int32, (r, D), 0), 1.0, 0.0).astype(low))
    lane = lax.broadcasted_iota(jnp.int32, (count, D), 1)
    row = lax.broadcasted_iota(jnp.int32, (count, D), 0)
    return copies, lane // r, row


def vector_table(vectors, partners, place):
    *small, inner = vectors
    copies, lane, _ = spread_rows(jnp.stack(small), place.me, len(small))
    table = [jnp.where(lane == place.me, copies, 0.0)]
    fold = D // inner.shape[0]
    copies, lane, row = spread_rows(inner[None], place.me, FF // D)
    table.append(jnp.where((row == place.me // fold) & (lane == place.me % fold), copies, 0.0))
    codes = jnp.stack([partners % 64, partners // 64]).astype(low)
    copies, lane, _ = spread_rows(codes, place.me, 2)
    table.append(jnp.where(lane == place.me, copies, 0.0))
    table.append(jnp.zeros((2, D), f32))
    return jnp.concatenate(table, axis=0).astype(low)


def pack_body(*refs):
    *mats, out = refs
    r = mats[0].shape[0]
    for i, mat in enumerate(mats):
        out[i * r : (i + 1) * r, :] = mat[...]


def pack(*mats):
    r, n = mats[0].shape
    return pl.pallas_call(pack_body, out_shape=S((len(mats) * r, n), low), name="pack")(*mats)


def plain_loss(units, partners, cls):
    sources, targets = units[:, :D], units[:, D:]
    npairs, own = units.shape[0], cls.shape[0]
    sims = nt(sources, targets) * sim_scale
    matched = partners[:, None] == jnp.arange(npairs, dtype=jnp.int32)[None, :]
    sims = sims - jnp.where(matched, sim_scale * sim_margin, 0.0)
    row_top = jnp.max(sims, axis=1, keepdims=True)
    row_lse = row_top + jnp.log(jnp.sum(jnp.exp(sims - row_top), axis=1, keepdims=True))
    col_top = jnp.max(sims, axis=0, keepdims=True)
    col_lse = col_top + jnp.log(jnp.sum(jnp.exp(sims - col_top), axis=0, keepdims=True))
    positive = jnp.sum(jnp.where(matched, sims, 0.0))
    loss = (jnp.sum(row_lse) + jnp.sum(col_lse) - 2.0 * positive) / (2.0 * npairs)
    d_sims = 0.5 * (jnp.exp(sims - row_lse) + jnp.exp(sims - col_lse)) - jnp.where(matched, 1.0, 0.0)
    d_low = (d_sims * sim_scale).astype(low)
    first = lax.axis_index(AXIS) * own
    du = [
        nn(lax.dynamic_slice_in_dim(d_low, first, own, 0), targets),
        tn(lax.dynamic_slice_in_dim(d_low, first, own, 1), sources),
    ]
    dc = []
    for side in range(2):
        c = cls[:, side * D : (side + 1) * D]
        inv = lax.rsqrt(jnp.sum(c * c, axis=-1, keepdims=True) + pool_eps)
        dc.append(inv * du[side] - c * (inv * inv * inv * jnp.sum(du[side] * c, axis=-1, keepdims=True)))
    return loss, jnp.concatenate(dc, axis=1)


def every(v):
    return lax.all_gather(v, AXIS, axis=0, tiled=True)


def scatter(v):
    return lax.psum_scatter(v, AXIS, scatter_dimension=0, tiled=True)


def local(
    tokens,
    lengths,
    partners,
    out_cotangent,
    w_query,
    w_key,
    w_value,
    w_output,
    b_query,
    b_value,
    b_output,
    gain_attn,
    shift_attn,
    w_inner,
    b_inner,
    w_outer,
    b_outer,
    gain_ffn,
    shift_ffn,
):
    cube = lax.axis_size(AXIS) == CUBE
    count = tokens.shape[0]
    x = tokens.reshape(count * LEN, D)
    vectors = (b_query, b_value, b_output, gain_attn, shift_attn, b_outer, gain_ffn, shift_ffn, b_inner)
    if cube:
        place = Place()
        qk = pack(w_query, w_key)
        vo = pack(w_value, w_output)
        vec = vector_table(vectors, partners, place)
        qk = join(qk, send(qk, FAR_Z), 0, place.far_z)
        vec = vec + send(vec, FAR_Z)
        qk, vec, vo = together(qk, vec, vo)
        qk = join(qk, send(qk, NEAR_Z), 1, place.near_z)
        vec = vec + send(vec, NEAR_Z)
        vo = join(vo, send(vo, FAR_Z), 0, place.far_z)
        qk, vec, vo, w_inner = together(qk, vec, vo, w_inner)
        qk = join(qk, send(qk, FIRST), 2, place.first).reshape(4, 2, 48, D)
        vec = vec + send(vec, FIRST)
        vo = join(vo, send(vo, NEAR_Z), 1, place.near_z)
        inn = join(w_inner, send(w_inner, FAR_Z), 0, place.far_z)
        qk, vec, vo, inn = together(qk, vec, vo, inn)
        far = send(qk, SECOND)
        other = send(qk, CORE)
        vec = vec + send(vec, SECOND)
        vo = join(vo, send(vo, FIRST), 2, place.first).reshape(4, 2, 48, D)
        inn = join(inn, send(inn, NEAR_Z), 1, place.near_z)
        far, other, vec, vo, inn = together(far, other, vec, vo, inn)
        qk_parts = (qk, far, other, send(far, CORE))
        vec = vec + send(vec, CORE)
        qk_parts, vec, vo, inn, w_outer = together(qk_parts, vec, vo, inn, w_outer)
        vo_far = send(vo, SECOND)
        other = send(vo, CORE)
        inn = join(inn, send(inn, FIRST), 2, place.first).reshape(4, 2, 24, FF)
        out = join(w_outer, send(w_outer, FAR_Z), 0, place.far_z)
        queries, keys, qk = project(x, vec, qk_parts, 2, (B_QUERY, None), cube)
        queries, vo_far, other, inn, out = together(queries, vo_far, other, inn, out)
        vo_parts = (vo, vo_far, other, send(vo_far, CORE))
        inn_far = send(inn, SECOND)
        values, vo = project(x, vec, vo_parts, 2, (B_VALUE,), cube)
        values, out = together(values, out)
        out = join(out, send(out, NEAR_Z), 1, place.near_z)
        probs, context = attend(lengths, queries, keys, values)
        context, inn, inn_far, out = together(context, inn, inn_far, out)
        inn_parts = (inn, inn_far, send(inn, CORE), send(inn_far, CORE))
        out = join(out, send(out, FIRST), 2, place.first).reshape(4, 2, 96, D)
        hat1, inv1, normed = close(x, context, vo, vec)
        normed, inn_parts, out = together(normed, inn_parts, out)
        out_far = send(out, SECOND)
        other = send(out, CORE)
        act, slope, inner_mat = inner(normed, vec, inn_parts, cube)
        act, out_far, other = together(act, out_far, other)
        out_parts = (out, out_far, other, send(out_far, CORE))
        block_out, hat2, inv2, cls, unit, outer_mat = outer(act, hat1, vec, out_parts, cube)
        near = spread(unit, place).reshape(4, 2, *unit.shape)
        far = send(near, SECOND)
        loss, d_cls = pair_loss((near, far, send(near, CORE), send(far, CORE)), vec, cls)
        dres, dbr, sums, *shares = outer_back(
            out_cotangent.reshape(count * LEN, D), d_cls, hat2, inv2, act, vec, cube
        )
        o = Reduction(shares, place)
        dbr, o.away = together(dbr, o.away)
        o.start(CORE)
        dh, sums, *shares = inner_back(dbr, normed, slope, outer_mat, sums, cube)
        i = Reduction(shares, place, early_z=True)
        dh, i.away = arrive([o], dh, i.away)
        i.start(CORE)
        o.settle()
        o.start(FIRST)
        dh, dres = together(dh, dres)
        d_resid, d_attn, d_context, sums = open_back(dres, dh, inner_mat, hat1, inv1, vo, vec, sums)
        (d_context,) = arrive([o, i], d_context)
        o.settle()
        o.start(SECOND)
        i.settle()
        i.start(NEAR_Z)
        d_queries, d_keys, d_values, *shares = heads_back(
            queries, keys, values, d_context, probs, x, sums, context, d_attn, cube
        )
        a = Reduction(shares, place)
        d_queries, a.away = arrive([o, i], d_queries, a.away)
        a.start(CORE)
        o.settle()
        i.settle()
        o.away, i.away = arrive([a], o.away, i.away)
        a.settle()
        a.start(FIRST)
        o.start(NEAR_Z)
        i.start(FIRST)
        grad_rows = token_grad(d_resid, d_queries, d_keys, d_values, qk, vo)
        (grad_rows,) = arrive([o, i, a], grad_rows)
        a.settle()
        a.start(SECOND)
        o.settle()
        o.start(FAR_Z)
        i.settle()
        i.start(SECOND)
        arrive([i, a])
        a.settle()
        a.start(NEAR_Z)
        i.settle()
        i.start(FAR_Z)
        grad_w_outer = o.total()
        (grad_w_outer,) = arrive([a], grad_w_outer)
        a.settle()
        a.start(FAR_Z)
        grad_w_inner = i.total()
        g_attn = a.total()
        g_mats = [g_attn[24 * n : 24 * (n + 1)] for n in range(4)]
        small, inner_part = g_attn[96:, D - WIDE :], g_attn[96, D - WIDE // 2 :]
        grads = [small[n, : D // CUBE] for n in range(B_INNER)] + [inner_part[: FF // CUBE]]
    else:
        rows = [every(v).reshape(-1, D) for v in vectors]
        vec = jnp.concatenate(rows + [jnp.zeros((4, D), low)], axis=0)
        qk_parts, vo_parts = ((jnp.stack([every(w) for w in ws]),) for ws in ((w_query, w_key), (w_value, w_output)))
        queries, keys, qk = project(x, vec, qk_parts, 2, (B_QUERY, None), cube)
        values, vo = project(x, vec, vo_parts, 2, (B_VALUE,), cube)
        probs, context = attend(lengths, queries, keys, values)
        hat1, inv1, normed = close(x, context, vo, vec)
        act, slope, inner_mat = inner(normed, vec, (every(w_inner),), cube)
        block_out, hat2, inv2, cls, unit, outer_mat = outer(act, hat1, vec, (every(w_outer),), cube)
        loss, d_cls = plain_loss(every(unit), every(partners), cls)
        dres, dbr, sums, d_outer = outer_back(
            out_cotangent.reshape(count * LEN, D), d_cls, hat2, inv2, act, vec, cube
        )
        dh, sums, d_inner = inner_back(dbr, normed, slope, outer_mat, sums, cube)
        d_resid, d_attn, d_context, sums = open_back(dres, dh, inner_mat, hat1, inv1, vo, vec, sums)
        d_queries, d_keys, d_values, sums, d_mats = heads_back(
            queries, keys, values, d_context, probs, x, sums, context, d_attn, cube
        )
        grad_rows = token_grad(d_resid, d_queries, d_keys, d_values, qk, vo)
        grad_w_outer, grad_w_inner = scatter(d_outer), scatter(d_inner)
        g_mats = [scatter(d_mats[n]) for n in range(4)]
        grads = [scatter(sums[n]) for n in range(B_INNER)] + [scatter(sums[B_INNER:CODES].reshape(-1))]
    (
        grad_b_query,
        grad_b_value,
        grad_b_output,
        grad_gain_attn,
        grad_shift_attn,
        grad_b_outer,
        grad_gain_ffn,
        grad_shift_ffn,
        grad_b_inner,
    ) = grads
    return (
        loss,
        block_out.reshape(count, LEN, D),
        grad_rows.reshape(count, LEN, D),
        g_mats[0],
        g_mats[1],
        g_mats[2],
        g_mats[3],
        grad_b_query,
        grad_b_value,
        grad_b_output,
        grad_gain_attn,
        grad_shift_attn,
        grad_w_inner,
        grad_b_inner,
        grad_w_outer,
        grad_b_outer,
        grad_gain_ffn,
        grad_shift_ffn,
    )


def solution(mesh):
    rows, cols = P(AXIS), P(AXIS, None)
    cube = P(AXIS, None, None)
    in_specs = (cube, rows, rows, cube) + (cols,) * 4 + (rows,) * 5 + (cols, rows, cols) + (rows,) * 3
    out_specs = (P(), cube, cube) + (cols,) * 4 + (rows,) * 5 + (cols, rows, cols) + (rows,) * 3
    return jax.shard_map(local, mesh=mesh, in_specs=in_specs, out_specs=out_specs, check_vma=False)
```
